32 devices in a mesh: row: 8 (over z, y), col: 4 (over x, core).
Axes of the slice: x: 2, y: 2, z: 4, core: 2. Of those that a mesh axis runs over, the one named last changes fastest.
Arguments:
- coupling: bfloat16 [32, 16, 12, 128, 128], P('row', 'col'), may hold values from -1 to 1
- neighbours: int32 [32, 16, 12], P('row', 'col'), may hold values from 0 to 24, as said below
- prolong: bfloat16 [32, 16, 128, 128], P('row', 'col'), may hold values from -0.5 to 0.5
- aggregate: int32 [32, 16], P('row', 'col'), may hold values from 0 to 63, as said below
Outputs:
- coarse: bfloat16 [8, 4, 2, 9, 2, 128, 128], P('row', None, None, None, None, 'col')
The draws below stay inside these ranges and needn't reach their ends.
Inputs may be any that keep to these rules, and one draw needn't show every extreme that they name: `neighbours`: slot 0 of every node holds the code of offset (0, 0); the other 11 slots of a node hold distinct codes of nonzero offsets. `aggregate`: each aligned 4 x 4 square of the grid, square (sx, sy), holds exactly two aggregates, numbered 2 (sx 4 + sy) and 2 (sx 4 + sy) + 1, which split the square into two halves of equal size either across its first or across its second dimension.
All inputs are finite; a program needn't handle non-finite values.
Results may differ from the reference program's by a relative error of at most 0.0049.
Values may be sent and summed in bfloat16 or wider, within the bound.
No kernel may reach another device: no remote copies, remote signals or barrier semaphores. Data moves between devices by JAX's collectives and lax.ppermute only.
A program may use at most 128 MiB of HBM per device.

```python
import jax
import jax.numpy as jnp
from jax import lax

BS = 128
KA = 12
REACH = 2
SIDE = 4
NX = 32
NY = 16
SBX = 8
SBY = 4


def draw_neighbours(key, part):
    window = 2 * REACH + 1
    centre_code = REACH * window + REACH
    others = jnp.array([code for code in range(window * window) if code != centre_code], dtype=jnp.int32)
    node_count = NX * NY
    candidates = jnp.broadcast_to(others, (node_count, others.shape[0]))
    shuffled = jax.random.permutation(key, candidates, axis=1, independent=True)
    centre = jnp.full((node_count, 1), centre_code, jnp.int32)
    return jnp.concatenate([centre, shuffled[:, :KA - 1]], axis=1).reshape(NX, NY, KA)


def draw_aggregate(key, part):
    flips = jax.random.randint(key, (SBX, SBY), 0, 2, dtype=jnp.int32)
    grid_x = jnp.arange(NX, dtype=jnp.int32)[:, None]
    grid_y = jnp.arange(NY, dtype=jnp.int32)[None, :]
    super_x = grid_x // SIDE
    super_y = grid_y // SIDE
    flip_at = flips[super_x, super_y]
    half_bit = jnp.where(flip_at == 1, grid_x % SIDE // (SIDE // 2), grid_y % SIDE // (SIDE // 2))
    return (2 * (super_x * SBY + super_y) + half_bit).astype(jnp.int32)


def block_levels(stream_key, shape, cuts, least, largest):
    gain = 1.0
    for axis_at, parts in cuts:
        draws = jax.random.uniform(jax.random.fold_in(jax.random.fold_in(stream_key, 6), axis_at), (parts,), jnp.float32, least / len(cuts), largest / len(cuts))
        gain = gain * jnp.repeat(jnp.exp(draws), shape[axis_at] // parts).reshape((-1,) + (1,) * (len(shape) - 1 - axis_at))
    return gain


def noise(stream_key, shape, scale, reach, cuts=(), kind=jnp.bfloat16):
    result = scale * jax.random.normal(stream_key, shape, jnp.float32)
    if cuts:
        result = result * block_levels(stream_key, shape, cuts, -0.22, 0.18)
    return jnp.clip(result, -reach, reach).astype(kind)


def setup_inputs(seed: int = 0) -> dict:
    arg_keys = jax.random.split(jax.random.key(seed), 5)
    return {
        "coupling": noise(arg_keys[0], (NX, NY, KA, BS, BS), (BS // 4) ** -0.5, 1.0, ((0, 8), (1, 4))),
        "neighbours": draw_neighbours(jax.random.fold_in(arg_keys[4], 71), 0),
        "prolong": noise(arg_keys[2], (NX, NY, BS, BS), BS ** -0.5, 0.5, ((0, 8), (1, 4))),
        "aggregate": draw_aggregate(jax.random.fold_in(arg_keys[4], 71), 0),
    }


def reference(coupling, neighbours, prolong, aggregate):
    window = 2 * REACH + 1
    padded = jnp.pad(prolong, ((REACH, REACH), (REACH, REACH), (0, 0), (0, 0)))
    flat_blocks = padded.reshape(-1, BS, BS)
    agg_padded = jnp.pad(aggregate, REACH).reshape(-1)
    pad_width = NY + 2 * REACH

    def strip_row(strip_index):
        first_x = strip_index * SIDE
        near_coupling = lax.dynamic_slice_in_dim(coupling, first_x, SIDE, 0)
        near_codes = lax.dynamic_slice_in_dim(neighbours, first_x, SIDE, 0)
        near_blocks = lax.dynamic_slice_in_dim(prolong, first_x, SIDE, 0)
        near_agg = lax.dynamic_slice_in_dim(aggregate, first_x, SIDE, 0)
        step_x = near_codes // window - REACH
        step_y = near_codes % window - REACH
        target_x = first_x + jnp.arange(SIDE, dtype=jnp.int32)[:, None, None] + step_x
        target_y = jnp.arange(NY, dtype=jnp.int32)[None, :, None] + step_y
        inside = (target_x >= 0) & (target_x < NX) & (target_y >= 0) & (target_y < NY)
        position = ((target_x + REACH) * pad_width + target_y + REACH).astype(jnp.int32)
        far_blocks = jnp.take(flat_blocks, position.reshape(-1), axis=0).reshape(SIDE, NY, KA, BS, BS)
        far_agg = jnp.take(agg_padded, position.reshape(-1)).reshape(SIDE, NY, KA)
        moved = jnp.einsum('xykab,xykbc->xykac', near_coupling.astype(jnp.float32), far_blocks.astype(jnp.float32)).astype(jnp.bfloat16)
        contribution = jnp.einsum('xyba,xykbc->xykac', near_blocks.astype(jnp.float32), moved.astype(jnp.float32))
        near_ids = near_agg[:, :, None]
        near_super = near_ids // 2
        far_super = far_agg // 2
        square_code = (far_super // SBY - near_super // SBY + 1) * 3 + (far_super % SBY - near_super % SBY + 1)
        segment = ((near_super % SBY) * 2 + near_ids % 2) * 18 + square_code * 2 + far_agg % 2
        segment = jnp.where(inside, segment, 0).astype(jnp.int32)
        summed = jax.ops.segment_sum(contribution.reshape(-1, BS * BS), segment.reshape(-1), num_segments=SBY * 36)
        return summed.reshape(SBY, 2, 9, 2, BS, BS).astype(jnp.bfloat16)

    return lax.map(strip_row, jnp.arange(SBX, dtype=jnp.int32))
```

```python
import functools

import jax
import jax.numpy as jnp
from jax import lax
from jax.experimental import pallas as pl
from jax.experimental.pallas import tpu as pltpu
from jax.sharding import PartitionSpec as P

BS = 128
KA = 12
SIDE = 4
QUAD = 4 * BS
HEAD = 16
ROWS = HEAD + QUAD
EARLY = 16
LATE = 6
ANY = pl.BlockSpec(memory_space=pl.ANY)
SMEM = pl.BlockSpec(memory_space=pltpu.SMEM)
VMEM = pl.BlockSpec(memory_space=pltpu.VMEM)
BF16 = jnp.bfloat16
F32 = jnp.float32


def flips():
    return lax.rem(lax.axis_index("row"), 2), lax.rem(lax.axis_index("col"), 2)


def turned(index, flip):
    return index + flip - 2 * index * flip


def rims_kernel(agg, prolong, row_a, row_b, col_a, col_b, sems):
    fx, fy = flips()
    copies = []
    plans = (
        (row_a, ((1, 0), (1, 1))),
        (row_b, ((0, 0), (0, 1))),
        (col_a, ((0, 1), (1, 1))),
        (col_b, ((0, 0), (1, 0))),
    )
    for out, quads in plans:
        for h, (u, v) in enumerate(quads):
            ur, vr = turned(u, fx), turned(v, fy)
            for m in range(2):
                copies.append(
                    pltpu.make_async_copy(
                        prolong.at[2 * ur + m, pl.ds(pl.multiple_of(vr * 256, 256), 256), :],
                        out.at[h, HEAD + 256 * m : HEAD + 256 * (m + 1), :],
                        sems.at[len(copies)],
                    )
                )
                copies[-1].start()
    for out, quads in plans:
        for h, (u, v) in enumerate(quads):
            ur, vr = turned(u, fx), turned(v, fy)
            bit = lax.rem(agg[2 * ur, 2 * vr], 2).astype(F32)
            out[h, 0:HEAD, :] = jnp.full((HEAD, BS), bit, F32).astype(BF16)
    for copy in copies:
        copy.wait()


def rims(agg, prolong_rows):
    shape = jax.ShapeDtypeStruct((2, ROWS, BS), BF16)
    return pl.pallas_call(
        rims_kernel,
        out_shape=(shape,) * 4,
        in_specs=[SMEM, ANY],
        out_specs=(VMEM,) * 4,
        scratch_shapes=[pltpu.SemaphoreType.DMA((16,))],
        compiler_params=pltpu.CompilerParams(vmem_limit_bytes=4 << 20),
        name="rims",
    )(agg, prolong_rows)


def step_one_kernel(codes, coupling, prolong, out, acc):
    quad, node = pl.program_id(0), pl.program_id(1)
    fx, fy = flips()
    ix, iy = node // 2, node % 2
    x, y = 2 * (quad // 2) + ix, 2 * (quad % 2) + iy

    @pl.when(node == 0)
    def _():
        acc[...] = jnp.zeros_like(acc)

    left = prolong[0, 0].T
    for k in range(0, KA, 2):
        pair = jnp.concatenate([coupling[0, 0, k], coupling[0, 0, k + 1]], axis=1)
        both = jnp.dot(left, pair, preferred_element_type=F32)
        for e in range(2):
            code = codes[x, y, k + e]
            off_x = lax.shift_right_logical(code * 13, 6)
            jx = ix + off_x
            jy = iy + code - 5 * off_x
            du, dv = lax.shift_right_logical(jx, 1), lax.shift_right_logical(jy, 1)
            du = du + fx * (2 - 2 * du)
            dv = dv + fy * (2 - 2 * dv)
            at = (du * 3 + dv) * 4 + 2 * (jx & 1) + (jy & 1)
            acc[at] += both[:, e * BS : (e + 1) * BS]

    @pl.when(node == 3)
    def _():
        for t in range(36):
            out[0, t // 4, :, (t % 4) * BS : (t % 4 + 1) * BS] = acc[t].astype(BF16)


def step_one(codes, coupling, prolong):
    def node_at(q, i):
        return 2 * (q // 2) + i // 2, 2 * (q % 2) + i % 2

    return pl.pallas_call(
        step_one_kernel,
        grid=(4, 4),
        out_shape=jax.ShapeDtypeStruct((4, 9, BS, QUAD), BF16),
        in_specs=[
            SMEM,
            pl.BlockSpec((1, 1, KA, BS, BS), lambda q, i: (*node_at(q, i), 0, 0, 0)),
            pl.BlockSpec((1, 1, BS, BS), lambda q, i: (*node_at(q, i), 0, 0)),
        ],
        out_specs=pl.BlockSpec((1, 9, BS, QUAD), lambda q, i: (q, 0, 0, 0)),
        scratch_shapes=[pltpu.VMEM((36, BS, BS), F32)],
        compiler_params=pltpu.CompilerParams(vmem_limit_bytes=16 << 20),
        cost_estimate=pl.CostEstimate(
            flops=2 * 192 * BS**3, bytes_accessed=2 * 192 * BS * BS, transcendentals=0
        ),
        name="step_one",
    )(codes, coupling, prolong)


def own_bits(agg, fx, fy):
    return {
        (u + 1, v + 1): lax.rem(agg[2 * turned(u, fx), 2 * turned(v, fy)], 2).astype(F32)
        for u in range(2)
        for v in range(2)
    }


def edge_slots(terms, halves, same_a):
    near = 1.0 - jnp.abs(halves[0] - halves[1])
    by_p = []
    for first, second in terms:
        shared = near * second
        by_p.append((first + shared, second - shared))
    base = [by_p[0][v] + same_a * by_p[1][v] for v in range(2)]
    extra = [(1.0 - same_a) * by_p[1][v] for v in range(2)]
    return base, extra


def store_pieces(slots, head, outs, count):
    rows = outs[0].shape[1]
    me = lax.axis_index("col")
    for s, out in enumerate(outs):
        start = pl.multiple_of((me ^ s) * rows, rows)
        for t in range(count):
            out[t] = slots[t, pl.ds(start, rows), :].astype(BF16)
        for t in range(out.shape[0] - count):
            out[count + t] = head[t * rows : (t + 1) * rows, :].astype(BF16)


def early_kernel(agg, r, prolong, row_a, col_a, col_b, corner_aa, corner_ab, *rest):
    outs, (slots, head) = rest[:-2], rest[-2:]
    fx, fy = flips()
    bits = own_bits(agg, fx, fy)
    split_x = 1.0 - jnp.abs(bits[1, 1] - bits[1, 2])

    def far(q):
        u, v = q
        if u == 3:
            return {0: corner_ab.at[0], 3: corner_aa.at[0]}.get(v, row_a.at[v - 1])
        return (col_a if v == 3 else col_b).at[u - 1]

    def blocks(q):
        u, v = q
        if 1 <= u <= 2 and 1 <= v <= 2:
            ur, vr = turned(u - 1, fx), turned(v - 1, fy)
            at = pl.ds(pl.multiple_of(vr * 256, 256), 256)
            return jnp.concatenate([prolong[2 * ur, at, :], prolong[2 * ur + 1, at, :]], axis=0)
        return far(q)[HEAD:, :]

    def term(p, q):
        raw = 2 * turned(p[0] - 1, fx) + turned(p[1] - 1, fy)
        near = r[raw, (q[0] - p[0] + 1) * 3 + q[1] - p[1] + 1]
        return jnp.dot(near, blocks(q), preferred_element_type=F32)

    def half(q):
        return far(q)[0:1, :].astype(F32)

    own = [(1, 1), (1, 2), (2, 1), (2, 2)]
    for i, p in enumerate(own):
        for j, q in enumerate(own):
            value = term(p, q)
            for a in range(2):
                for b in range(2):
                    ia = bits[p] if a else 1.0 - bits[p]
                    ib = bits[q] if b else 1.0 - bits[q]
                    part = (ia * ib) * value
                    if i + j == 0:
                        slots[2 * a + b] = part
                    else:
                        slots[2 * a + b] += part

    rows_a = [(2, 1), (2, 2)], [(3, 1), (3, 2)], split_x
    cols_a = [(1, 2), (2, 2)], [(1, 3), (2, 3)], 1.0 - split_x
    cols_b = [(1, 1), (2, 1)], [(1, 0), (2, 0)], 1.0 - split_x
    extras = []
    for e, (ps, qs, same_a) in enumerate((rows_a, cols_a, cols_b)):
        terms = [[term(p, q) for q in qs] for p in ps]
        base, extra = edge_slots(terms, [half(q) for q in qs], same_a)
        for v in range(2):
            slots[4 + 2 * e + v] = base[v]
            if e == 0:
                slots[12 + v] = extra[v]
                extras.append(extra[v])
            elif e == 1:
                slots[12 + v] += extra[v]
            else:
                slots[14 + v] = extra[v]
    slots[10] = term((2, 2), (3, 3))
    slots[11] = term((2, 1), (3, 0))
    for k, p in enumerate(own):
        head[k : k + 1, :] = jnp.full((1, BS), bits[p], F32)
    for k, q in enumerate(((3, 1), (3, 2), (1, 3), (2, 3), (1, 0), (2, 0), (3, 3), (3, 0))):
        head[4 + k : 5 + k, :] = half(q)
    head[12:, :] = jnp.zeros((head.shape[0] - 12, BS), F32)
    store_pieces(slots, head, outs, EARLY)


def late_kernel(agg, r, row_b, corner_ba, corner_bb, *rest):
    outs, (slots, head, near, sems) = rest[:-4], rest[-4:]
    fx, fy = flips()
    copies = []
    for v in range(2):
        raw = 2 * fx + turned(v, fy)
        copies.append(pltpu.make_async_copy(r.at[raw, 0:3], near.at[v], sems.at[v]))
        copies[-1].start()
    bits = own_bits(agg, fx, fy)
    split_x = 1.0 - jnp.abs(bits[1, 1] - bits[1, 2])

    def far(v):
        return {0: corner_bb.at[0], 3: corner_ba.at[0]}.get(v, row_b.at[v - 1])

    def term(p, v):
        return jnp.dot(near[p - 1, v - p + 1], far(v)[HEAD:, :], preferred_element_type=F32)

    def half(v):
        return far(v)[0:1, :].astype(F32)

    for k, p in enumerate([(1, 1), (1, 2), (2, 1), (2, 2)]):
        head[k : k + 1, :] = jnp.full((1, BS), bits[p], F32)
    for k, v in enumerate((1, 2, 3, 0)):
        head[4 + k : 5 + k, :] = half(v)
    head[8:, :] = jnp.zeros((head.shape[0] - 8, BS), F32)
    for copy in copies:
        copy.wait()
    terms = [[term(p, v) for v in (1, 2)] for p in (1, 2)]
    base, extra = edge_slots(terms, [half(1), half(2)], split_x)
    for v in range(2):
        slots[v] = base[v]
        slots[4 + v] = extra[v]
    slots[2] = term(2, 3)
    slots[3] = term(1, 0)
    store_pieces(slots, head, outs, LATE)


def pieces(kernel, operands, specs, count, parts, extra_scratch, cost, name):
    rows = BS // parts
    heads = -(-HEAD // rows)
    shape = jax.ShapeDtypeStruct((count + heads, rows, BS), BF16)
    return pl.pallas_call(
        kernel,
        out_shape=(shape,) * parts,
        in_specs=specs,
        out_specs=(VMEM,) * parts,
        scratch_shapes=[
            pltpu.VMEM((count, BS, BS), F32),
            pltpu.VMEM((heads * rows, BS), F32),
        ]
        + extra_scratch,
        compiler_params=pltpu.CompilerParams(vmem_limit_bytes=24 << 20),
        cost_estimate=pl.CostEstimate(flops=cost, bytes_accessed=1 << 20, transcendentals=0),
        name=name,
    )(*operands)


def early_unpack_kernel(parts, *refs):
    ins, out, buf, sems = refs[:parts], refs[parts], refs[parts + 1], refs[parts + 2]
    me = lax.axis_index("col")
    fx, _ = flips()
    copies = []
    for s, ref in enumerate(ins):
        square = me ^ s
        fy = lax.rem(square, 2)
        one = functools.partial(bit_row, ref, EARLY)
        split_y = jnp.abs(one(0) - one(1))
        spread(buf, (s, 0, 1), center=[ref[t].astype(F32) for t in range(4)])
        spread_edge(buf, (s, 3, 1), ref, one, (2, 3), (4, 5), (4, 5), (12, 13), split_y)
        spread_edge(buf, (s, 0, turn3(2, fy)), ref, one, (1, 3), (6, 7), (6, 7), (12, 13), 1.0 - split_y)
        spread_edge(buf, (s, 0, turn3(0, fy)), ref, one, (0, 2), (8, 9), (8, 9), (14, 15), 1.0 - split_y)
        spread_corner(buf, (s, 3, turn3(2, fy)), ref[10].astype(F32), one(3), one(10))
        spread_corner(buf, (s, 3, turn3(0, fy)), ref[11].astype(F32), one(2), one(11))
        for a in range(2):
            for g, at in ((0, 3), (3, 6 - 6 * fx)):
                copies.append(
                    pltpu.make_async_copy(
                        buf.at[s, a, g : g + 3], out.at[square, a, pl.ds(at, 3)], sems.at[len(copies)]
                    )
                )
                copies[-1].start()
    for copy in copies:
        copy.wait()


def late_unpack_kernel(parts, *refs):
    ins, out, buf, sems = refs[:parts], refs[parts + 1], refs[parts + 2], refs[parts + 3]
    me = lax.axis_index("col")
    fx, _ = flips()
    copies = []
    for s, ref in enumerate(ins):
        square = me ^ s
        fy = lax.rem(square, 2)
        one = functools.partial(bit_row, ref, LATE)
        split_y = jnp.abs(one(0) - one(1))
        spread_edge(buf, (s, 0, 1), ref, one, (0, 1), (4, 5), (0, 1), (4, 5), split_y)
        spread_corner(buf, (s, 0, turn3(2, fy)), ref[2].astype(F32), one(1), one(6))
        spread_corner(buf, (s, 0, turn3(0, fy)), ref[3].astype(F32), one(0), one(7))
        for a in range(2):
            copies.append(
                pltpu.make_async_copy(
                    buf.at[s, a], out.at[square, a, pl.ds(6 * fx, 3)], sems.at[len(copies)]
                )
            )
            copies[-1].start()
    for copy in copies:
        copy.wait()


def turn3(index, flip):
    return index + flip * (2 - 2 * index)


def bit_row(ref, count, k):
    rows = ref.shape[1]
    return ref[count + k // rows, k % rows : k % rows + 1, :].astype(F32)


def spread(buf, at, center):
    s, group, column = at
    for a in range(2):
        for b in range(2):
            buf[s, a, group + column, b] = center[2 * a + b].astype(BF16)


def spread_edge(buf, at, ref, one, ps, qs, base, extra, used):
    a_bits = [one(p) for p in ps]
    b_bits = [one(q) for q in qs]
    values = [ref[t].astype(F32) for t in base]
    more = [ref[t].astype(F32) for t in extra]
    center = [None] * 4
    for b in range(2):
        picks = [bit if b else 1.0 - bit for bit in b_bits]
        first = picks[0] * values[0] + picks[1] * values[1]
        second = (used * picks[0]) * more[0] + (used * picks[1]) * more[1]
        for a in range(2):
            ia = [bit if a else 1.0 - bit for bit in a_bits]
            center[2 * a + b] = ia[0] * first + ia[1] * second
    spread(buf, at, center)


def spread_corner(buf, at, value, a_bit, b_bit):
    center = []
    for a in range(2):
        for b in range(2):
            center.append(((a_bit if a else 1.0 - a_bit) * (b_bit if b else 1.0 - b_bit)) * value)
    spread(buf, at, center)


def unpack_early(messages):
    parts = len(messages)
    rows = messages[0].shape[1]
    return pl.pallas_call(
        functools.partial(early_unpack_kernel, parts),
        out_shape=jax.ShapeDtypeStruct((parts, 2, 9, 2, rows, BS), BF16),
        in_specs=[VMEM] * parts,
        out_specs=ANY,
        scratch_shapes=[
            pltpu.VMEM((parts, 2, 6, 2, rows, BS), BF16),
            pltpu.SemaphoreType.DMA((4 * parts,)),
        ],
        compiler_params=pltpu.CompilerParams(vmem_limit_bytes=16 << 20),
        name="unpack_early",
    )(*messages)


def unpack_late(messages, coarse):
    parts = len(messages)
    rows = messages[0].shape[1]
    return pl.pallas_call(
        functools.partial(late_unpack_kernel, parts),
        out_shape=jax.ShapeDtypeStruct(coarse.shape, BF16),
        in_specs=[VMEM] * parts + [ANY],
        out_specs=ANY,
        scratch_shapes=[
            pltpu.VMEM((parts, 2, 3, 2, rows, BS), BF16),
            pltpu.SemaphoreType.DMA((2 * parts,)),
        ],
        input_output_aliases={parts: 0},
        compiler_params=pltpu.CompilerParams(vmem_limit_bytes=16 << 20),
        name="unpack_late",
    )(*messages, coarse)


def swap(value, axis, side):
    count = lax.axis_size(axis)
    first = range(side, count - 1, 2)
    return lax.ppermute(value, axis, [(i, i + 1) for i in first] + [(i + 1, i) for i in first])


def scatter_rows(outs):
    count = len(outs)
    return [outs[0]] + [
        lax.ppermute(outs[s], "col", [(i, i ^ s) for i in range(count)]) for s in range(1, count)
    ]


def local(coupling, neighbours, prolong, aggregate):
    parts = lax.axis_size("col")
    prolong_rows = prolong.reshape(SIDE, SIDE * BS, BS)
    to_row_a, to_row_b, to_col_a, to_col_b = rims(aggregate, prolong_rows)
    row_a = swap(to_row_a, "row", 0)
    col_a = swap(to_col_a, "col", 0)
    col_b = swap(to_col_b, "col", 1)
    row_b = swap(to_row_b, "row", 1)
    r = step_one(neighbours, coupling, prolong)
    corner_aa = swap(row_a[1:2], "col", 0)
    corner_ab = swap(row_a[0:1], "col", 1)
    corner_ba = swap(row_b[1:2], "col", 0)
    corner_bb = swap(row_b[0:1], "col", 1)
    early = pieces(
        early_kernel,
        (aggregate, r, prolong_rows, row_a, col_a, col_b, corner_aa, corner_ab),
        [SMEM] + [VMEM] * 7,
        EARLY,
        parts,
        [],
        2 * 30 * BS * BS * QUAD,
        "early_terms",
    )
    late = pieces(
        late_kernel,
        (aggregate, r, row_b, corner_ba, corner_bb),
        [SMEM, ANY] + [VMEM] * 3,
        LATE,
        parts,
        [pltpu.VMEM((2, 3, BS, QUAD), BF16), pltpu.SemaphoreType.DMA((2,))],
        2 * 6 * BS * BS * QUAD,
        "late_terms",
    )
    coarse = unpack_early(scatter_rows(early))
    coarse = unpack_late(scatter_rows(late), coarse)
    return coarse[None]


def solution(mesh):
    return jax.shard_map(
        local,
        mesh=mesh,
        in_specs=(
            P("row", "col", None, None, None),
            P("row", "col", None),
            P("row", "col", None, None),
            P("row", "col"),
        ),
        out_specs=P("row", None, None, None, None, "col", None),
        check_vma=False,
    )
```

```python
import functools

import jax
import jax.numpy as jnp
from jax import lax
from jax.experimental import pallas as pl
from jax.experimental.pallas import tpu as pltpu
from jax.sharding import PartitionSpec as P

BS = 128
KA = 12
SIDE = 4
QUAD = 4 * BS
HEAD = 16
ROWS = HEAD + QUAD
EARLY = 16
LATE = 6
ANY = pl.BlockSpec(memory_space=pl.ANY)
VMEM = pl.BlockSpec(memory_space=pltpu.VMEM)
HBM = pl.BlockSpec(memory_space=pltpu.HBM)
BF16 = jnp.bfloat16
F32 = jnp.float32


def flips():
    return lax.rem(lax.axis_index("row"), 2), lax.rem(lax.axis_index("col"), 2)


def turned(index, flip):
    return index + flip - 2 * index * flip


def rims_kernel(agg_hbm, prolong, row_a, row_b, col_a, col_b, bits, agg, sems):
    fx, fy = flips()
    load = pltpu.make_async_copy(agg_hbm, agg, sems.at[16])
    load.start()
    copies = []
    plans = (
        (row_a, ((1, 0), (1, 1))),
        (row_b, ((0, 0), (0, 1))),
        (col_a, ((0, 1), (1, 1))),
        (col_b, ((0, 0), (1, 0))),
    )
    for out, quads in plans:
        for h, (u, v) in enumerate(quads):
            ur, vr = turned(u, fx), turned(v, fy)
            for m in range(2):
                copies.append(
                    pltpu.make_async_copy(
                        prolong.at[2 * ur + m, pl.ds(pl.multiple_of(vr * 256, 256), 256), :],
                        out.at[h, HEAD + 256 * m : HEAD + 256 * (m + 1), :],
                        sems.at[len(copies)],
                    )
                )
                copies[-1].start()
    load.wait()
    own = {}
    for k, (u, v) in enumerate(((0, 0), (0, 1), (1, 0), (1, 1))):
        own[u, v] = lax.rem(agg[2 * turned(u, fx), 2 * turned(v, fy)], 2).astype(F32)
        bits[k : k + 1, :] = jnp.full((1, BS), own[u, v], F32)
    bits[4:, :] = jnp.zeros((4, BS), F32)
    for out, quads in plans:
        for h, quad in enumerate(quads):
            out[h, 0:HEAD, :] = jnp.full((HEAD, BS), own[quad], F32).astype(BF16)
    for copy in copies:
        copy.wait()


def rims(agg, prolong_rows):
    shape = jax.ShapeDtypeStruct((2, ROWS, BS), BF16)
    return pl.pallas_call(
        rims_kernel,
        out_shape=(shape,) * 4 + (jax.ShapeDtypeStruct((8, BS), F32),),
        in_specs=[HBM, HBM],
        out_specs=(VMEM,) * 5,
        scratch_shapes=[pltpu.SMEM((SIDE, SIDE), jnp.int32), pltpu.SemaphoreType.DMA((17,))],
        compiler_params=pltpu.CompilerParams(vmem_limit_bytes=4 << 20),
        name="rims",
    )(agg, prolong_rows)


NONE = 16 * KA


def step_one_kernel(codes_hbm, coupling, prolong_hbm, bits, out, center, blocks, prolong, codes, slot_of, sems):
    fx, fy = flips()
    load_codes = pltpu.make_async_copy(codes_hbm, codes, sems.at[8])
    load_codes.start()
    load_prolong = pltpu.make_async_copy(prolong_hbm, prolong, sems.at[9])
    load_prolong.start()

    def load(quad, m):
        first = (2 * (quad // 2) + m) * SIDE + 2 * (quad % 2)
        at = pl.ds(first * KA, 2 * KA)
        return pltpu.make_async_copy(coupling.at[at], blocks.at[at], sems.at[2 * quad + m])

    for quad in range(4):
        for m in range(2):
            load(quad, m).start()
    blocks[NONE] = jnp.zeros((BS, BS), BF16)

    @pl.loop(0, 16)
    def _(n):
        for t in range(25):
            slot_of[n * 25 + t] = NONE

    load_codes.wait()

    @pl.loop(0, 16)
    def _(n):
        for k in range(KA):
            slot_of[n * 25 + codes[n // SIDE, n % SIDE, k]] = n * KA + k

    load_prolong.wait()
    zero = jnp.zeros((BS, BS), BF16)

    @pl.loop(0, 4)
    def _(quad):
        qx, qy = quad // 2, quad % 2
        for m in range(2):
            load(quad, m).wait()
        left = []
        for ix in range(2):
            rows = prolong[2 * qx + ix, pl.ds(pl.multiple_of(qy * 256, 256), 256), :]
            left.append(rows.T)

        def block(ix, iy, jx, jy):
            if not (0 <= jy - iy <= 4):
                return zero
            n = (2 * qx + ix) * SIDE + 2 * qy + iy
            return blocks[slot_of[n * 25 + (jx - ix) * 5 + jy - iy]]

        for jx in range(6):
            for t in range(3):
                total = None
                for ix in range(2):
                    if not (0 <= jx - ix <= 4):
                        continue
                    right = jnp.concatenate(
                        [
                            jnp.concatenate([block(ix, iy, jx, 2 * t + e) for e in range(2)], axis=1)
                            for iy in range(2)
                        ],
                        axis=0,
                    )
                    part = jnp.dot(left[ix], right, preferred_element_type=F32)
                    total = part if total is None else total + part
                du, dv = jx // 2, t
                at = (du + fx * (2 - 2 * du)) * 3 + dv + fy * (2 - 2 * dv)
                out[quad, at, :, (jx % 2) * 256 : (jx % 2 + 1) * 256] = total.astype(BF16)

    own = [(1, 1), (1, 2), (2, 1), (2, 2)]
    far = []
    for u, v in own:
        ur, vr = turned(u - 1, fx), turned(v - 1, fy)
        at = pl.ds(pl.multiple_of(vr * 256, 256), 256)
        far.append(jnp.concatenate([prolong[2 * ur, at, :], prolong[2 * ur + 1, at, :]], axis=0))
    for i, p in enumerate(own):
        raw = 2 * turned(p[0] - 1, fx) + turned(p[1] - 1, fy)
        by_b = [None, None]
        for j, q in enumerate(own):
            near = out[raw, (q[0] - p[0] + 1) * 3 + q[1] - p[1] + 1]
            value = jnp.dot(near, far[j], preferred_element_type=F32)
            high = bits[j : j + 1, :] * value
            low = value - high
            by_b = [low if j == 0 else by_b[0] + low, high if j == 0 else by_b[1] + high]
        for b in range(2):
            high = bits[i : i + 1, :] * by_b[b]
            low = by_b[b] - high
            if i == 0:
                center[b] = low
                center[2 + b] = high
            else:
                center[b] += low
                center[2 + b] += high


def step_one(codes, coupling, prolong_rows, bits):
    return pl.pallas_call(
        step_one_kernel,
        out_shape=(
            jax.ShapeDtypeStruct((4, 9, BS, QUAD), BF16),
            jax.ShapeDtypeStruct((4, BS, BS), F32),
        ),
        in_specs=[HBM, HBM, HBM, VMEM],
        out_specs=(VMEM, VMEM),
        scratch_shapes=[
            pltpu.VMEM((NONE + 1, BS, BS), BF16),
            pltpu.VMEM((SIDE, SIDE * BS, BS), BF16),
            pltpu.SMEM((SIDE, SIDE, KA), jnp.int32),
            pltpu.SMEM((400,), jnp.int32),
            pltpu.SemaphoreType.DMA((10,)),
        ],
        compiler_params=pltpu.CompilerParams(vmem_limit_bytes=16 << 20),
        cost_estimate=pl.CostEstimate(
            flops=2 * 192 * BS**3, bytes_accessed=2 * 192 * BS * BS, transcendentals=0
        ),
        name="step_one",
    )(codes, coupling, prolong_rows, bits)


def edge_slots(terms, halves, same_a):
    near = 1.0 - jnp.abs(halves[0] - halves[1])
    by_p = []
    for first, second in terms:
        shared = near * second
        by_p.append((first + shared, second - shared))
    base = [by_p[0][v] + same_a * by_p[1][v] for v in range(2)]
    extra = [(1.0 - same_a) * by_p[1][v] for v in range(2)]
    return base, extra


def store_pieces(slots, head, outs, count):
    rows = outs[0].shape[1]
    me = lax.axis_index("col")
    for s, out in enumerate(outs):
        start = pl.multiple_of((me ^ s) * rows, rows)
        for t in range(count):
            out[t] = slots[t, pl.ds(start, rows), :].astype(BF16)
        for t in range(out.shape[0] - count):
            out[count + t] = head[t * rows : (t + 1) * rows, :].astype(BF16)


OWN = ((1, 1), (1, 2), (2, 1), (2, 2))


def early_kernel(bits, r, center, row_a, col_a, col_b, corner_aa, corner_ab, *rest):
    outs, (slots, head) = rest[:-2], rest[-2:]
    fx, fy = flips()
    split_x = 1.0 - jnp.abs(bits[0:1, :] - bits[1:2, :])

    def far(q):
        u, v = q
        if u == 3:
            return {0: corner_ab.at[0], 3: corner_aa.at[0]}.get(v, row_a.at[v - 1])
        return (col_a if v == 3 else col_b).at[u - 1]

    def term(p, q):
        raw = 2 * turned(p[0] - 1, fx) + turned(p[1] - 1, fy)
        near = r[raw, (q[0] - p[0] + 1) * 3 + q[1] - p[1] + 1]
        return jnp.dot(near, far(q)[HEAD:, :], preferred_element_type=F32)

    def half(q):
        return far(q)[0:1, :].astype(F32)

    for t in range(4):
        slots[t] = center[t]
    rows_a = [(2, 1), (2, 2)], [(3, 1), (3, 2)], split_x
    cols_a = [(1, 2), (2, 2)], [(1, 3), (2, 3)], 1.0 - split_x
    cols_b = [(1, 1), (2, 1)], [(1, 0), (2, 0)], 1.0 - split_x
    for e, (ps, qs, same_a) in enumerate((rows_a, cols_a, cols_b)):
        terms = [[term(p, q) for q in qs] for p in ps]
        base, extra = edge_slots(terms, [half(q) for q in qs], same_a)
        for v in range(2):
            slots[4 + 2 * e + v] = base[v]
            if e == 1:
                slots[12 + v] += extra[v]
            else:
                slots[12 + e + v] = extra[v]
    slots[10] = term((2, 2), (3, 3))
    slots[11] = term((2, 1), (3, 0))
    head[0:8, :] = bits[...]
    for k, q in enumerate(((3, 1), (3, 2), (1, 3), (2, 3), (1, 0), (2, 0), (3, 3), (3, 0))):
        head[4 + k : 5 + k, :] = half(q)
    head[12:, :] = jnp.zeros((head.shape[0] - 12, BS), F32)
    store_pieces(slots, head, outs, EARLY)


def late_kernel(bits, r, row_b, corner_ba, corner_bb, *rest):
    outs, (slots, head) = rest[:-2], rest[-2:]
    fx, fy = flips()
    split_x = 1.0 - jnp.abs(bits[0:1, :] - bits[1:2, :])

    def far(v):
        return {0: corner_bb.at[0], 3: corner_ba.at[0]}.get(v, row_b.at[v - 1])

    def term(p, v):
        near = r[2 * fx + turned(p - 1, fy), v - p + 1]
        return jnp.dot(near, far(v)[HEAD:, :], preferred_element_type=F32)

    def half(v):
        return far(v)[0:1, :].astype(F32)

    head[0:8, :] = bits[...]
    for k, v in enumerate((1, 2, 3, 0)):
        head[4 + k : 5 + k, :] = half(v)
    head[8:, :] = jnp.zeros((head.shape[0] - 8, BS), F32)
    terms = [[term(p, v) for v in (1, 2)] for p in (1, 2)]
    base, extra = edge_slots(terms, [half(1), half(2)], split_x)
    for v in range(2):
        slots[v] = base[v]
        slots[4 + v] = extra[v]
    slots[2] = term(2, 3)
    slots[3] = term(1, 0)
    store_pieces(slots, head, outs, LATE)


def pieces(kernel, operands, count, parts, cost, name):
    rows = BS // parts
    heads = -(-HEAD // rows)
    shape = jax.ShapeDtypeStruct((count + heads, rows, BS), BF16)
    return pl.pallas_call(
        kernel,
        out_shape=(shape,) * parts,
        in_specs=[VMEM] * len(operands),
        out_specs=(VMEM,) * parts,
        scratch_shapes=[
            pltpu.VMEM((count, BS, BS), F32),
            pltpu.VMEM((heads * rows, BS), F32),
        ],
        compiler_params=pltpu.CompilerParams(vmem_limit_bytes=24 << 20),
        cost_estimate=pl.CostEstimate(flops=cost, bytes_accessed=1 << 20, transcendentals=0),
        name=name,
    )(*operands)


def early_unpack_kernel(parts, *refs):
    ins, out, buf, sems = refs[:parts], refs[parts], refs[parts + 1], refs[parts + 2]
    me = lax.axis_index("col")
    fx, _ = flips()
    copies = []
    for s, ref in enumerate(ins):
        square = me ^ s
        fy = lax.rem(square, 2)
        one = functools.partial(bit_row, ref, EARLY)
        split_y = jnp.abs(one(0) - one(1))
        spread(buf, (s, 0, 1), center=[ref[t].astype(F32) for t in range(4)])
        spread_edge(buf, (s, 3, 1), ref, one, (2, 3), (4, 5), (4, 5), (12, 13), split_y)
        spread_edge(buf, (s, 0, turn3(2, fy)), ref, one, (1, 3), (6, 7), (6, 7), (12, 13), 1.0 - split_y)
        spread_edge(buf, (s, 0, turn3(0, fy)), ref, one, (0, 2), (8, 9), (8, 9), (14, 15), 1.0 - split_y)
        spread_corner(buf, (s, 3, turn3(2, fy)), ref[10].astype(F32), one(3), one(10))
        spread_corner(buf, (s, 3, turn3(0, fy)), ref[11].astype(F32), one(2), one(11))
        for a in range(2):
            for g, at in ((0, 3), (3, 6 - 6 * fx)):
                copies.append(
                    pltpu.make_async_copy(
                        buf.at[s, a, g : g + 3], out.at[square, a, pl.ds(at, 3)], sems.at[len(copies)]
                    )
                )
                copies[-1].start()
    for copy in copies:
        copy.wait()


def late_unpack_kernel(parts, *refs):
    ins, out, buf, sems = refs[:parts], refs[parts + 1], refs[parts + 2], refs[parts + 3]
    me = lax.axis_index("col")
    fx, _ = flips()
    copies = []
    for s, ref in enumerate(ins):
        square = me ^ s
        fy = lax.rem(square, 2)
        one = functools.partial(bit_row, ref, LATE)
        split_y = jnp.abs(one(0) - one(1))
        spread_edge(buf, (s, 0, 1), ref, one, (0, 1), (4, 5), (0, 1), (4, 5), split_y)
        spread_corner(buf, (s, 0, turn3(2, fy)), ref[2].astype(F32), one(1), one(6))
        spread_corner(buf, (s, 0, turn3(0, fy)), ref[3].astype(F32), one(0), one(7))
        for a in range(2):
            copies.append(
                pltpu.make_async_copy(
                    buf.at[s, a], out.at[square, a, pl.ds(6 * fx, 3)], sems.at[len(copies)]
                )
            )
            copies[-1].start()
    for copy in copies:
        copy.wait()


def turn3(index, flip):
    return index + flip * (2 - 2 * index)


def bit_row(ref, count, k):
    rows = ref.shape[1]
    return ref[count + k // rows, k % rows : k % rows + 1, :].astype(F32)


def spread(buf, at, center):
    s, group, column = at
    for a in range(2):
        for b in range(2):
            buf[s, a, group + column, b] = center[2 * a + b].astype(BF16)


def spread_edge(buf, at, ref, one, ps, qs, base, extra, used):
    a_bits = [one(p) for p in ps]
    b_bits = [one(q) for q in qs]
    values = [ref[t].astype(F32) for t in base]
    more = [ref[t].astype(F32) for t in extra]
    center = [None] * 4
    for b in range(2):
        picks = [bit if b else 1.0 - bit for bit in b_bits]
        first = picks[0] * values[0] + picks[1] * values[1]
        second = (used * picks[0]) * more[0] + (used * picks[1]) * more[1]
        for a in range(2):
            ia = [bit if a else 1.0 - bit for bit in a_bits]
            center[2 * a + b] = ia[0] * first + ia[1] * second
    spread(buf, at, center)


def spread_corner(buf, at, value, a_bit, b_bit):
    center = []
    for a in range(2):
        for b in range(2):
            center.append(((a_bit if a else 1.0 - a_bit) * (b_bit if b else 1.0 - b_bit)) * value)
    spread(buf, at, center)


def unpack_early(messages):
    parts = len(messages)
    rows = messages[0].shape[1]
    return pl.pallas_call(
        functools.partial(early_unpack_kernel, parts),
        out_shape=jax.ShapeDtypeStruct((parts, 2, 9, 2, rows, BS), BF16),
        in_specs=[VMEM] * parts,
        out_specs=ANY,
        scratch_shapes=[
            pltpu.VMEM((parts, 2, 6, 2, rows, BS), BF16),
            pltpu.SemaphoreType.DMA((4 * parts,)),
        ],
        compiler_params=pltpu.CompilerParams(vmem_limit_bytes=16 << 20),
        name="unpack_early",
    )(*messages)


def unpack_late(messages, coarse):
    parts = len(messages)
    rows = messages[0].shape[1]
    return pl.pallas_call(
        functools.partial(late_unpack_kernel, parts),
        out_shape=jax.ShapeDtypeStruct(coarse.shape, BF16),
        in_specs=[VMEM] * parts + [ANY],
        out_specs=ANY,
        scratch_shapes=[
            pltpu.VMEM((parts, 2, 3, 2, rows, BS), BF16),
            pltpu.SemaphoreType.DMA((2 * parts,)),
        ],
        input_output_aliases={parts: 0},
        compiler_params=pltpu.CompilerParams(vmem_limit_bytes=16 << 20),
        name="unpack_late",
    )(*messages, coarse)


def swap(value, axis, side):
    count = lax.axis_size(axis)
    first = range(side, count - 1, 2)
    return lax.ppermute(value, axis, [(i, i + 1) for i in first] + [(i + 1, i) for i in first])


def scatter_rows(outs):
    count = len(outs)
    return [outs[0]] + [
        lax.ppermute(outs[s], "col", [(i, i ^ s) for i in range(count)]) for s in range(1, count)
    ]


def local(coupling, neighbours, prolong, aggregate):
    parts = lax.axis_size("col")
    coupling = pltpu.with_memory_space_constraint(coupling.reshape(-1, BS, BS), pltpu.HBM)
    neighbours = pltpu.with_memory_space_constraint(neighbours, pltpu.HBM)
    aggregate = pltpu.with_memory_space_constraint(aggregate, pltpu.HBM)
    prolong_rows = pltpu.with_memory_space_constraint(prolong.reshape(SIDE, SIDE * BS, BS), pltpu.HBM)
    to_row_a, to_row_b, to_col_a, to_col_b, bits = rims(aggregate, prolong_rows)
    row_a = swap(to_row_a, "row", 0)
    col_a = swap(to_col_a, "col", 0)
    col_b = swap(to_col_b, "col", 1)
    row_b = swap(to_row_b, "row", 1)
    r, center = step_one(neighbours, coupling, prolong_rows, bits)
    corner_aa = swap(row_a[1:2], "col", 0)
    corner_ab = swap(row_a[0:1], "col", 1)
    corner_ba = swap(row_b[1:2], "col", 0)
    corner_bb = swap(row_b[0:1], "col", 1)
    early = pieces(
        early_kernel,
        (bits, r, center, row_a, col_a, col_b, corner_aa, corner_ab),
        EARLY,
        parts,
        2 * 14 * BS * BS * QUAD,
        "early_terms",
    )
    late = pieces(
        late_kernel,
        (bits, r, row_b, corner_ba, corner_bb),
        LATE,
        parts,
        2 * 6 * BS * BS * QUAD,
        "late_terms",
    )
    coarse = unpack_early(scatter_rows(early))
    coarse = unpack_late(scatter_rows(late), coarse)
    return coarse[None]


def solution(mesh):
    return jax.shard_map(
        local,
        mesh=mesh,
        in_specs=(
            P("row", "col", None, None, None),
            P("row", "col", None),
            P("row", "col", None, None),
            P("row", "col"),
        ),
        out_specs=P("row", None, None, None, None, "col", None),
        check_vma=False,
    )
```

```python
import functools

import jax
import jax.numpy as jnp
from jax import lax
from jax.experimental import pallas as pl
from jax.experimental.pallas import tpu as pltpu
from jax.sharding import PartitionSpec as P

BS = 128
KA = 12
SIDE = 4
QUAD = 4 * BS
HEAD = 16
ROWS = HEAD + QUAD
TALL = BS + HEAD
SLOTS = 20
ANY = pl.BlockSpec(memory_space=pl.ANY)
VMEM = pl.BlockSpec(memory_space=pltpu.VMEM)
HBM = pl.BlockSpec(memory_space=pltpu.HBM)
BF16 = jnp.bfloat16
F32 = jnp.float32


def flips():
    return lax.rem(lax.axis_index("row"), 2), lax.rem(lax.axis_index("col"), 2)


def turned(index, flip):
    return index + flip - 2 * index * flip


def rims_kernel(agg_hbm, prolong, row_a, row_b, col_a, col_b, bits, agg, sems):
    fx, fy = flips()
    load = pltpu.make_async_copy(agg_hbm, agg, sems.at[16])
    load.start()
    copies = []
    plans = (
        (row_a, ((1, 0), (1, 1))),
        (row_b, ((0, 0), (0, 1))),
        (col_a, ((0, 1), (1, 1))),
        (col_b, ((0, 0), (1, 0))),
    )
    for out, quads in plans:
        for h, (u, v) in enumerate(quads):
            ur, vr = turned(u, fx), turned(v, fy)
            for m in range(2):
                copies.append(
                    pltpu.make_async_copy(
                        prolong.at[2 * ur + m, pl.ds(pl.multiple_of(vr * 256, 256), 256), :],
                        out.at[h, HEAD + 256 * m : HEAD + 256 * (m + 1), :],
                        sems.at[len(copies)],
                    )
                )
                copies[-1].start()
    load.wait()
    own = {}
    for k, (u, v) in enumerate(((0, 0), (0, 1), (1, 0), (1, 1))):
        own[u, v] = lax.rem(agg[2 * turned(u, fx), 2 * turned(v, fy)], 2).astype(F32)
        bits[k : k + 1, :] = jnp.full((1, BS), own[u, v], F32)
    bits[4:, :] = jnp.zeros((4, BS), F32)
    for out, quads in plans:
        for h, quad in enumerate(quads):
            out[h, 0:HEAD, :] = jnp.full((HEAD, BS), own[quad], F32).astype(BF16)
    for copy in copies:
        copy.wait()


def rims(agg, prolong_rows):
    shape = jax.ShapeDtypeStruct((2, ROWS, BS), BF16)
    return pl.pallas_call(
        rims_kernel,
        out_shape=(shape,) * 4 + (jax.ShapeDtypeStruct((8, BS), F32),),
        in_specs=[HBM, HBM],
        out_specs=(VMEM,) * 5,
        scratch_shapes=[pltpu.SMEM((SIDE, SIDE), jnp.int32), pltpu.SemaphoreType.DMA((17,))],
        compiler_params=pltpu.CompilerParams(vmem_limit_bytes=4 << 20),
        name="rims",
    )(agg, prolong_rows)


def sums(r, p, quads):
    fx, fy = flips()
    raw = 2 * turned(p[0] - 1, fx) + turned(p[1] - 1, fy)
    blocks = [r[raw, (u - p[0] + 1) * 3 + v - p[1] + 1] for u, v in quads]
    return blocks[0] if len(blocks) == 1 else jnp.concatenate(blocks, axis=1)


OWN = ((1, 1), (1, 2), (2, 1), (2, 2))
NONE = 16 * KA


def step_one_kernel(
    codes_hbm, coupling, prolong_hbm, bits, out, center, to_a, to_b, blocks, prolong, far, codes, slot_of, sems
):
    fx, fy = flips()
    load_codes = pltpu.make_async_copy(codes_hbm, codes, sems.at[8])
    load_codes.start()
    load_prolong = pltpu.make_async_copy(prolong_hbm, prolong, sems.at[9])
    load_prolong.start()

    def load(quad, m):
        first = (2 * (quad // 2) + m) * SIDE + 2 * (quad % 2)
        at = pl.ds(first * KA, 2 * KA)
        return pltpu.make_async_copy(coupling.at[at], blocks.at[at], sems.at[2 * quad + m])

    for quad in range(4):
        for m in range(2):
            load(quad, m).start()
    blocks[NONE] = jnp.zeros((BS, BS), BF16)

    @pl.loop(0, 16)
    def _(n):
        for t in range(25):
            slot_of[n * 25 + t] = NONE

    load_codes.wait()

    @pl.loop(0, 16)
    def _(n):
        for k in range(KA):
            slot_of[n * 25 + codes[n // SIDE, n % SIDE, k]] = n * KA + k

    load_prolong.wait()
    zero = jnp.zeros((BS, BS), BF16)

    @pl.loop(0, 4)
    def _(quad):
        qx, qy = quad // 2, quad % 2
        for m in range(2):
            load(quad, m).wait()
        left = []
        for ix in range(2):
            rows = prolong[2 * qx + ix, pl.ds(pl.multiple_of(qy * 256, 256), 256), :]
            left.append(rows.T)

        def block(ix, iy, jx, jy):
            if not (0 <= jy - iy <= 4):
                return zero
            n = (2 * qx + ix) * SIDE + 2 * qy + iy
            return blocks[slot_of[n * 25 + (jx - ix) * 5 + jy - iy]]

        for jx in range(6):
            for t in range(3):
                total = None
                for ix in range(2):
                    if not (0 <= jx - ix <= 4):
                        continue
                    right = jnp.concatenate(
                        [
                            jnp.concatenate([block(ix, iy, jx, 2 * t + e) for e in range(2)], axis=1)
                            for iy in range(2)
                        ],
                        axis=0,
                    )
                    part = jnp.dot(left[ix], right, preferred_element_type=F32)
                    total = part if total is None else total + part
                du, dv = jx // 2, t
                at = (du + fx * (2 - 2 * du)) * 3 + dv + fy * (2 - 2 * dv)
                out[quad, at, :, (jx % 2) * 256 : (jx % 2 + 1) * 256] = total.astype(BF16)

    for ref, e, j, q in ((to_b, 0, 2, (3, 0)), (to_b, 1, 0, (0, 0)), (to_a, 0, 3, (3, 3)), (to_a, 1, 1, (0, 3))):
        ref[e, 0:BS, :] = sums(out, OWN[j], (q,))
        bit = jnp.broadcast_to(bits[j : j + 1, :], (HEAD, BS)).astype(BF16)
        ref[e, BS:, :] = jnp.concatenate([bit] * 4, axis=1)
    for j, (u, v) in enumerate(OWN):
        ur, vr = turned(u - 1, fx), turned(v - 1, fy)
        at = pl.ds(pl.multiple_of(vr * 256, 256), 256)
        for m in range(2):
            rows = slice(QUAD * j + 256 * m, QUAD * j + 256 * (m + 1))
            part = prolong[2 * ur + m, at, :]
            high = part * bits[j : j + 1, :].astype(BF16)
            far[rows, 0:BS] = part - high
            far[rows, BS:] = high
    for i, p in enumerate(OWN):
        raw = 2 * turned(p[0] - 1, fx) + turned(p[1] - 1, fy)
        near = [out[raw, (q[0] - p[0] + 1) * 3 + q[1] - p[1] + 1] for q in OWN]
        value = jnp.dot(jnp.concatenate(near, axis=1), far[...], preferred_element_type=F32)
        for b in range(2):
            one = value[:, b * BS : (b + 1) * BS]
            high = bits[i : i + 1, :] * one
            low = one - high
            if i == 0:
                center[b] = low
                center[2 + b] = high
            else:
                center[b] += low
                center[2 + b] += high


def step_one(codes, coupling, prolong_rows, bits):
    return pl.pallas_call(
        step_one_kernel,
        out_shape=(
            jax.ShapeDtypeStruct((4, 9, BS, QUAD), BF16),
            jax.ShapeDtypeStruct((4, BS, BS), F32),
            jax.ShapeDtypeStruct((2, TALL, QUAD), BF16),
            jax.ShapeDtypeStruct((2, TALL, QUAD), BF16),
        ),
        in_specs=[HBM, HBM, HBM, VMEM],
        out_specs=(VMEM,) * 4,
        scratch_shapes=[
            pltpu.VMEM((NONE + 1, BS, BS), BF16),
            pltpu.VMEM((SIDE, SIDE * BS, BS), BF16),
            pltpu.VMEM((4 * QUAD, 2 * BS), BF16),
            pltpu.SMEM((SIDE, SIDE, KA), jnp.int32),
            pltpu.SMEM((400,), jnp.int32),
            pltpu.SemaphoreType.DMA((10,)),
        ],
        compiler_params=pltpu.CompilerParams(vmem_limit_bytes=16 << 20),
        cost_estimate=pl.CostEstimate(flops=1 << 33, bytes_accessed=1 << 20, transcendentals=0),
        name="step_one",
    )(codes, coupling, prolong_rows, bits)


def half_of(ref):
    return ref[0:1, :].astype(F32)


def edge_slots(near, far, same_a):
    same_b = 1.0 - jnp.abs(half_of(far[0]) - half_of(far[1]))
    second = far[1][HEAD:, :]
    shared = second * same_b.astype(BF16)
    right = jnp.concatenate(
        [
            jnp.concatenate([far[0][HEAD:, :], jnp.zeros_like(second)], axis=1),
            jnp.concatenate([shared, second - shared], axis=1),
        ],
        axis=0,
    )
    by_p = [jnp.dot(rows, right, preferred_element_type=F32) for rows in near]
    base, extra = [], []
    for v in range(2):
        one, two = (value[:, v * BS : (v + 1) * BS] for value in by_p)
        shared = same_a * two
        base.append(one + shared)
        extra.append(two - shared)
    return base, extra


def inside(axis, count):
    at = lax.axis_index(axis)
    return jnp.where(at == 0, 0.0, jnp.where(at == count - 1, 0.0, 1.0)).astype(F32)


def store_pieces(outs, at, values):
    rows = outs[0].shape[1]
    me = lax.axis_index("col")
    for s, out in enumerate(outs):
        start = pl.multiple_of((me ^ s) * rows, rows)
        for t in range(values.shape[0]):
            out[at + t] = values[t, pl.ds(start, rows), :].astype(BF16)


def store_head(outs, head):
    rows = outs[0].shape[1]
    for out in outs:
        for t in range(out.shape[0] - SLOTS):
            out[SLOTS + t] = head[t * rows : (t + 1) * rows, :].astype(BF16)


def edge_terms(r, bits, edges, same_a, slots, head):
    for e, (far, own, quads, scale) in enumerate(edges):
        base, extra = edge_slots([sums(r, p, quads) for p in own], [far.at[0], far.at[1]], same_a)
        for t in range(2):
            slots[2 * e + t] = base[t] if scale is None else base[t] * scale
            slots[4 + 2 * e + t] = extra[t] if scale is None else extra[t] * scale
            head[2 * e + t : 2 * e + t + 1, :] = half_of(far.at[t])


def near_kernel(counts, bits, r, center, col_a, col_b, *rest):
    outs, (head, slots) = rest[:-2], rest[-2:]
    split_y = jnp.abs(bits[0:1, :] - bits[1:2, :])
    edges = (
        (col_a, ((1, 2), (2, 2)), ((1, 3), (2, 3)), None),
        (col_b, ((1, 1), (2, 1)), ((1, 0), (2, 0)), inside("col", counts[1])),
    )
    head[...] = jnp.zeros_like(head)
    edge_terms(r, bits, edges, split_y, slots, head.at[8:12])
    head[0:4, :] = bits[0:4, :]
    store_pieces(outs, 0, center)
    store_pieces(outs, 8, slots.at[0:4])
    store_pieces(outs, 16, slots.at[4:8])


def far_kernel(counts, bits, r, row_a, row_b, from_a, from_b, head_in, *rest):
    parts = counts[1]
    ins, outs, (slots, head) = rest[:parts], rest[parts : 2 * parts], rest[2 * parts :]
    split_x = 1.0 - jnp.abs(bits[0:1, :] - bits[1:2, :])
    row_in, col_in = inside("row", counts[0]), inside("col", parts)
    edges = (
        (row_a, ((2, 1), (2, 2)), ((3, 1), (3, 2)), None),
        (row_b, ((1, 1), (1, 2)), ((0, 1), (0, 2)), row_in),
    )
    head[...] = head_in[...]
    edge_terms(r, bits, edges, split_x, slots, head.at[4:8])
    corners = (
        (from_a.at[0], row_a.at[1], None),
        (from_b.at[0], row_a.at[0], col_in),
        (from_a.at[1], row_b.at[1], row_in),
        (from_b.at[1], row_b.at[0], row_in * col_in),
    )
    for e, (near, far, scale) in enumerate(corners):
        value = jnp.dot(near[0:BS, :], far[HEAD:, :], preferred_element_type=F32)
        slots[8 + e] = value if scale is None else value * scale
        head[12 + e : 13 + e, :] = near[BS : BS + 1, 0:BS].astype(F32)
    store_pieces(outs, 4, slots.at[0:4])
    store_pieces(outs, 12, slots.at[8:12])
    rows = outs[0].shape[1]
    me = lax.axis_index("col")
    for s in range(parts):
        start = pl.multiple_of((me ^ s) * rows, rows)
        for t in range(4):
            part = slots[4 + t, pl.ds(start, rows), :] + ins[s][16 + t].astype(F32)
            outs[s][16 + t] = part.astype(BF16)
    store_head(outs, head)


def message_shapes(parts):
    rows = BS // parts
    heads = -(-HEAD // rows)
    return jax.ShapeDtypeStruct((SLOTS + heads, rows, BS), BF16), jax.ShapeDtypeStruct((heads * rows, BS), F32)


def near_terms(counts, *operands):
    message, head = message_shapes(counts[1])
    return pl.pallas_call(
        functools.partial(near_kernel, counts),
        out_shape=(message,) * counts[1] + (head,),
        in_specs=[VMEM] * len(operands),
        out_specs=(VMEM,) * (counts[1] + 1),
        scratch_shapes=[pltpu.VMEM((8, BS, BS), F32)],
        compiler_params=pltpu.CompilerParams(vmem_limit_bytes=16 << 20),
        cost_estimate=pl.CostEstimate(flops=1, bytes_accessed=1, transcendentals=0),
        name="near_terms",
    )(*operands)


def far_terms(counts, *operands):
    message, head = message_shapes(counts[1])
    first = len(operands) - counts[1]
    return pl.pallas_call(
        functools.partial(far_kernel, counts),
        out_shape=(message,) * counts[1],
        in_specs=[VMEM] * len(operands),
        out_specs=(VMEM,) * counts[1],
        scratch_shapes=[pltpu.VMEM((12, BS, BS), F32), pltpu.VMEM(head.shape, F32)],
        input_output_aliases={first + s: s for s in range(counts[1])},
        compiler_params=pltpu.CompilerParams(vmem_limit_bytes=16 << 20),
        cost_estimate=pl.CostEstimate(flops=1, bytes_accessed=1, transcendentals=0),
        name="far_terms",
    )(*operands)


def unpack_kernel(parts, steps, fresh, *refs):
    ins = refs[: len(steps)]
    out, buf, sems = refs[-3:]
    me = lax.axis_index("col")
    fx, _ = flips()
    copies = []
    for i, (s, ref) in enumerate(zip(steps, ins)):
        square = me ^ s
        fy = lax.rem(square, 2)
        one = functools.partial(bit_row, ref)
        split_y = jnp.abs(one(0) - one(1))
        split_x = 1.0 - split_y

        def send(places):
            for piece, (owner, code) in places:
                for a in range(2):
                    copies.append(
                        pltpu.make_async_copy(
                            buf.at[i, piece, a], out.at[owner, a, code], sems.at[len(copies)]
                        )
                    )
                    copies[-1].start()

        spread(buf, (i, 0), [ref[t].astype(F32) for t in range(4)])
        send([(0, (square, 4))])
        edges = (
            ((2, 3), split_y, 7 - 6 * fx),
            ((0, 1), split_y, 1 + 6 * fx),
            ((1, 3), split_x, 3 + turn3(2, fy)),
            ((0, 2), split_x, 3 + turn3(0, fy)),
        )
        for e, (ps, used, code) in enumerate(edges):
            at = 2 * e % 4
            spread_edge(
                buf, (i, 1 + e), ref, one, ps, (4 + 2 * e, 5 + 2 * e), (4 + 2 * e, 5 + 2 * e), (16 + at, 17 + at), used
            )
            send([(1 + e, (square, code))])
        high = square ^ 1
        low = square + 2 * fy - 1
        low = jnp.where((low < 0) | (low >= parts), square, low)
        for e, (owner, group, side, b_bit) in enumerate(
            ((high, 6 - 6 * fx, 2, 5), (low, 6 - 6 * fx, 0, 4), (high, 6 * fx, 2, 7), (low, 6 * fx, 0, 6))
        ):
            spread_corner(buf, (i, 5 + e), ref[12 + e].astype(F32), one(12 + e), one(b_bit))
            send([(5 + e, (owner, group + turn3(side, lax.rem(owner, 2))))])
    for copy in copies:
        copy.wait()


def unpack(messages, steps, coarse):
    parts = lax.axis_size("col")
    rows = messages[0].shape[1]
    fresh = coarse is None
    return pl.pallas_call(
        functools.partial(unpack_kernel, parts, steps, fresh),
        out_shape=jax.ShapeDtypeStruct((parts, 2, 9, 2, rows, BS), BF16),
        in_specs=[VMEM] * len(steps) + [ANY] * (not fresh),
        out_specs=ANY,
        scratch_shapes=[
            pltpu.VMEM((len(steps), 9, 2, 2, rows, BS), BF16),
            pltpu.SemaphoreType.DMA((18 * len(steps),)),
        ],
        input_output_aliases={} if fresh else {len(steps): 0},
        compiler_params=pltpu.CompilerParams(vmem_limit_bytes=16 << 20),
        cost_estimate=pl.CostEstimate(flops=1, bytes_accessed=1, transcendentals=0),
        name="unpack",
    )(*messages, *(() if fresh else (coarse,)))


def turn3(index, flip):
    return index + flip * (2 - 2 * index)


def bit_row(ref, k):
    rows = ref.shape[1]
    return ref[SLOTS + k // rows, k % rows : k % rows + 1, :].astype(F32)


def spread(buf, at, center):
    i, piece = at
    for a in range(2):
        for b in range(2):
            buf[i, piece, a, b] = center[2 * a + b].astype(BF16)


def spread_edge(buf, at, ref, one, ps, qs, base, extra, used):
    a_bits = [one(p) for p in ps]
    b_bits = [one(q) for q in qs]
    values = [ref[t].astype(F32) for t in base]
    more = [ref[t].astype(F32) for t in extra]
    center = [None] * 4
    for b in range(2):
        picks = [bit if b else 1.0 - bit for bit in b_bits]
        first = picks[0] * values[0] + picks[1] * values[1]
        second = (used * picks[0]) * more[0] + (used * picks[1]) * more[1]
        for a in range(2):
            ia = [bit if a else 1.0 - bit for bit in a_bits]
            center[2 * a + b] = ia[0] * first + ia[1] * second
    spread(buf, at, center)


def spread_corner(buf, at, value, a_bit, b_bit):
    center = []
    for a in range(2):
        for b in range(2):
            center.append(((a_bit if a else 1.0 - a_bit) * (b_bit if b else 1.0 - b_bit)) * value)
    spread(buf, at, center)


def gate_kernel(first, second, after, first_out, second_out):
    pass


def gate(first, second, after):
    return pl.pallas_call(
        gate_kernel,
        out_shape=tuple(jax.ShapeDtypeStruct(v.shape, v.dtype) for v in (first, second)),
        in_specs=[ANY, ANY, ANY],
        out_specs=(ANY, ANY),
        input_output_aliases={0: 0, 1: 1},
        compiler_params=pltpu.CompilerParams(vmem_limit_bytes=1 << 20),
        cost_estimate=pl.CostEstimate(flops=1 << 33, bytes_accessed=1, transcendentals=0),
        name="gate",
    )(first, second, after)


def other_side(index):
    return index + 1 if index % 2 else index - 1


def row_low(r, c, rows, cols):
    far = other_side(r)
    return (far, c) if 0 <= far < rows else (r, c ^ 1)


def col_low(r, c, rows, cols):
    far = other_side(c)
    return (r, far) if 0 <= far < cols else (r ^ 2, c)


def row_high(r, c, rows, cols):
    return r ^ 1, c


def col_high(r, c, rows, cols):
    return r, c ^ 1


def swap(value, partner):
    rows, cols = lax.axis_size("row"), lax.axis_size("col")
    pairs = []
    for r in range(rows):
        for c in range(cols):
            to_r, to_c = partner(r, c, rows, cols)
            pairs.append((r * cols + c, to_r * cols + to_c))
    return lax.ppermute(value, ("row", "col"), pairs)


def scatter_rows(outs):
    count = len(outs)
    return [outs[0]] + [
        lax.ppermute(outs[s], "col", [(i, i ^ s) for i in range(count)]) for s in range(1, count)
    ]


def local(coupling, neighbours, prolong, aggregate):
    parts = lax.axis_size("col")
    counts = (lax.axis_size("row"), parts)
    coupling = pltpu.with_memory_space_constraint(coupling.reshape(-1, BS, BS), pltpu.HBM)
    neighbours = pltpu.with_memory_space_constraint(neighbours, pltpu.HBM)
    aggregate = pltpu.with_memory_space_constraint(aggregate, pltpu.HBM)
    prolong_rows = pltpu.with_memory_space_constraint(prolong.reshape(SIDE, SIDE * BS, BS), pltpu.HBM)
    to_row_a, to_row_b, to_col_a, to_col_b, bits = rims(aggregate, prolong_rows)
    row_a = swap(to_row_a, row_high)
    row_b = swap(to_row_b, row_low)
    col_a = swap(to_col_a, col_high)
    col_b = swap(to_col_b, col_low)
    r, center, to_a, to_b = step_one(neighbours, coupling, prolong_rows, bits)
    from_b = swap(to_b, col_low)
    from_a = swap(to_a, col_high)
    *outs, head = near_terms(counts, bits, r, center, col_a, col_b)
    row_a, row_b = gate(row_a, row_b, head)
    outs = far_terms(counts, bits, r, row_a, row_b, from_a, from_b, head, *outs)
    outs = scatter_rows(outs)
    coarse = None
    for first, last in ((0, 2), (2, parts - 1), (parts - 1, parts)):
        coarse = unpack(outs[first:last], range(first, last), coarse)
    return coarse[None]


def solution(mesh):
    return jax.shard_map(
        local,
        mesh=mesh,
        in_specs=(
            P("row", "col", None, None, None),
            P("row", "col", None),
            P("row", "col", None, None),
            P("row", "col"),
        ),
        out_specs=P("row", None, None, None, None, "col", None),
        check_vma=False,
    )
```

```python
import functools

import jax
import jax.numpy as jnp
from jax import lax
from jax.experimental import pallas as pl
from jax.experimental.pallas import tpu as pltpu
from jax.sharding import PartitionSpec as P

BS = 128
KA = 12
SIDE = 4
QUAD = 4 * BS
HEAD = 16
ROWS = HEAD + QUAD
OWN_SLOTS = 4
SLOTS = 16
ANY = pl.BlockSpec(memory_space=pl.ANY)
VMEM = pl.BlockSpec(memory_space=pltpu.VMEM)
HBM = pl.BlockSpec(memory_space=pltpu.HBM)
BF16 = jnp.bfloat16
F32 = jnp.float32


def flips():
    return lax.rem(lax.axis_index("row"), 2), lax.rem(lax.axis_index("col"), 2)


def turned(index, flip):
    return index + flip - 2 * index * flip


def rims_kernel(agg_hbm, prolong, row_a, row_b, col_a, col_b, bits, agg, sems):
    fx, fy = flips()
    load = pltpu.make_async_copy(agg_hbm, agg, sems.at[16])
    load.start()
    copies = []
    plans = (
        (row_a, ((1, 0), (1, 1))),
        (row_b, ((0, 0), (0, 1))),
        (col_a, ((0, 1), (1, 1))),
        (col_b, ((0, 0), (1, 0))),
    )
    for out, quads in plans:
        for h, (u, v) in enumerate(quads):
            ur, vr = turned(u, fx), turned(v, fy)
            for m in range(2):
                copies.append(
                    pltpu.make_async_copy(
                        prolong.at[2 * ur + m, pl.ds(pl.multiple_of(vr * 256, 256), 256), :],
                        out.at[h, HEAD + 256 * m : HEAD + 256 * (m + 1), :],
                        sems.at[len(copies)],
                    )
                )
                copies[-1].start()
    load.wait()
    own = {}
    for k, (u, v) in enumerate(((0, 0), (0, 1), (1, 0), (1, 1))):
        own[u, v] = lax.rem(agg[2 * turned(u, fx), 2 * turned(v, fy)], 2).astype(F32)
        bits[k : k + 1, :] = jnp.full((1, BS), own[u, v], F32)
    bits[4:, :] = jnp.zeros((4, BS), F32)
    for out, quads in plans:
        for h, quad in enumerate(quads):
            out[h, 0:HEAD, :] = jnp.full((HEAD, BS), own[quad], F32).astype(BF16)
    for copy in copies:
        copy.wait()


def rims(agg, prolong_rows):
    shape = jax.ShapeDtypeStruct((2, ROWS, BS), BF16)
    return pl.pallas_call(
        rims_kernel,
        out_shape=(shape,) * 4 + (jax.ShapeDtypeStruct((8, BS), F32),),
        in_specs=[HBM, HBM],
        out_specs=(VMEM,) * 5,
        scratch_shapes=[pltpu.SMEM((SIDE, SIDE), jnp.int32), pltpu.SemaphoreType.DMA((17,))],
        compiler_params=pltpu.CompilerParams(vmem_limit_bytes=4 << 20),
        name="rims",
    )(agg, prolong_rows)


def sums(r, p, quads):
    fx, fy = flips()
    raw = 2 * turned(p[0] - 1, fx) + turned(p[1] - 1, fy)
    blocks = [r[raw, (u - p[0] + 1) * 3 + v - p[1] + 1] for u, v in quads]
    return blocks[0] if len(blocks) == 1 else jnp.concatenate(blocks, axis=1)


OWN = ((1, 1), (1, 2), (2, 1), (2, 2))
NONE = 16 * KA


def step_one_kernel(
    codes_hbm, coupling, prolong_hbm, after, out, to_a, to_b, prolong, blocks, codes, slot_of, sems
):
    fx, fy = flips()
    load_codes = pltpu.make_async_copy(codes_hbm, codes, sems.at[8])
    load_codes.start()
    load_prolong = pltpu.make_async_copy(prolong_hbm, prolong, sems.at[9])
    load_prolong.start()

    def load(quad, m):
        first = (2 * (quad // 2) + m) * SIDE + 2 * (quad % 2)
        at = pl.ds(first * KA, 2 * KA)
        return pltpu.make_async_copy(coupling.at[at], blocks.at[at], sems.at[2 * quad + m])

    for quad in range(4):
        for m in range(2):
            load(quad, m).start()
    blocks[NONE] = jnp.zeros((BS, BS), BF16)

    @pl.loop(0, 16)
    def _(n):
        for t in range(25):
            slot_of[n * 25 + t] = NONE

    load_codes.wait()

    @pl.loop(0, 16)
    def _(n):
        for k in range(KA):
            slot_of[n * 25 + codes[n // SIDE, n % SIDE, k]] = n * KA + k

    load_prolong.wait()
    zero = jnp.zeros((BS, BS), BF16)

    @pl.loop(0, 4)
    def _(quad):
        qx, qy = quad // 2, quad % 2
        for m in range(2):
            load(quad, m).wait()
        left = []
        for ix in range(2):
            rows = prolong[2 * qx + ix, pl.ds(pl.multiple_of(qy * 256, 256), 256), :]
            left.append(rows.T)

        def block(ix, iy, jx, jy):
            if not (0 <= jy - iy <= 4):
                return zero
            n = (2 * qx + ix) * SIDE + 2 * qy + iy
            return blocks[slot_of[n * 25 + (jx - ix) * 5 + jy - iy]]

        for jx in range(6):
            for t in range(3):
                total = None
                for ix in range(2):
                    if not (0 <= jx - ix <= 4):
                        continue
                    right = jnp.concatenate(
                        [
                            jnp.concatenate([block(ix, iy, jx, 2 * t + e) for e in range(2)], axis=1)
                            for iy in range(2)
                        ],
                        axis=0,
                    )
                    part = jnp.dot(left[ix], right, preferred_element_type=F32)
                    total = part if total is None else total + part
                du, dv = jx // 2, t
                at = (du + fx * (2 - 2 * du)) * 3 + dv + fy * (2 - 2 * dv)
                out[quad, at, :, (jx % 2) * 256 : (jx % 2 + 1) * 256] = total.astype(BF16)

    for ref, e, p, q in (
        (to_b, 0, (2, 1), (3, 0)),
        (to_b, 1, (1, 1), (0, 0)),
        (to_a, 0, (2, 2), (3, 3)),
        (to_a, 1, (1, 2), (0, 3)),
    ):
        ref[e] = sums(out, p, (q,))


def step_one(codes, coupling, prolong_rows, after):
    corner = jax.ShapeDtypeStruct((2, BS, QUAD), BF16)
    return pl.pallas_call(
        step_one_kernel,
        out_shape=(
            jax.ShapeDtypeStruct((4, 9, BS, QUAD), BF16),
            corner,
            corner,
            jax.ShapeDtypeStruct(prolong_rows.shape, BF16),
        ),
        in_specs=[HBM] * 3 + [ANY],
        out_specs=(VMEM,) * 4,
        scratch_shapes=[
            pltpu.VMEM((NONE + 1, BS, BS), BF16),
            pltpu.SMEM((SIDE, SIDE, KA), jnp.int32),
            pltpu.SMEM((400,), jnp.int32),
            pltpu.SemaphoreType.DMA((10,)),
        ],
        compiler_params=pltpu.CompilerParams(vmem_limit_bytes=16 << 20),
        cost_estimate=pl.CostEstimate(flops=1 << 33, bytes_accessed=1 << 20, transcendentals=0),
        name="step_one",
    )(codes, coupling, prolong_rows, after)


def half_of(ref):
    return ref[0:1, :].astype(F32)


def edge_slots(near, far, same_a):
    same_b = 1.0 - jnp.abs(half_of(far[0]) - half_of(far[1]))
    second = far[1][HEAD:, :]
    shared = second * same_b.astype(BF16)
    right = jnp.concatenate(
        [
            jnp.concatenate([far[0][HEAD:, :], jnp.zeros_like(second)], axis=1),
            jnp.concatenate([shared, second - shared], axis=1),
        ],
        axis=0,
    )
    by_p = [jnp.dot(rows, right, preferred_element_type=F32) for rows in near]
    base, extra = [], []
    for v in range(2):
        one, two = (value[:, v * BS : (v + 1) * BS] for value in by_p)
        shared = same_a * two
        base.append(one + shared)
        extra.append(two - shared)
    return base, extra


def inside(axis, count):
    at = lax.axis_index(axis)
    return jnp.where(at == 0, 0.0, jnp.where(at == count - 1, 0.0, 1.0)).astype(F32)


def store_pieces(outs, at, values):
    rows = outs[0].shape[1]
    me = lax.axis_index("col")
    for s, out in enumerate(outs):
        start = pl.multiple_of((me ^ s) * rows, rows)
        for t in range(values.shape[0]):
            out[at + t] = values[t, pl.ds(start, rows), :].astype(BF16)


def near_kernel(parts, bits, r, prolong, after, *rest):
    outs, (slots, right) = rest[:-2], rest[-2:]
    fx, fy = flips()

    def by_halves(quads, own, first):
        for j, (_, parts_of, bit) in enumerate(quads):
            for m, rows in enumerate(parts_of):
                step = rows.shape[0]
                at = QUAD * j + step * m
                high = rows * bit.astype(BF16)
                right[at : at + step, 0:BS] = rows - high
                right[at : at + step, BS:] = high
        names = [q for q, _, _ in quads]
        for i, k in enumerate(own):
            value = jnp.dot(sums(r, OWN[k], names), right[0 : QUAD * len(quads), :], preferred_element_type=F32)
            for b in range(2):
                one = value[:, b * BS : (b + 1) * BS]
                high = bits[k : k + 1, :] * one
                low = one - high
                if i == 0:
                    slots[first + b] = low
                    slots[first + 2 + b] = high
                else:
                    slots[first + b] += low
                    slots[first + 2 + b] += high

    quads = []
    for j, (u, v) in enumerate(OWN):
        ur, vr = turned(u - 1, fx), turned(v - 1, fy)
        at = pl.ds(pl.multiple_of(vr * 256, 256), 256)
        quads.append(((u, v), [prolong[2 * ur + m, at, :] for m in range(2)], bits[j : j + 1, :]))
    by_halves(quads, range(4), 0)
    rows = BS // parts
    me = lax.axis_index("col")
    for s in range(parts):
        start = pl.multiple_of((me ^ s) * rows, rows)
        out = outs[s] if s < 2 else outs[s // 2 + 1]
        for t in range(OWN_SLOTS):
            value = slots[t, pl.ds(start, rows), :].astype(BF16)
            if s < 2:
                out[t] = value
            else:
                out[s % 2, t] = value


def near_terms(parts, *operands):
    rows = BS // parts
    one = jax.ShapeDtypeStruct((OWN_SLOTS, rows, BS), BF16)
    two = jax.ShapeDtypeStruct((2, OWN_SLOTS, rows, BS), BF16)
    shapes = (one, one) + (two,) * (parts // 2 - 1)
    return pl.pallas_call(
        functools.partial(near_kernel, parts),
        out_shape=shapes,
        in_specs=[VMEM] * (len(operands) - 1) + [ANY],
        out_specs=(VMEM,) * len(shapes),
        scratch_shapes=[pltpu.VMEM((OWN_SLOTS, BS, BS), F32), pltpu.VMEM((4 * QUAD, 2 * BS), BF16)],
        compiler_params=pltpu.CompilerParams(vmem_limit_bytes=16 << 20),
        cost_estimate=pl.CostEstimate(flops=1, bytes_accessed=1, transcendentals=0),
        name="near_terms",
    )(*operands)


def far_kernel(counts, bits, r, row_a, row_b, col_a, col_b, from_a, from_b, *rest):
    outs, (slots, head) = rest[:-2], rest[-2:]
    split_y = jnp.abs(bits[0:1, :] - bits[1:2, :])
    split_x = 1.0 - split_y
    row_in, col_in = inside("row", counts[0]), inside("col", counts[1])
    head[...] = jnp.zeros_like(head)
    head[0:4, :] = bits[0:4, :]
    edges = (
        (row_a, ((2, 1), (2, 2)), ((3, 1), (3, 2)), split_x, None),
        (row_b, ((1, 1), (1, 2)), ((0, 1), (0, 2)), split_x, row_in),
        (col_a, ((1, 2), (2, 2)), ((1, 3), (2, 3)), split_y, None),
        (col_b, ((1, 1), (2, 1)), ((1, 0), (2, 0)), split_y, col_in),
    )
    for e, (far, own, quads, same_a, scale) in enumerate(edges):
        base, extra = edge_slots([sums(r, p, quads) for p in own], [far.at[0], far.at[1]], same_a)
        for t in range(2):
            slots[2 * e + t] = base[t] if scale is None else base[t] * scale
            more = extra[t] if scale is None else extra[t] * scale
            if e < 2:
                slots[12 + 2 * e + t] = more
            else:
                slots[8 + 2 * e + t] += more
            head[4 + 2 * e + t : 5 + 2 * e + t, :] = half_of(far.at[t])
    corners = (
        (from_a.at[0], row_a.at[1], None),
        (from_b.at[0], row_a.at[0], col_in),
        (from_a.at[1], row_b.at[1], row_in),
        (from_b.at[1], row_b.at[0], row_in * col_in),
    )
    for e, (near, far, scale) in enumerate(corners):
        value = jnp.dot(near[...], far[HEAD:, :], preferred_element_type=F32)
        slots[8 + e] = value if scale is None else value * scale
    store_pieces(outs, 0, slots)
    rows = outs[0].shape[1]
    for out in outs:
        for t in range(out.shape[0] - SLOTS):
            out[SLOTS + t] = head[t * rows : (t + 1) * rows, :].astype(BF16)


def far_terms(counts, *operands):
    parts = counts[1]
    rows = BS // parts
    heads = -(-HEAD // rows)
    message = jax.ShapeDtypeStruct((SLOTS + heads, rows, BS), BF16)
    return pl.pallas_call(
        functools.partial(far_kernel, counts),
        out_shape=(message,) * parts,
        in_specs=[VMEM] * len(operands),
        out_specs=(VMEM,) * parts,
        scratch_shapes=[pltpu.VMEM((SLOTS, BS, BS), F32), pltpu.VMEM((heads * rows, BS), F32)],
        compiler_params=pltpu.CompilerParams(vmem_limit_bytes=16 << 20),
        cost_estimate=pl.CostEstimate(flops=1, bytes_accessed=1, transcendentals=0),
        name="far_terms",
    )(*operands)


def place_kernel(parts, own, relayed, *rest):
    direct, (out, sems) = rest[:-3], rest[-2:]
    me = lax.axis_index("col")
    pieces = {0: own}
    for h in range(parts // 2):
        pieces[2 * h + 1] = relayed.at[h]
        if h:
            pieces[2 * h] = direct[h - 1].at[0]
    copies = []
    for s in range(parts):
        square = me ^ s
        for a in range(2):
            copies.append(
                pltpu.make_async_copy(
                    pieces[s].at[2 * a : 2 * a + 2], out.at[square, a, 4], sems.at[len(copies)]
                )
            )
            copies[-1].start()
    for copy in copies:
        copy.wait()


def place(own, relayed, direct, coarse):
    parts = lax.axis_size("col")
    return pl.pallas_call(
        functools.partial(place_kernel, parts),
        out_shape=jax.ShapeDtypeStruct(coarse.shape, BF16),
        in_specs=[VMEM] * (2 + len(direct)) + [ANY],
        out_specs=ANY,
        scratch_shapes=[pltpu.SemaphoreType.DMA((2 * parts,))],
        input_output_aliases={2 + len(direct): 0},
        compiler_params=pltpu.CompilerParams(vmem_limit_bytes=4 << 20),
        cost_estimate=pl.CostEstimate(flops=1, bytes_accessed=1, transcendentals=0),
        name="place",
    )(own, relayed, *direct, coarse)


def unpack_kernel(parts, steps, *refs):
    ins = refs[: len(steps)]
    out, buf, sems = refs[-3:]
    me = lax.axis_index("col")
    fx, _ = flips()
    copies = []
    for i, (s, ref) in enumerate(zip(steps, ins)):
        square = me ^ s
        fy = lax.rem(square, 2)
        one = functools.partial(bit_row, ref)
        split_y = jnp.abs(one(0) - one(1))

        def send(piece, owner, code):
            for a in range(2):
                copies.append(
                    pltpu.make_async_copy(buf.at[i, piece, a], out.at[owner, a, code], sems.at[len(copies)])
                )
                copies[-1].start()

        split_x = 1.0 - split_y
        edges = (
            ((2, 3), (12, 13), split_y, 7 - 6 * fx),
            ((0, 1), (14, 15), split_y, 1 + 6 * fx),
            ((1, 3), (12, 13), split_x, 3 + turn3(2, fy)),
            ((0, 2), (14, 15), split_x, 3 + turn3(0, fy)),
        )
        for e, (ps, more, used, code) in enumerate(edges):
            spread_edge(buf, (i, e), ref, one, ps, (4 + 2 * e, 5 + 2 * e), (2 * e, 2 * e + 1), more, used)
            send(e, square, code)
        high = square ^ 1
        low = square + 2 * fy - 1
        low = jnp.where((low < 0) | (low >= parts), square, low)
        corners = (
            (high, 6 - 6 * fx, 2, 9, 5),
            (low, 6 - 6 * fx, 0, 11, 4),
            (high, 6 * fx, 2, 8, 7),
            (low, 6 * fx, 0, 10, 6),
        )
        for e, (owner, group, side, a_bit, b_bit) in enumerate(corners):
            spread_corner(buf, (i, 4 + e), ref[8 + e].astype(F32), one(a_bit), one(b_bit))
            send(4 + e, owner, group + turn3(side, lax.rem(owner, 2)))
    for copy in copies:
        copy.wait()


def unpack(messages, steps, coarse):
    parts = lax.axis_size("col")
    rows = messages[0].shape[1]
    fresh = coarse is None
    return pl.pallas_call(
        functools.partial(unpack_kernel, parts, steps),
        out_shape=jax.ShapeDtypeStruct((parts, 2, 9, 2, rows, BS), BF16),
        in_specs=[VMEM] * len(steps) + [ANY] * (not fresh),
        out_specs=ANY,
        scratch_shapes=[
            pltpu.VMEM((len(steps), 8, 2, 2, rows, BS), BF16),
            pltpu.SemaphoreType.DMA((16 * len(steps),)),
        ],
        input_output_aliases={} if fresh else {len(steps): 0},
        compiler_params=pltpu.CompilerParams(vmem_limit_bytes=16 << 20),
        cost_estimate=pl.CostEstimate(flops=1, bytes_accessed=1, transcendentals=0),
        name="unpack",
    )(*messages, *(() if fresh else (coarse,)))


def turn3(index, flip):
    return index + flip * (2 - 2 * index)


def bit_row(ref, k):
    rows = ref.shape[1]
    return ref[SLOTS + k // rows, k % rows : k % rows + 1, :].astype(F32)


def spread(buf, at, center):
    i, piece = at
    for a in range(2):
        for b in range(2):
            buf[i, piece, a, b] = center[2 * a + b].astype(BF16)


def spread_edge(buf, at, ref, one, ps, qs, base, extra, used):
    a_bits = [one(p) for p in ps]
    b_bits = [one(q) for q in qs]
    values = [ref[t].astype(F32) for t in base]
    more = [ref[t].astype(F32) for t in extra]
    center = [None] * 4
    for b in range(2):
        picks = [bit if b else 1.0 - bit for bit in b_bits]
        first = picks[0] * values[0] + picks[1] * values[1]
        second = (used * picks[0]) * more[0] + (used * picks[1]) * more[1]
        for a in range(2):
            ia = [bit if a else 1.0 - bit for bit in a_bits]
            center[2 * a + b] = ia[0] * first + ia[1] * second
    spread(buf, at, center)


def spread_corner(buf, at, value, a_bit, b_bit):
    center = []
    for a in range(2):
        for b in range(2):
            center.append(((a_bit if a else 1.0 - a_bit) * (b_bit if b else 1.0 - b_bit)) * value)
    spread(buf, at, center)


def gate_kernel(*refs):
    pass


def gate(values, after):
    count = len(values)
    return pl.pallas_call(
        gate_kernel,
        out_shape=tuple(jax.ShapeDtypeStruct(v.shape, v.dtype) for v in values),
        in_specs=[ANY] * (count + len(after)),
        out_specs=(ANY,) * count,
        input_output_aliases={i: i for i in range(count)},
        compiler_params=pltpu.CompilerParams(vmem_limit_bytes=1 << 20),
        cost_estimate=pl.CostEstimate(flops=1 << 33, bytes_accessed=1, transcendentals=0),
        name="gate",
    )(*values, *after)


def other_side(index):
    return index + 1 if index % 2 else index - 1


def row_low(r, c, rows, cols):
    far = other_side(r)
    return (far, c) if 0 <= far < rows else (r, c ^ 1)


def col_low(r, c, rows, cols):
    far = other_side(c)
    return (r, far) if 0 <= far < cols else (r ^ 2, c)


def row_high(r, c, rows, cols):
    return r ^ 1, c


def col_high(r, c, rows, cols):
    return r, c ^ 1


def swap(value, partner):
    rows, cols = lax.axis_size("row"), lax.axis_size("col")
    pairs = []
    for r in range(rows):
        for c in range(cols):
            to_r, to_c = partner(r, c, rows, cols)
            pairs.append((r * cols + c, to_r * cols + to_c))
    return lax.ppermute(value, ("row", "col"), pairs)


def xor_swap(value, s):
    return lax.ppermute(value, "col", [(i, i ^ s) for i in range(lax.axis_size("col"))])


def local(coupling, neighbours, prolong, aggregate):
    parts = lax.axis_size("col")
    counts = (lax.axis_size("row"), parts)
    coupling = pltpu.with_memory_space_constraint(coupling.reshape(-1, BS, BS), pltpu.HBM)
    neighbours = pltpu.with_memory_space_constraint(neighbours, pltpu.HBM)
    aggregate = pltpu.with_memory_space_constraint(aggregate, pltpu.HBM)
    prolong_rows = pltpu.with_memory_space_constraint(prolong.reshape(SIDE, SIDE * BS, BS), pltpu.HBM)
    to_row_a, to_row_b, to_col_a, to_col_b, bits = rims(aggregate, prolong_rows)
    row_a = swap(to_row_a, row_high)
    row_b = swap(to_row_b, row_low)
    col_a = swap(to_col_a, col_high)
    col_b = swap(to_col_b, col_low)
    r, to_a, to_b, own_blocks = step_one(neighbours, coupling, prolong_rows, bits)
    from_b = swap(to_b, col_low)
    from_a = swap(to_a, col_high)
    mine, pair, *cross = near_terms(parts, bits, r, own_blocks, col_a)
    from_a, *cross = lax.optimization_barrier((from_a, *cross))
    direct = [xor_swap(value, 2 * h + 2) for h, value in enumerate(cross)]
    row_a, row_b, col_b, from_b = gate((row_a, row_b, col_b, from_b), (mine,))
    outs = list(far_terms(counts, bits, r, row_a, row_b, col_a, col_b, from_a, from_b))
    outs[0], *direct = lax.optimization_barrier((outs[0], *direct))
    outs = [outs[0]] + [xor_swap(outs[s], s) for s in range(1, parts)]
    relayed = xor_swap(jnp.stack([pair] + [value[1] for value in direct]), 1)
    coarse = unpack(outs[:2], range(2), None)
    coarse = place(mine, relayed, direct, coarse)
    coarse = unpack(outs[2:], range(2, parts), coarse)
    return coarse[None]


def solution(mesh):
    return jax.shard_map(
        local,
        mesh=mesh,
        in_specs=(
            P("row", "col", None, None, None),
            P("row", "col", None),
            P("row", "col", None, None),
            P("row", "col"),
        ),
        out_specs=P("row", None, None, None, None, "col", None),
        check_vma=False,
    )
```

```python
import functools

import jax
import jax.numpy as jnp
from jax import lax
from jax.experimental import pallas as pl
from jax.experimental.pallas import tpu as pltpu
from jax.sharding import PartitionSpec as P

BS = 128
KA = 12
SIDE = 4
QUAD = 4 * BS
HEAD = 8
ROWS = 2 * QUAD + HEAD
BITS = 16
OWN_SLOTS = 4
SLOTS = 16
ANY = pl.BlockSpec(memory_space=pl.ANY)
VMEM = pl.BlockSpec(memory_space=pltpu.VMEM)
HBM = pl.BlockSpec(memory_space=pltpu.HBM)
BF16 = jnp.bfloat16
F32 = jnp.float32


def flips():
    return lax.rem(lax.axis_index("row"), 2), lax.rem(lax.axis_index("col"), 2)


def turned(index, flip):
    return index + flip - 2 * index * flip


def rims_kernel(agg_hbm, prolong, row_a, row_b, col_a, col_b, bits, agg, sems):
    fx, fy = flips()
    load = pltpu.make_async_copy(agg_hbm, agg, sems.at[16])
    load.start()
    copies = []
    plans = (
        (row_a, ((1, 0), (1, 1))),
        (row_b, ((0, 0), (0, 1))),
        (col_a, ((0, 1), (1, 1))),
        (col_b, ((0, 0), (1, 0))),
    )
    for out, quads in plans:
        for h, (u, v) in enumerate(quads):
            ur, vr = turned(u, fx), turned(v, fy)
            for m in range(2):
                copies.append(
                    pltpu.make_async_copy(
                        prolong.at[2 * ur + m, pl.ds(pl.multiple_of(vr * 256, 256), 256), :],
                        out.at[QUAD * h + 256 * m : QUAD * h + 256 * (m + 1), :],
                        sems.at[len(copies)],
                    )
                )
                copies[-1].start()
    load.wait()
    own = {}
    for k, (u, v) in enumerate(((0, 0), (0, 1), (1, 0), (1, 1))):
        own[u, v] = lax.rem(agg[2 * turned(u, fx), 2 * turned(v, fy)], 2).astype(F32)
        bits[k : k + 1, :] = jnp.full((1, BS), own[u, v], F32)
    bits[4:, :] = jnp.zeros((4, BS), F32)
    for out, quads in plans:
        at = lax.broadcasted_iota(jnp.int32, (HEAD, BS), 0)
        out[2 * QUAD :, :] = jnp.where(at == 0, own[quads[0]], own[quads[1]]).astype(BF16)
    for copy in copies:
        copy.wait()


def rims(agg, prolong_rows):
    shape = jax.ShapeDtypeStruct((ROWS, BS), BF16)
    return pl.pallas_call(
        rims_kernel,
        out_shape=(shape,) * 4 + (jax.ShapeDtypeStruct((8, BS), F32),),
        in_specs=[HBM, HBM],
        out_specs=(VMEM,) * 5,
        scratch_shapes=[pltpu.SMEM((SIDE, SIDE), jnp.int32), pltpu.SemaphoreType.DMA((17,))],
        compiler_params=pltpu.CompilerParams(vmem_limit_bytes=4 << 20),
        name="rims",
    )(agg, prolong_rows)


def sums(r, p, quads):
    fx, fy = flips()
    raw = 2 * turned(p[0] - 1, fx) + turned(p[1] - 1, fy)
    blocks = [r[raw, (u - p[0] + 1) * 3 + v - p[1] + 1] for u, v in quads]
    return blocks[0] if len(blocks) == 1 else jnp.concatenate(blocks, axis=1)


OWN = ((1, 1), (1, 2), (2, 1), (2, 2))
NONE = 16 * KA


def step_one_kernel(
    codes_hbm, coupling, prolong_hbm, after, out, to_a, to_b, prolong, blocks, codes, slot_of, sems
):
    fx, fy = flips()
    load_codes = pltpu.make_async_copy(codes_hbm, codes, sems.at[8])
    load_codes.start()
    load_prolong = pltpu.make_async_copy(prolong_hbm, prolong, sems.at[9])
    load_prolong.start()

    def load(quad, m):
        first = (2 * (quad // 2) + m) * SIDE + 2 * (quad % 2)
        at = pl.ds(first * KA, 2 * KA)
        return pltpu.make_async_copy(coupling.at[at], blocks.at[at], sems.at[2 * quad + m])

    def start(quad):
        for m in range(2):
            load(quad, m).start()

    start(0)
    blocks[NONE] = jnp.zeros((BS, BS), BF16)

    @pl.loop(0, 16)
    def _(n):
        for t in range(25):
            slot_of[n * 25 + t] = NONE

    start(1)
    load_codes.wait()

    @pl.loop(0, 16)
    def _(n):
        for k in range(KA):
            slot_of[n * 25 + codes[n // SIDE, n % SIDE, k]] = n * KA + k

    start(2)
    load_prolong.wait()
    zero = jnp.zeros((BS, BS), BF16)

    @pl.loop(0, 4)
    def _(quad):
        qx, qy = quad // 2, quad % 2
        for m in range(2):
            load(quad, m).wait()

        @pl.when(quad == 0)
        def _():
            start(3)

        left = []
        for ix in range(2):
            rows = prolong[2 * qx + ix, pl.ds(pl.multiple_of(qy * 256, 256), 256), :]
            left.append(rows.T)

        def block(ix, iy, jx, jy):
            if not (0 <= jy - iy <= 4):
                return zero
            n = (2 * qx + ix) * SIDE + 2 * qy + iy
            return blocks[slot_of[n * 25 + (jx - ix) * 5 + jy - iy]]

        for jx in range(6):
            for t in range(3):
                total = None
                for ix in range(2):
                    if not (0 <= jx - ix <= 4):
                        continue
                    right = jnp.concatenate(
                        [
                            jnp.concatenate([block(ix, iy, jx, 2 * t + e) for e in range(2)], axis=1)
                            for iy in range(2)
                        ],
                        axis=0,
                    )
                    part = jnp.dot(left[ix], right, preferred_element_type=F32)
                    total = part if total is None else total + part
                du, dv = jx // 2, t
                at = (du + fx * (2 - 2 * du)) * 3 + dv + fy * (2 - 2 * dv)
                out[quad, at, :, (jx % 2) * 256 : (jx % 2 + 1) * 256] = total.astype(BF16)

    for ref, e, p, q in (
        (to_b, 0, (2, 1), (3, 0)),
        (to_b, 1, (1, 1), (0, 0)),
        (to_a, 0, (2, 2), (3, 3)),
        (to_a, 1, (1, 2), (0, 3)),
    ):
        ref[e] = sums(out, p, (q,))


def step_one(codes, coupling, prolong_rows, after):
    corner = jax.ShapeDtypeStruct((2, BS, QUAD), BF16)
    return pl.pallas_call(
        step_one_kernel,
        out_shape=(
            jax.ShapeDtypeStruct((4, 9, BS, QUAD), BF16),
            corner,
            corner,
            jax.ShapeDtypeStruct(prolong_rows.shape, BF16),
        ),
        in_specs=[HBM] * 3 + [ANY],
        out_specs=(VMEM,) * 4,
        scratch_shapes=[
            pltpu.VMEM((NONE + 1, BS, BS), BF16),
            pltpu.SMEM((SIDE, SIDE, KA), jnp.int32),
            pltpu.SMEM((400,), jnp.int32),
            pltpu.SemaphoreType.DMA((10,)),
        ],
        compiler_params=pltpu.CompilerParams(vmem_limit_bytes=16 << 20),
        cost_estimate=pl.CostEstimate(flops=1 << 33, bytes_accessed=1 << 20, transcendentals=0),
        name="step_one",
    )(codes, coupling, prolong_rows, after)


def half_of(ref, h):
    return ref[2 * QUAD + h : 2 * QUAD + h + 1, :].astype(F32)


def quad_of(ref, h):
    return ref[QUAD * h : QUAD * (h + 1), :]


def edge_slots(near, far, same_a):
    same_b = 1.0 - jnp.abs(half_of(far, 0) - half_of(far, 1))
    second = quad_of(far, 1)
    shared = second * same_b.astype(BF16)
    right = jnp.concatenate(
        [
            jnp.concatenate([quad_of(far, 0), jnp.zeros_like(second)], axis=1),
            jnp.concatenate([shared, second - shared], axis=1),
        ],
        axis=0,
    )
    by_p = [jnp.dot(rows, right, preferred_element_type=F32) for rows in near]
    base, extra = [], []
    for v in range(2):
        one, two = (value[:, v * BS : (v + 1) * BS] for value in by_p)
        shared = same_a * two
        base.append(one + shared)
        extra.append(two - shared)
    return base, extra


def inside(axis, count):
    at = lax.axis_index(axis)
    return jnp.where(at == 0, 0.0, jnp.where(at == count - 1, 0.0, 1.0)).astype(F32)


def store_pieces(outs, at, values):
    rows = BS // len(outs)
    me = lax.axis_index("col")
    for s, out in enumerate(outs):
        start = pl.multiple_of((me ^ s) * rows, rows)
        for t in range(values.shape[0]):
            first = (at + t) * rows
            out[first : first + rows, :] = values[t, pl.ds(start, rows), :].astype(BF16)


def near_kernel(parts, bits, r, prolong, after, *rest):
    outs, (slots, right) = rest[:-2], rest[-2:]
    fx, fy = flips()

    def by_halves(quads, own, first):
        for j, (_, parts_of, bit) in enumerate(quads):
            for m, rows in enumerate(parts_of):
                step = rows.shape[0]
                at = QUAD * j + step * m
                high = rows * bit.astype(BF16)
                right[at : at + step, 0:BS] = rows - high
                right[at : at + step, BS:] = high
        names = [q for q, _, _ in quads]
        for i, k in enumerate(own):
            value = jnp.dot(sums(r, OWN[k], names), right[0 : QUAD * len(quads), :], preferred_element_type=F32)
            for b in range(2):
                one = value[:, b * BS : (b + 1) * BS]
                high = bits[k : k + 1, :] * one
                low = one - high
                if i == 0:
                    slots[first + b] = low
                    slots[first + 2 + b] = high
                else:
                    slots[first + b] += low
                    slots[first + 2 + b] += high

    quads = []
    for j, (u, v) in enumerate(OWN):
        ur, vr = turned(u - 1, fx), turned(v - 1, fy)
        at = pl.ds(pl.multiple_of(vr * 256, 256), 256)
        quads.append(((u, v), [prolong[2 * ur + m, at, :] for m in range(2)], bits[j : j + 1, :]))
    by_halves(quads, range(4), 0)
    rows = BS // parts
    me = lax.axis_index("col")
    for s in range(parts):
        start = pl.multiple_of((me ^ s) * rows, rows)
        out = outs[s] if s < 2 else outs[s // 2 + 1]
        for t in range(OWN_SLOTS):
            value = slots[t, pl.ds(start, rows), :].astype(BF16)
            if s < 2:
                out[t] = value
            else:
                out[s % 2, t] = value


def near_terms(parts, *operands):
    rows = BS // parts
    one = jax.ShapeDtypeStruct((OWN_SLOTS, rows, BS), BF16)
    two = jax.ShapeDtypeStruct((2, OWN_SLOTS, rows, BS), BF16)
    shapes = (one, one) + (two,) * (parts // 2 - 1)
    return pl.pallas_call(
        functools.partial(near_kernel, parts),
        out_shape=shapes,
        in_specs=[VMEM] * (len(operands) - 1) + [ANY],
        out_specs=(VMEM,) * len(shapes),
        scratch_shapes=[pltpu.VMEM((OWN_SLOTS, BS, BS), F32), pltpu.VMEM((4 * QUAD, 2 * BS), BF16)],
        compiler_params=pltpu.CompilerParams(vmem_limit_bytes=16 << 20),
        cost_estimate=pl.CostEstimate(flops=1, bytes_accessed=1, transcendentals=0),
        name="near_terms",
    )(*operands)


def fill_edges(r, edges, slots, head):
    for e, (far, own, quads, same_a, scale) in enumerate(edges):
        base, extra = edge_slots([sums(r, p, quads) for p in own], far, same_a)
        for t in range(2):
            slots[2 * e + t] = base[t] if scale is None else base[t] * scale
            slots[4 + 2 * e + t] = extra[t] if scale is None else extra[t] * scale
            head[2 * e + t : 2 * e + t + 1, :] = half_of(far, t)


def mid_kernel(parts, bits, r, col_a, col_b, slots, head):
    split_y = jnp.abs(bits[0:1, :] - bits[1:2, :])
    edges = (
        (col_a, ((1, 2), (2, 2)), ((1, 3), (2, 3)), split_y, None),
        (col_b, ((1, 1), (2, 1)), ((1, 0), (2, 0)), split_y, inside("col", parts)),
    )
    fill_edges(r, edges, slots, head)
    head[4:8, :] = bits[0:4, :]


def mid_terms(parts, *operands):
    return pl.pallas_call(
        functools.partial(mid_kernel, parts),
        out_shape=(jax.ShapeDtypeStruct((8, BS, BS), F32), jax.ShapeDtypeStruct((8, BS), F32)),
        in_specs=[VMEM] * len(operands),
        out_specs=(VMEM, VMEM),
        compiler_params=pltpu.CompilerParams(vmem_limit_bytes=8 << 20),
        cost_estimate=pl.CostEstimate(flops=1, bytes_accessed=1, transcendentals=0),
        name="mid_terms",
    )(*operands)


def far_kernel(counts, bits, r, row_a, row_b, from_a, from_b, columns, column_head, *rest):
    outs, (slots, head) = rest[:-2], rest[-2:]
    split_x = 1.0 - jnp.abs(bits[0:1, :] - bits[1:2, :])
    row_in, col_in = inside("row", counts[0]), inside("col", counts[1])
    head[...] = jnp.zeros_like(head)
    head[0:4, :] = bits[0:4, :]
    head[8:12, :] = column_head[0:4, :]
    edges = (
        (row_a, ((2, 1), (2, 2)), ((3, 1), (3, 2)), split_x, None),
        (row_b, ((1, 1), (1, 2)), ((0, 1), (0, 2)), split_x, row_in),
    )
    fill_edges(r, edges, slots, head.at[4:8])
    for t in range(4):
        slots[4 + t] += columns[4 + t]
    corners = (
        (from_a.at[0], quad_of(row_a, 1), None),
        (from_b.at[0], quad_of(row_a, 0), col_in),
        (from_a.at[1], quad_of(row_b, 1), row_in),
        (from_b.at[1], quad_of(row_b, 0), row_in * col_in),
    )
    for e, (near, far, scale) in enumerate(corners):
        value = jnp.dot(near[...], far, preferred_element_type=F32)
        slots[8 + e] = value if scale is None else value * scale
    store_pieces(outs, 0, slots.at[0:4])
    store_pieces(outs, 4, columns.at[0:4])
    store_pieces(outs, 8, slots.at[8:12])
    store_pieces(outs, 12, slots.at[4:8])
    for out in outs:
        out[out.shape[0] - BITS :, :] = head[...].astype(BF16)


def far_terms(counts, *operands):
    parts = counts[1]
    message = jax.ShapeDtypeStruct((SLOTS * (BS // parts) + BITS, BS), BF16)
    return pl.pallas_call(
        functools.partial(far_kernel, counts),
        out_shape=(message,) * parts,
        in_specs=[VMEM] * len(operands),
        out_specs=(VMEM,) * parts,
        scratch_shapes=[pltpu.VMEM((12, BS, BS), F32), pltpu.VMEM((BITS, BS), F32)],
        compiler_params=pltpu.CompilerParams(vmem_limit_bytes=16 << 20),
        cost_estimate=pl.CostEstimate(flops=1, bytes_accessed=1, transcendentals=0),
        name="far_terms",
    )(*operands)


def place_kernel(parts, own, relayed, *rest):
    direct, (out, sems) = rest[:-3], rest[-2:]
    me = lax.axis_index("col")
    pieces = {0: own}
    for h in range(parts // 2):
        pieces[2 * h + 1] = relayed.at[h]
        if h:
            pieces[2 * h] = direct[h - 1].at[0]
    copies = []
    for s in range(parts):
        square = me ^ s
        for a in range(2):
            copies.append(
                pltpu.make_async_copy(
                    pieces[s].at[2 * a : 2 * a + 2], out.at[square, a, 4], sems.at[len(copies)]
                )
            )
            copies[-1].start()
    for copy in copies:
        copy.wait()


def place(own, relayed, direct, coarse):
    parts = lax.axis_size("col")
    return pl.pallas_call(
        functools.partial(place_kernel, parts),
        out_shape=jax.ShapeDtypeStruct(coarse.shape, BF16),
        in_specs=[VMEM] * (2 + len(direct)) + [ANY],
        out_specs=ANY,
        scratch_shapes=[pltpu.SemaphoreType.DMA((2 * parts,))],
        input_output_aliases={2 + len(direct): 0},
        compiler_params=pltpu.CompilerParams(vmem_limit_bytes=4 << 20),
        cost_estimate=pl.CostEstimate(flops=1, bytes_accessed=1, transcendentals=0),
        name="place",
    )(own, relayed, *direct, coarse)


def unpack_kernel(parts, steps, *refs):
    ins = refs[: len(steps)]
    out, buf, sems = refs[-3:]
    me = lax.axis_index("col")
    fx, _ = flips()
    copies = []
    for i, (s, ref) in enumerate(zip(steps, ins)):
        square = me ^ s
        fy = lax.rem(square, 2)
        one = functools.partial(bit_row, ref)
        split_y = jnp.abs(one(0) - one(1))

        def send(piece, owner, code):
            copies.append(pltpu.make_async_copy(buf.at[i, piece], out.at[owner, :, code], sems.at[len(copies)]))
            copies[-1].start()

        split_x = 1.0 - split_y
        edges = (
            ((2, 3), (12, 13), split_y, 7 - 6 * fx),
            ((0, 1), (14, 15), split_y, 1 + 6 * fx),
            ((1, 3), (12, 13), split_x, 3 + turn3(2, fy)),
            ((0, 2), (14, 15), split_x, 3 + turn3(0, fy)),
        )
        for e, (ps, more, used, code) in enumerate(edges):
            spread_edge(buf, (i, e), ref, one, ps, (4 + 2 * e, 5 + 2 * e), (2 * e, 2 * e + 1), more, used)
            send(e, square, code)
        high = square ^ 1
        low = square + 2 * fy - 1
        low = jnp.where((low < 0) | (low >= parts), square, low)
        corners = (
            (high, 6 - 6 * fx, 2, 9, 5),
            (low, 6 - 6 * fx, 0, 11, 4),
            (high, 6 * fx, 2, 8, 7),
            (low, 6 * fx, 0, 10, 6),
        )
        for e, (owner, group, side, a_bit, b_bit) in enumerate(corners):
            spread_corner(buf, (i, 4 + e), slot(ref, 8 + e), one(a_bit), one(b_bit))
            send(4 + e, owner, group + turn3(side, lax.rem(owner, 2)))
    for copy in copies:
        copy.wait()


def unpack(messages, steps, coarse):
    parts = lax.axis_size("col")
    rows = BS // parts
    fresh = coarse is None
    return pl.pallas_call(
        functools.partial(unpack_kernel, parts, steps),
        out_shape=jax.ShapeDtypeStruct((parts, 2, 9, 2, rows, BS), BF16),
        in_specs=[VMEM] * len(steps) + [ANY] * (not fresh),
        out_specs=ANY,
        scratch_shapes=[
            pltpu.VMEM((len(steps), 8, 2, 2, rows, BS), BF16),
            pltpu.SemaphoreType.DMA((8 * len(steps),)),
        ],
        input_output_aliases={} if fresh else {len(steps): 0},
        compiler_params=pltpu.CompilerParams(vmem_limit_bytes=16 << 20),
        cost_estimate=pl.CostEstimate(flops=1, bytes_accessed=1, transcendentals=0),
        name="unpack",
    )(*messages, *(() if fresh else (coarse,)))


def turn3(index, flip):
    return index + flip * (2 - 2 * index)


def bit_row(ref, k):
    at = ref.shape[0] - BITS + k
    return ref[at : at + 1, :].astype(F32)


def slot(ref, t):
    rows = (ref.shape[0] - BITS) // SLOTS
    return ref[t * rows : (t + 1) * rows, :].astype(F32)


def spread(buf, at, center):
    i, piece = at
    for a in range(2):
        for b in range(2):
            buf[i, piece, a, b] = center[2 * a + b].astype(BF16)


def spread_edge(buf, at, ref, one, ps, qs, base, extra, used):
    a_bits = [one(p) for p in ps]
    b_bits = [one(q) for q in qs]
    values = [slot(ref, t) for t in base]
    more = [slot(ref, t) for t in extra]
    center = [None] * 4
    for b in range(2):
        picks = [bit if b else 1.0 - bit for bit in b_bits]
        first = picks[0] * values[0] + picks[1] * values[1]
        second = (used * picks[0]) * more[0] + (used * picks[1]) * more[1]
        for a in range(2):
            ia = [bit if a else 1.0 - bit for bit in a_bits]
            center[2 * a + b] = ia[0] * first + ia[1] * second
    spread(buf, at, center)


def spread_corner(buf, at, value, a_bit, b_bit):
    center = []
    for a in range(2):
        for b in range(2):
            center.append(((a_bit if a else 1.0 - a_bit) * (b_bit if b else 1.0 - b_bit)) * value)
    spread(buf, at, center)


def gate_kernel(*refs):
    pass


def gate(values, after):
    count = len(values)
    return pl.pallas_call(
        gate_kernel,
        out_shape=tuple(jax.ShapeDtypeStruct(v.shape, v.dtype) for v in values),
        in_specs=[ANY] * (count + len(after)),
        out_specs=(ANY,) * count,
        input_output_aliases={i: i for i in range(count)},
        compiler_params=pltpu.CompilerParams(vmem_limit_bytes=1 << 20),
        cost_estimate=pl.CostEstimate(flops=1 << 33, bytes_accessed=1, transcendentals=0),
        name="gate",
    )(*values, *after)


def other_side(index):
    return index + 1 if index % 2 else index - 1


def row_low(r, c, rows, cols):
    far = other_side(r)
    return (far, c) if 0 <= far < rows else (r, c ^ 1)


def col_low(r, c, rows, cols):
    far = other_side(c)
    return (r, far) if 0 <= far < cols else (r ^ 2, c)


def row_high(r, c, rows, cols):
    return r ^ 1, c


def col_high(r, c, rows, cols):
    return r, c ^ 1


def swap(value, partner):
    rows, cols = lax.axis_size("row"), lax.axis_size("col")
    pairs = []
    for r in range(rows):
        for c in range(cols):
            to_r, to_c = partner(r, c, rows, cols)
            pairs.append((r * cols + c, to_r * cols + to_c))
    return lax.ppermute(value, ("row", "col"), pairs)


def xor_swap(value, s):
    return lax.ppermute(value, "col", [(i, i ^ s) for i in range(lax.axis_size("col"))])


def local(coupling, neighbours, prolong, aggregate):
    parts = lax.axis_size("col")
    counts = (lax.axis_size("row"), parts)
    coupling = pltpu.with_memory_space_constraint(coupling.reshape(-1, BS, BS), pltpu.HBM)
    neighbours = pltpu.with_memory_space_constraint(neighbours, pltpu.HBM)
    aggregate = pltpu.with_memory_space_constraint(aggregate, pltpu.HBM)
    prolong_rows = pltpu.with_memory_space_constraint(prolong.reshape(SIDE, SIDE * BS, BS), pltpu.HBM)
    to_row_a, to_row_b, to_col_a, to_col_b, bits = rims(aggregate, prolong_rows)
    row_a = swap(to_row_a, row_high)
    row_b = swap(to_row_b, row_low)
    col_a = swap(to_col_a, col_high)
    col_b = swap(to_col_b, col_low)
    r, to_a, to_b, own_blocks = step_one(neighbours, coupling, prolong_rows, bits)
    from_b = swap(to_b, col_low)
    from_a = swap(to_a, col_high)
    mine, pair, *cross = near_terms(parts, bits, r, own_blocks, col_a)
    from_a, *cross = lax.optimization_barrier((from_a, *cross))
    direct = [xor_swap(value, 2 * h + 2) for h, value in enumerate(cross)]
    columns, column_head = mid_terms(parts, bits, r, col_a, col_b)
    row_a, row_b, columns, from_b = gate((row_a, row_b, columns, from_b), (mine,))
    outs = list(far_terms(counts, bits, r, row_a, row_b, from_a, from_b, columns, column_head))
    outs[0], *direct = lax.optimization_barrier((outs[0], *direct))
    outs = [outs[0]] + [xor_swap(outs[s], s) for s in range(1, parts)]
    relayed = xor_swap(jnp.stack([pair] + [value[1] for value in direct]), 1)
    coarse = unpack(outs[:2], range(2), None)
    coarse = place(mine, relayed, direct, coarse)
    coarse = unpack(outs[2:], range(2, parts), coarse)
    return coarse[None]


def solution(mesh):
    return jax.shard_map(
        local,
        mesh=mesh,
        in_specs=(
            P("row", "col", None, None, None),
            P("row", "col", None),
            P("row", "col", None, None),
            P("row", "col"),
        ),
        out_specs=P("row", None, None, None, None, "col", None),
        check_vma=False,
    )
```

```python
import functools

import jax
import jax.numpy as jnp
from jax import lax
from jax.experimental import pallas as pl
from jax.experimental.pallas import tpu as pltpu
from jax.sharding import PartitionSpec as P

BS = 128
KA = 12
SIDE = 4
QUAD = 4 * BS
HEAD = 8
ROWS = 2 * QUAD + HEAD
BITS = 16
OWN_SLOTS = 6
SLOTS = 14
ANY = pl.BlockSpec(memory_space=pl.ANY)
VMEM = pl.BlockSpec(memory_space=pltpu.VMEM)
HBM = pl.BlockSpec(memory_space=pltpu.HBM)
BF16 = jnp.bfloat16
F32 = jnp.float32


def flips():
    return lax.rem(lax.axis_index("row"), 2), lax.rem(lax.axis_index("col"), 2)


def turned(index, flip):
    return index + flip - 2 * index * flip


def rims_kernel(agg_hbm, prolong, row_a, row_b, col_a, col_b, bits, agg, sems):
    fx, fy = flips()
    load = pltpu.make_async_copy(agg_hbm, agg, sems.at[16])
    load.start()
    copies = []
    plans = (
        (row_a, ((1, 0), (1, 1))),
        (row_b, ((0, 0), (0, 1))),
        (col_a, ((0, 1), (1, 1))),
        (col_b, ((0, 0), (1, 0))),
    )
    for out, quads in plans:
        for h, (u, v) in enumerate(quads):
            ur, vr = turned(u, fx), turned(v, fy)
            for m in range(2):
                copies.append(
                    pltpu.make_async_copy(
                        prolong.at[2 * ur + m, pl.ds(pl.multiple_of(vr * 256, 256), 256), :],
                        out.at[QUAD * h + 256 * m : QUAD * h + 256 * (m + 1), :],
                        sems.at[len(copies)],
                    )
                )
                copies[-1].start()
    load.wait()
    own = {}
    for k, (u, v) in enumerate(((0, 0), (0, 1), (1, 0), (1, 1))):
        own[u, v] = lax.rem(agg[2 * turned(u, fx), 2 * turned(v, fy)], 2).astype(F32)
        bits[k : k + 1, :] = jnp.full((1, BS), own[u, v], F32)
    bits[4:, :] = jnp.zeros((4, BS), F32)
    for out, quads in plans:
        at = lax.broadcasted_iota(jnp.int32, (HEAD, BS), 0)
        out[2 * QUAD :, :] = jnp.where(at == 0, own[quads[0]], own[quads[1]]).astype(BF16)
    for copy in copies:
        copy.wait()


def rims(agg, prolong_rows):
    shape = jax.ShapeDtypeStruct((ROWS, BS), BF16)
    return pl.pallas_call(
        rims_kernel,
        out_shape=(shape,) * 4 + (jax.ShapeDtypeStruct((8, BS), F32),),
        in_specs=[HBM, HBM],
        out_specs=(VMEM,) * 5,
        scratch_shapes=[pltpu.SMEM((SIDE, SIDE), jnp.int32), pltpu.SemaphoreType.DMA((17,))],
        compiler_params=pltpu.CompilerParams(vmem_limit_bytes=4 << 20),
        name="rims",
    )(agg, prolong_rows)


def sums(r, p, quads):
    fx, fy = flips()
    raw = 2 * turned(p[0] - 1, fx) + turned(p[1] - 1, fy)
    blocks = [r[raw, (u - p[0] + 1) * 3 + v - p[1] + 1] for u, v in quads]
    return blocks[0] if len(blocks) == 1 else jnp.concatenate(blocks, axis=1)


OWN = ((1, 1), (1, 2), (2, 1), (2, 2))
NONE = 16 * KA


def step_one_kernel(
    codes_hbm, coupling, prolong_hbm, after, out, to_a, to_b, prolong, blocks, codes, slot_of, sems
):
    fx, fy = flips()
    load_codes = pltpu.make_async_copy(codes_hbm, codes, sems.at[8])
    load_codes.start()
    load_prolong = pltpu.make_async_copy(prolong_hbm, prolong, sems.at[9])
    load_prolong.start()

    def load(quad, m):
        first = (2 * (quad // 2) + m) * SIDE + 2 * (quad % 2)
        at = pl.ds(first * KA, 2 * KA)
        return pltpu.make_async_copy(coupling.at[at], blocks.at[at], sems.at[2 * quad + m])

    def start(quad):
        for m in range(2):
            load(quad, m).start()

    start(0)
    blocks[NONE] = jnp.zeros((BS, BS), BF16)

    @pl.loop(0, 16)
    def _(n):
        for t in range(25):
            slot_of[n * 25 + t] = NONE

    start(1)
    load_codes.wait()

    @pl.loop(0, 16)
    def _(n):
        for k in range(KA):
            slot_of[n * 25 + codes[n // SIDE, n % SIDE, k]] = n * KA + k

    start(2)
    load_prolong.wait()
    zero = jnp.zeros((BS, BS), BF16)

    @pl.loop(0, 4)
    def _(quad):
        qx, qy = quad // 2, quad % 2
        for m in range(2):
            load(quad, m).wait()

        @pl.when(quad == 0)
        def _():
            start(3)

        left = []
        for ix in range(2):
            rows = prolong[2 * qx + ix, pl.ds(pl.multiple_of(qy * 256, 256), 256), :]
            left.append(rows.T)

        def block(ix, iy, jx, jy):
            if not (0 <= jy - iy <= 4):
                return zero
            n = (2 * qx + ix) * SIDE + 2 * qy + iy
            return blocks[slot_of[n * 25 + (jx - ix) * 5 + jy - iy]]

        for jx in range(6):
            for t in range(3):
                total = None
                for ix in range(2):
                    if not (0 <= jx - ix <= 4):
                        continue
                    right = jnp.concatenate(
                        [
                            jnp.concatenate([block(ix, iy, jx, 2 * t + e) for e in range(2)], axis=1)
                            for iy in range(2)
                        ],
                        axis=0,
                    )
                    part = jnp.dot(left[ix], right, preferred_element_type=F32)
                    total = part if total is None else total + part
                du, dv = jx // 2, t
                at = (du + fx * (2 - 2 * du)) * 3 + dv + fy * (2 - 2 * dv)
                out[quad, at, :, (jx % 2) * 256 : (jx % 2 + 1) * 256] = total.astype(BF16)

    for ref, e, p, q in (
        (to_b, 0, (2, 1), (3, 0)),
        (to_b, 1, (1, 1), (0, 0)),
        (to_a, 0, (2, 2), (3, 3)),
        (to_a, 1, (1, 2), (0, 3)),
    ):
        ref[e] = sums(out, p, (q,))


def step_one(codes, coupling, prolong_rows, after):
    corner = jax.ShapeDtypeStruct((2, BS, QUAD), BF16)
    return pl.pallas_call(
        step_one_kernel,
        out_shape=(
            jax.ShapeDtypeStruct((4, 9, BS, QUAD), BF16),
            corner,
            corner,
            jax.ShapeDtypeStruct(prolong_rows.shape, BF16),
        ),
        in_specs=[HBM] * 3 + [ANY],
        out_specs=(VMEM,) * 4,
        scratch_shapes=[
            pltpu.VMEM((NONE + 1, BS, BS), BF16),
            pltpu.SMEM((SIDE, SIDE, KA), jnp.int32),
            pltpu.SMEM((400,), jnp.int32),
            pltpu.SemaphoreType.DMA((10,)),
        ],
        compiler_params=pltpu.CompilerParams(vmem_limit_bytes=16 << 20),
        cost_estimate=pl.CostEstimate(flops=1 << 33, bytes_accessed=1 << 20, transcendentals=0),
        name="step_one",
    )(codes, coupling, prolong_rows, after)


def half_of(ref, h):
    return ref[2 * QUAD + h : 2 * QUAD + h + 1, :].astype(F32)


def quad_of(ref, h):
    return ref[QUAD * h : QUAD * (h + 1), :]


def edge_slots(near, far, same_a):
    same_b = 1.0 - jnp.abs(half_of(far, 0) - half_of(far, 1))
    second = quad_of(far, 1)
    shared = second * same_b.astype(BF16)
    right = jnp.concatenate(
        [
            jnp.concatenate([quad_of(far, 0), jnp.zeros_like(second)], axis=1),
            jnp.concatenate([shared, second - shared], axis=1),
        ],
        axis=0,
    )
    by_p = [jnp.dot(rows, right, preferred_element_type=F32) for rows in near]
    base, extra = [], []
    for v in range(2):
        one, two = (value[:, v * BS : (v + 1) * BS] for value in by_p)
        shared = same_a * two
        base.append(one + shared)
        extra.append(two - shared)
    return base, extra


def inside(axis, count):
    at = lax.axis_index(axis)
    return jnp.where(at == 0, 0.0, jnp.where(at == count - 1, 0.0, 1.0)).astype(F32)


def store_pieces(outs, at, values):
    rows = BS // len(outs)
    me = lax.axis_index("col")
    for s, out in enumerate(outs):
        start = pl.multiple_of((me ^ s) * rows, rows)
        for t in range(values.shape[0]):
            first = (at + t) * rows
            out[first : first + rows, :] = values[t, pl.ds(start, rows), :].astype(BF16)


def near_kernel(parts, bits, r, prolong, col_a, *rest):
    outs, (extra_a, slots, right) = rest[:-3], rest[-3:]
    fx, fy = flips()

    def by_halves(quads, own, first):
        for j, (_, parts_of, bit) in enumerate(quads):
            for m, rows in enumerate(parts_of):
                step = rows.shape[0]
                at = QUAD * j + step * m
                high = rows * bit.astype(BF16)
                right[at : at + step, 0:BS] = rows - high
                right[at : at + step, BS:] = high
        names = [q for q, _, _ in quads]
        for i, k in enumerate(own):
            value = jnp.dot(sums(r, OWN[k], names), right[0 : QUAD * len(quads), :], preferred_element_type=F32)
            for b in range(2):
                one = value[:, b * BS : (b + 1) * BS]
                high = bits[k : k + 1, :] * one
                low = one - high
                if i == 0:
                    slots[first + b] = low
                    slots[first + 2 + b] = high
                else:
                    slots[first + b] += low
                    slots[first + 2 + b] += high

    quads = []
    for j, (u, v) in enumerate(OWN):
        ur, vr = turned(u - 1, fx), turned(v - 1, fy)
        at = pl.ds(pl.multiple_of(vr * 256, 256), 256)
        quads.append(((u, v), [prolong[2 * ur + m, at, :] for m in range(2)], bits[j : j + 1, :]))
    by_halves(quads, range(4), 0)
    near = [sums(r, p, ((1, 3), (2, 3))) for p in ((1, 2), (2, 2))]
    base, extra = edge_slots(near, col_a, jnp.abs(bits[0:1, :] - bits[1:2, :]))
    for t in range(2):
        slots[4 + t] = base[t]
        extra_a[t] = extra[t]
    rows = BS // parts
    me = lax.axis_index("col")
    for s in range(parts):
        start = pl.multiple_of((me ^ s) * rows, rows)
        out = outs[s] if s < 2 else outs[s // 2 + 1]
        for t in range(OWN_SLOTS):
            value = slots[t, pl.ds(start, rows), :].astype(BF16)
            if s < 2:
                out[t] = value
            else:
                out[s % 2, t] = value


def near_terms(parts, *operands):
    rows = BS // parts
    one = jax.ShapeDtypeStruct((OWN_SLOTS, rows, BS), BF16)
    two = jax.ShapeDtypeStruct((2, OWN_SLOTS, rows, BS), BF16)
    shapes = (one, one) + (two,) * (parts // 2 - 1) + (jax.ShapeDtypeStruct((2, BS, BS), F32),)
    return pl.pallas_call(
        functools.partial(near_kernel, parts),
        out_shape=shapes,
        in_specs=[VMEM] * len(operands),
        out_specs=(VMEM,) * len(shapes),
        scratch_shapes=[pltpu.VMEM((OWN_SLOTS, BS, BS), F32), pltpu.VMEM((4 * QUAD, 2 * BS), BF16)],
        compiler_params=pltpu.CompilerParams(vmem_limit_bytes=16 << 20),
        cost_estimate=pl.CostEstimate(flops=1, bytes_accessed=1, transcendentals=0),
        name="near_terms",
    )(*operands)


def fill_edges(r, edges, slots, head):
    for e, (far, own, quads, same_a, scale) in enumerate(edges):
        base, extra = edge_slots([sums(r, p, quads) for p in own], far, same_a)
        for t in range(2):
            slots[2 * e + t] = base[t] if scale is None else base[t] * scale
            slots[4 + 2 * e + t] = extra[t] if scale is None else extra[t] * scale
            head[2 * e + t : 2 * e + t + 1, :] = half_of(far, t)


def mid_kernel(parts, bits, r, col_a, col_b, columns, head):
    near = [sums(r, p, ((1, 0), (2, 0))) for p in ((1, 1), (2, 1))]
    base, extra = edge_slots(near, col_b, jnp.abs(bits[0:1, :] - bits[1:2, :]))
    scale = inside("col", parts)
    for t in range(2):
        columns[t] = base[t] * scale
        columns[2 + t] = extra[t] * scale
        head[t : t + 1, :] = half_of(col_a, t)
        head[2 + t : 3 + t, :] = half_of(col_b, t)
    head[4:8, :] = bits[0:4, :]


def mid_terms(parts, *operands):
    return pl.pallas_call(
        functools.partial(mid_kernel, parts),
        out_shape=(jax.ShapeDtypeStruct((4, BS, BS), F32), jax.ShapeDtypeStruct((8, BS), F32)),
        in_specs=[VMEM] * len(operands),
        out_specs=(VMEM, VMEM),
        compiler_params=pltpu.CompilerParams(vmem_limit_bytes=8 << 20),
        cost_estimate=pl.CostEstimate(flops=1, bytes_accessed=1, transcendentals=0),
        name="mid_terms",
    )(*operands)


def far_kernel(counts, bits, r, row_a, row_b, from_a, from_b, columns, column_head, extra_a, *rest):
    outs, (slots, head) = rest[:-2], rest[-2:]
    split_x = 1.0 - jnp.abs(bits[0:1, :] - bits[1:2, :])
    row_in, col_in = inside("row", counts[0]), inside("col", counts[1])
    head[...] = jnp.zeros_like(head)
    head[0:4, :] = bits[0:4, :]
    head[8:12, :] = column_head[0:4, :]
    edges = (
        (row_a, ((2, 1), (2, 2)), ((3, 1), (3, 2)), split_x, None),
        (row_b, ((1, 1), (1, 2)), ((0, 1), (0, 2)), split_x, row_in),
    )
    fill_edges(r, edges, slots, head.at[4:8])
    for t in range(2):
        slots[4 + t] += extra_a[t]
        slots[6 + t] += columns[2 + t]
    corners = (
        (from_a.at[0], quad_of(row_a, 1), None),
        (from_b.at[0], quad_of(row_a, 0), col_in),
        (from_a.at[1], quad_of(row_b, 1), row_in),
        (from_b.at[1], quad_of(row_b, 0), row_in * col_in),
    )
    for e, (near, far, scale) in enumerate(corners):
        value = jnp.dot(near[...], far, preferred_element_type=F32)
        slots[8 + e] = value if scale is None else value * scale
    store_pieces(outs, 0, slots.at[0:4])
    store_pieces(outs, 4, columns.at[0:2])
    store_pieces(outs, 6, slots.at[8:12])
    store_pieces(outs, 10, slots.at[4:8])
    for out in outs:
        out[out.shape[0] - BITS :, :] = head[...].astype(BF16)


def far_terms(counts, *operands):
    parts = counts[1]
    message = jax.ShapeDtypeStruct((SLOTS * (BS // parts) + BITS, BS), BF16)
    return pl.pallas_call(
        functools.partial(far_kernel, counts),
        out_shape=(message,) * parts,
        in_specs=[VMEM] * len(operands),
        out_specs=(VMEM,) * parts,
        scratch_shapes=[pltpu.VMEM((12, BS, BS), F32), pltpu.VMEM((BITS, BS), F32)],
        compiler_params=pltpu.CompilerParams(vmem_limit_bytes=16 << 20),
        cost_estimate=pl.CostEstimate(flops=1, bytes_accessed=1, transcendentals=0),
        name="far_terms",
    )(*operands)


def unpack_kernel(parts, steps, *refs):
    ins, owns = refs[: len(steps)], refs[len(steps) : 2 * len(steps)]
    out, buf, sems = refs[-3:]
    me = lax.axis_index("col")
    fx, _ = flips()
    copies = []
    for i, (s, ref) in enumerate(zip(steps, ins)):
        square = me ^ s
        fy = lax.rem(square, 2)
        own = owns[i] if s == 0 else owns[i].at[s // 2 if s % 2 else 0]
        for a in range(2):
            copies.append(
                pltpu.make_async_copy(own.at[2 * a : 2 * a + 2], out.at[square, a, 4], sems.at[len(copies)])
            )
            copies[-1].start()
        one = functools.partial(bit_row, ref)
        split_y = jnp.abs(one(0) - one(1))

        def send(piece, owner, code):
            copies.append(pltpu.make_async_copy(buf.at[i, piece], out.at[owner, :, code], sems.at[len(copies)]))
            copies[-1].start()

        split_x = 1.0 - split_y
        edges = (
            ((2, 3), (0, 1), (10, 11), split_y, 7 - 6 * fx),
            ((0, 1), (2, 3), (12, 13), split_y, 1 + 6 * fx),
            ((1, 3), None, (10, 11), split_x, 3 + turn3(2, fy)),
            ((0, 2), (4, 5), (12, 13), split_x, 3 + turn3(0, fy)),
        )
        for e, (ps, base, more, used, code) in enumerate(edges):
            values = [slot(ref, t) for t in base] if base else [own[4 + t].astype(F32) for t in range(2)]
            second = [slot(ref, t) for t in more]
            spread_edge(buf, (i, e), one, ps, (4 + 2 * e, 5 + 2 * e), values, second, used)
            send(e, square, code)
        high = square ^ 1
        low = square + 2 * fy - 1
        low = jnp.where((low < 0) | (low >= parts), square, low)
        corners = (
            (high, 6 - 6 * fx, 2, 9, 5),
            (low, 6 - 6 * fx, 0, 11, 4),
            (high, 6 * fx, 2, 8, 7),
            (low, 6 * fx, 0, 10, 6),
        )
        for e, (owner, group, side, a_bit, b_bit) in enumerate(corners):
            spread_corner(buf, (i, 4 + e), slot(ref, 6 + e), one(a_bit), one(b_bit))
            send(4 + e, owner, group + turn3(side, lax.rem(owner, 2)))
    for copy in copies:
        copy.wait()


def unpack(messages, owns, steps, coarse):
    parts = lax.axis_size("col")
    rows = BS // parts
    fresh = coarse is None
    return pl.pallas_call(
        functools.partial(unpack_kernel, parts, steps),
        out_shape=jax.ShapeDtypeStruct((parts, 2, 9, 2, rows, BS), BF16),
        in_specs=[VMEM] * (2 * len(steps)) + [ANY] * (not fresh),
        out_specs=ANY,
        scratch_shapes=[
            pltpu.VMEM((len(steps), 8, 2, 2, rows, BS), BF16),
            pltpu.SemaphoreType.DMA((10 * len(steps),)),
        ],
        input_output_aliases={} if fresh else {2 * len(steps): 0},
        compiler_params=pltpu.CompilerParams(vmem_limit_bytes=16 << 20),
        cost_estimate=pl.CostEstimate(flops=1, bytes_accessed=1, transcendentals=0),
        name="unpack",
    )(*messages, *owns, *(() if fresh else (coarse,)))


def turn3(index, flip):
    return index + flip * (2 - 2 * index)


def bit_row(ref, k):
    at = ref.shape[0] - BITS + k
    return ref[at : at + 1, :].astype(F32)


def slot(ref, t):
    rows = (ref.shape[0] - BITS) // SLOTS
    return ref[t * rows : (t + 1) * rows, :].astype(F32)


def spread(buf, at, center):
    i, piece = at
    for a in range(2):
        for b in range(2):
            buf[i, piece, a, b] = center[2 * a + b].astype(BF16)


def spread_edge(buf, at, one, ps, qs, values, more, used):
    a_bits = [one(p) for p in ps]
    b_bits = [one(q) for q in qs]
    center = [None] * 4
    for b in range(2):
        picks = [bit if b else 1.0 - bit for bit in b_bits]
        first = picks[0] * values[0] + picks[1] * values[1]
        second = (used * picks[0]) * more[0] + (used * picks[1]) * more[1]
        for a in range(2):
            ia = [bit if a else 1.0 - bit for bit in a_bits]
            center[2 * a + b] = ia[0] * first + ia[1] * second
    spread(buf, at, center)


def spread_corner(buf, at, value, a_bit, b_bit):
    center = []
    for a in range(2):
        for b in range(2):
            center.append(((a_bit if a else 1.0 - a_bit) * (b_bit if b else 1.0 - b_bit)) * value)
    spread(buf, at, center)


def gate_kernel(*refs):
    pass


def gate(values, after):
    count = len(values)
    return pl.pallas_call(
        gate_kernel,
        out_shape=tuple(jax.ShapeDtypeStruct(v.shape, v.dtype) for v in values),
        in_specs=[ANY] * (count + len(after)),
        out_specs=(ANY,) * count,
        input_output_aliases={i: i for i in range(count)},
        compiler_params=pltpu.CompilerParams(vmem_limit_bytes=1 << 20),
        cost_estimate=pl.CostEstimate(flops=1 << 33, bytes_accessed=1, transcendentals=0),
        name="gate",
    )(*values, *after)


def other_side(index):
    return index + 1 if index % 2 else index - 1


def row_low(r, c, rows, cols):
    far = other_side(r)
    return (far, c) if 0 <= far < rows else (r, c ^ 1)


def col_low(r, c, rows, cols):
    far = other_side(c)
    return (r, far) if 0 <= far < cols else (r ^ 2, c)


def row_high(r, c, rows, cols):
    return r ^ 1, c


def col_high(r, c, rows, cols):
    return r, c ^ 1


def swap(value, partner):
    rows, cols = lax.axis_size("row"), lax.axis_size("col")
    pairs = []
    for r in range(rows):
        for c in range(cols):
            to_r, to_c = partner(r, c, rows, cols)
            pairs.append((r * cols + c, to_r * cols + to_c))
    return lax.ppermute(value, ("row", "col"), pairs)


def xor_swap(value, s):
    return lax.ppermute(value, "col", [(i, i ^ s) for i in range(lax.axis_size("col"))])


def local(coupling, neighbours, prolong, aggregate):
    parts = lax.axis_size("col")
    counts = (lax.axis_size("row"), parts)
    coupling = pltpu.with_memory_space_constraint(coupling.reshape(-1, BS, BS), pltpu.HBM)
    neighbours = pltpu.with_memory_space_constraint(neighbours, pltpu.HBM)
    aggregate = pltpu.with_memory_space_constraint(aggregate, pltpu.HBM)
    prolong_rows = pltpu.with_memory_space_constraint(prolong.reshape(SIDE, SIDE * BS, BS), pltpu.HBM)
    to_row_a, to_row_b, to_col_a, to_col_b, bits = rims(aggregate, prolong_rows)
    row_a = swap(to_row_a, row_high)
    row_b = swap(to_row_b, row_low)
    col_a = swap(to_col_a, col_high)
    col_b = swap(to_col_b, col_low)
    r, to_a, to_b, own_blocks = step_one(neighbours, coupling, prolong_rows, bits)
    from_b = swap(to_b, col_low)
    from_a = swap(to_a, col_high)
    mine, pair, *cross, extra_a = near_terms(parts, bits, r, own_blocks, col_a)
    from_a, *cross = lax.optimization_barrier((from_a, *cross))
    direct = [xor_swap(value, 2 * h + 2) for h, value in enumerate(cross)]
    columns, column_head = mid_terms(parts, bits, r, col_a, col_b)
    row_a, row_b, columns, from_b = gate((row_a, row_b, columns, from_b), (mine,))
    outs = list(far_terms(counts, bits, r, row_a, row_b, from_a, from_b, columns, column_head, extra_a))
    outs[0], *direct = lax.optimization_barrier((outs[0], *direct))
    outs = [outs[0]] + [xor_swap(outs[s], s) for s in range(1, parts)]
    relayed = xor_swap(jnp.stack([pair] + [value[1] for value in direct]), 1)
    owns = [mine, relayed]
    for value in direct:
        owns += [value, relayed]
    coarse = unpack(outs[:2], owns[:2], range(2), None)
    coarse = unpack(outs[2:], owns[2:], range(2, parts), coarse)
    return coarse[None]


def solution(mesh):
    return jax.shard_map(
        local,
        mesh=mesh,
        in_specs=(
            P("row", "col", None, None, None),
            P("row", "col", None),
            P("row", "col", None, None),
            P("row", "col"),
        ),
        out_specs=P("row", None, None, None, None, "col", None),
        check_vma=False,
    )
```

```python
import functools

import jax
import jax.numpy as jnp
from jax import lax
from jax.experimental import pallas as pl
from jax.experimental.pallas import tpu as pltpu
from jax.sharding import PartitionSpec as P

BS = 128
KA = 12
SIDE = 4
QUAD = 4 * BS
HEAD = 8
ROWS = 2 * QUAD + HEAD
BITS = 16
OWN_SLOTS = 6
SLOTS = 14
ANY = pl.BlockSpec(memory_space=pl.ANY)
VMEM = pl.BlockSpec(memory_space=pltpu.VMEM)
HBM = pl.BlockSpec(memory_space=pltpu.HBM)
BF16 = jnp.bfloat16
F32 = jnp.float32


def flips():
    return lax.rem(lax.axis_index("row"), 2), lax.rem(lax.axis_index("col"), 2)


def turned(index, flip):
    return index + flip - 2 * index * flip


def rims_kernel(agg_hbm, prolong, row_a, row_b, col_a, col_b, bits, agg, sems):
    fx, fy = flips()
    load = pltpu.make_async_copy(agg_hbm, agg, sems.at[16])
    load.start()
    copies = []
    plans = (
        (row_a, ((1, 0), (1, 1))),
        (row_b, ((0, 0), (0, 1))),
        (col_a, ((0, 1), (1, 1))),
        (col_b, ((0, 0), (1, 0))),
    )
    for out, quads in plans:
        for h, (u, v) in enumerate(quads):
            ur, vr = turned(u, fx), turned(v, fy)
            for m in range(2):
                copies.append(
                    pltpu.make_async_copy(
                        prolong.at[2 * ur + m, pl.ds(pl.multiple_of(vr * 256, 256), 256), :],
                        out.at[QUAD * h + 256 * m : QUAD * h + 256 * (m + 1), :],
                        sems.at[len(copies)],
                    )
                )
                copies[-1].start()
    load.wait()
    own = {}
    for k, (u, v) in enumerate(((0, 0), (0, 1), (1, 0), (1, 1))):
        own[u, v] = lax.rem(agg[2 * turned(u, fx), 2 * turned(v, fy)], 2).astype(F32)
        bits[k : k + 1, :] = jnp.full((1, BS), own[u, v], F32)
    bits[4:, :] = jnp.zeros((4, BS), F32)
    for out, quads in plans:
        at = lax.broadcasted_iota(jnp.int32, (HEAD, BS), 0)
        out[2 * QUAD :, :] = jnp.where(at == 0, own[quads[0]], own[quads[1]]).astype(BF16)
    for copy in copies:
        copy.wait()


def rims(agg, prolong_rows):
    shape = jax.ShapeDtypeStruct((ROWS, BS), BF16)
    return pl.pallas_call(
        rims_kernel,
        out_shape=(shape,) * 4 + (jax.ShapeDtypeStruct((8, BS), F32),),
        in_specs=[HBM, HBM],
        out_specs=(VMEM,) * 5,
        scratch_shapes=[pltpu.SMEM((SIDE, SIDE), jnp.int32), pltpu.SemaphoreType.DMA((17,))],
        compiler_params=pltpu.CompilerParams(vmem_limit_bytes=4 << 20),
        name="rims",
    )(agg, prolong_rows)


def sums(r, p, quads):
    fx, fy = flips()
    raw = 2 * turned(p[0] - 1, fx) + turned(p[1] - 1, fy)
    blocks = [r[raw, (u - p[0] + 1) * 3 + v - p[1] + 1] for u, v in quads]
    return blocks[0] if len(blocks) == 1 else jnp.concatenate(blocks, axis=1)


OWN = ((1, 1), (1, 2), (2, 1), (2, 2))
NONE = 16 * KA


def step_one_kernel(
    codes_hbm, coupling, prolong_hbm, after, out, to_a, to_b, prolong, blocks, codes, slot_of, sems
):
    fx, fy = flips()
    load_codes = pltpu.make_async_copy(codes_hbm, codes, sems.at[8])
    load_codes.start()
    load_prolong = pltpu.make_async_copy(prolong_hbm, prolong, sems.at[9])
    load_prolong.start()

    def load(quad, m):
        first = (2 * (quad // 2) + m) * SIDE + 2 * (quad % 2)
        at = pl.ds(first * KA, 2 * KA)
        return pltpu.make_async_copy(coupling.at[at], blocks.at[at], sems.at[2 * quad + m])

    def start(quad):
        for m in range(2):
            load(quad, m).start()

    start(0)
    blocks[NONE] = jnp.zeros((BS, BS), BF16)

    @pl.loop(0, 16)
    def _(n):
        for t in range(25):
            slot_of[n * 25 + t] = NONE

    start(1)
    load_codes.wait()

    @pl.loop(0, 16)
    def _(n):
        for k in range(KA):
            slot_of[n * 25 + codes[n // SIDE, n % SIDE, k]] = n * KA + k

    start(2)
    load_prolong.wait()
    zero = jnp.zeros((BS, BS), BF16)

    @pl.loop(0, 4)
    def _(quad):
        qx, qy = quad // 2, quad % 2
        for m in range(2):
            load(quad, m).wait()

        @pl.when(quad == 0)
        def _():
            start(3)

        left = []
        for ix in range(2):
            rows = prolong[2 * qx + ix, pl.ds(pl.multiple_of(qy * 256, 256), 256), :]
            left.append(rows.T)

        def block(ix, iy, jx, jy):
            if not (0 <= jy - iy <= 4):
                return zero
            n = (2 * qx + ix) * SIDE + 2 * qy + iy
            return blocks[slot_of[n * 25 + (jx - ix) * 5 + jy - iy]]

        for jx in range(6):
            for t in range(3):
                total = None
                for ix in range(2):
                    if not (0 <= jx - ix <= 4):
                        continue
                    right = jnp.concatenate(
                        [
                            jnp.concatenate([block(ix, iy, jx, 2 * t + e) for e in range(2)], axis=1)
                            for iy in range(2)
                        ],
                        axis=0,
                    )
                    part = jnp.dot(left[ix], right, preferred_element_type=F32)
                    total = part if total is None else total + part
                du, dv = jx // 2, t
                at = (du + fx * (2 - 2 * du)) * 3 + dv + fy * (2 - 2 * dv)
                out[quad, at, :, (jx % 2) * 256 : (jx % 2 + 1) * 256] = total.astype(BF16)

    for ref, e, p, q in (
        (to_b, 0, (2, 1), (3, 0)),
        (to_b, 1, (1, 1), (0, 0)),
        (to_a, 0, (2, 2), (3, 3)),
        (to_a, 1, (1, 2), (0, 3)),
    ):
        ref[e] = sums(out, p, (q,))


def step_one(codes, coupling, prolong_rows, after):
    corner = jax.ShapeDtypeStruct((2, BS, QUAD), BF16)
    return pl.pallas_call(
        step_one_kernel,
        out_shape=(
            jax.ShapeDtypeStruct((4, 9, BS, QUAD), BF16),
            corner,
            corner,
            jax.ShapeDtypeStruct(prolong_rows.shape, BF16),
        ),
        in_specs=[HBM] * 3 + [ANY],
        out_specs=(VMEM,) * 4,
        scratch_shapes=[
            pltpu.VMEM((NONE + 1, BS, BS), BF16),
            pltpu.SMEM((SIDE, SIDE, KA), jnp.int32),
            pltpu.SMEM((400,), jnp.int32),
            pltpu.SemaphoreType.DMA((10,)),
        ],
        compiler_params=pltpu.CompilerParams(vmem_limit_bytes=16 << 20),
        cost_estimate=pl.CostEstimate(flops=1 << 33, bytes_accessed=1 << 20, transcendentals=0),
        name="step_one",
    )(codes, coupling, prolong_rows, after)


def half_of(ref, h):
    return ref[2 * QUAD + h : 2 * QUAD + h + 1, :].astype(F32)


def quad_of(ref, h):
    return ref[QUAD * h : QUAD * (h + 1), :]


def edge_slots(near, far, same_a):
    same_b = 1.0 - jnp.abs(half_of(far, 0) - half_of(far, 1))
    second = quad_of(far, 1)
    shared = second * same_b.astype(BF16)
    right = jnp.concatenate(
        [
            jnp.concatenate([quad_of(far, 0), jnp.zeros_like(second)], axis=1),
            jnp.concatenate([shared, second - shared], axis=1),
        ],
        axis=0,
    )
    by_p = [jnp.dot(rows, right, preferred_element_type=F32) for rows in near]
    base, extra = [], []
    for v in range(2):
        one, two = (value[:, v * BS : (v + 1) * BS] for value in by_p)
        shared = same_a * two
        base.append(one + shared)
        extra.append(two - shared)
    return base, extra


def inside(axis, count):
    at = lax.axis_index(axis)
    return jnp.where(at == 0, 0.0, jnp.where(at == count - 1, 0.0, 1.0)).astype(F32)


def store_pieces(outs, at, values):
    rows = BS // len(outs)
    me = lax.axis_index("col")
    for s, out in enumerate(outs):
        start = pl.multiple_of((me ^ s) * rows, rows)
        for t in range(values.shape[0]):
            first = (at + t) * rows
            out[first : first + rows, :] = values[t, pl.ds(start, rows), :].astype(BF16)


def near_kernel(parts, bits, r, prolong, col_a, *rest):
    outs, (extra_a, slots, right) = rest[:-3], rest[-3:]
    fx, fy = flips()

    def by_halves(quads, own, first):
        for j, (_, parts_of, bit) in enumerate(quads):
            for m, rows in enumerate(parts_of):
                step = rows.shape[0]
                at = QUAD * j + step * m
                high = rows * bit.astype(BF16)
                right[at : at + step, 0:BS] = rows - high
                right[at : at + step, BS:] = high
        names = [q for q, _, _ in quads]
        for i, k in enumerate(own):
            value = jnp.dot(sums(r, OWN[k], names), right[0 : QUAD * len(quads), :], preferred_element_type=F32)
            for b in range(2):
                one = value[:, b * BS : (b + 1) * BS]
                high = bits[k : k + 1, :] * one
                low = one - high
                if i == 0:
                    slots[first + b] = low
                    slots[first + 2 + b] = high
                else:
                    slots[first + b] += low
                    slots[first + 2 + b] += high

    quads = []
    for j, (u, v) in enumerate(OWN):
        ur, vr = turned(u - 1, fx), turned(v - 1, fy)
        at = pl.ds(pl.multiple_of(vr * 256, 256), 256)
        quads.append(((u, v), [prolong[2 * ur + m, at, :] for m in range(2)], bits[j : j + 1, :]))
    by_halves(quads, range(4), 0)
    near = [sums(r, p, ((1, 3), (2, 3))) for p in ((1, 2), (2, 2))]
    base, extra = edge_slots(near, col_a, jnp.abs(bits[0:1, :] - bits[1:2, :]))
    for t in range(2):
        slots[4 + t] = base[t]
        extra_a[t] = extra[t]
    rows = BS // parts
    me = lax.axis_index("col")
    for s in range(parts):
        start = pl.multiple_of((me ^ s) * rows, rows)
        out = outs[s] if s < 2 else outs[s // 2 + 1]
        for t in range(OWN_SLOTS):
            value = slots[t, pl.ds(start, rows), :].astype(BF16)
            if s < 2:
                out[t] = value
            else:
                out[s % 2, t] = value


def near_terms(parts, *operands):
    rows = BS // parts
    one = jax.ShapeDtypeStruct((OWN_SLOTS, rows, BS), BF16)
    two = jax.ShapeDtypeStruct((2, OWN_SLOTS, rows, BS), BF16)
    shapes = (one, one) + (two,) * (parts // 2 - 1) + (jax.ShapeDtypeStruct((2, BS, BS), F32),)
    return pl.pallas_call(
        functools.partial(near_kernel, parts),
        out_shape=shapes,
        in_specs=[VMEM] * len(operands),
        out_specs=(VMEM,) * len(shapes),
        scratch_shapes=[pltpu.VMEM((OWN_SLOTS, BS, BS), F32), pltpu.VMEM((4 * QUAD, 2 * BS), BF16)],
        compiler_params=pltpu.CompilerParams(vmem_limit_bytes=16 << 20),
        cost_estimate=pl.CostEstimate(flops=1, bytes_accessed=1, transcendentals=0),
        name="near_terms",
    )(*operands)


def fill_edges(r, edges, slots, head):
    for e, (far, own, quads, same_a, scale) in enumerate(edges):
        base, extra = edge_slots([sums(r, p, quads) for p in own], far, same_a)
        for t in range(2):
            slots[2 * e + t] = base[t] if scale is None else base[t] * scale
            slots[4 + 2 * e + t] = extra[t] if scale is None else extra[t] * scale
            head[2 * e + t : 2 * e + t + 1, :] = half_of(far, t)


def mid_kernel(parts, bits, r, col_a, col_b, columns, head):
    near = [sums(r, p, ((1, 0), (2, 0))) for p in ((1, 1), (2, 1))]
    base, extra = edge_slots(near, col_b, jnp.abs(bits[0:1, :] - bits[1:2, :]))
    scale = inside("col", parts)
    for t in range(2):
        columns[t] = base[t] * scale
        columns[2 + t] = extra[t] * scale
        head[t : t + 1, :] = half_of(col_a, t)
        head[2 + t : 3 + t, :] = half_of(col_b, t)
    head[4:8, :] = bits[0:4, :]


def mid_terms(parts, *operands):
    return pl.pallas_call(
        functools.partial(mid_kernel, parts),
        out_shape=(jax.ShapeDtypeStruct((4, BS, BS), F32), jax.ShapeDtypeStruct((8, BS), F32)),
        in_specs=[VMEM] * len(operands),
        out_specs=(VMEM, VMEM),
        compiler_params=pltpu.CompilerParams(vmem_limit_bytes=8 << 20),
        cost_estimate=pl.CostEstimate(flops=1, bytes_accessed=1, transcendentals=0),
        name="mid_terms",
    )(*operands)


def far_kernel(counts, bits, r, row_a, row_b, from_a, from_b, columns, column_head, extra_a, *rest):
    outs, (slots, head) = rest[:-2], rest[-2:]
    split_x = 1.0 - jnp.abs(bits[0:1, :] - bits[1:2, :])
    row_in, col_in = inside("row", counts[0]), inside("col", counts[1])
    head[...] = jnp.zeros_like(head)
    head[0:4, :] = bits[0:4, :]
    head[8:12, :] = column_head[0:4, :]
    edges = (
        (row_a, ((2, 1), (2, 2)), ((3, 1), (3, 2)), split_x, None),
        (row_b, ((1, 1), (1, 2)), ((0, 1), (0, 2)), split_x, row_in),
    )
    fill_edges(r, edges, slots, head.at[4:8])
    for t in range(2):
        slots[4 + t] += extra_a[t]
        slots[6 + t] += columns[2 + t]
    corners = (
        (from_a.at[0], quad_of(row_a, 1), None),
        (from_b.at[0], quad_of(row_a, 0), col_in),
        (from_a.at[1], quad_of(row_b, 1), row_in),
        (from_b.at[1], quad_of(row_b, 0), row_in * col_in),
    )
    for e, (near, far, scale) in enumerate(corners):
        value = jnp.dot(near[...], far, preferred_element_type=F32)
        slots[8 + e] = value if scale is None else value * scale
    store_pieces(outs, 0, slots.at[0:4])
    store_pieces(outs, 4, columns.at[0:2])
    store_pieces(outs, 6, slots.at[8:12])
    store_pieces(outs, 10, slots.at[4:8])
    for out in outs:
        out[out.shape[0] - BITS :, :] = head[...].astype(BF16)


def far_terms(counts, *operands):
    parts = counts[1]
    message = jax.ShapeDtypeStruct((SLOTS * (BS // parts) + BITS, BS), BF16)
    return pl.pallas_call(
        functools.partial(far_kernel, counts),
        out_shape=(message,) * parts,
        in_specs=[VMEM] * len(operands),
        out_specs=(VMEM,) * parts,
        scratch_shapes=[pltpu.VMEM((12, BS, BS), F32), pltpu.VMEM((BITS, BS), F32)],
        compiler_params=pltpu.CompilerParams(vmem_limit_bytes=16 << 20),
        cost_estimate=pl.CostEstimate(flops=1, bytes_accessed=1, transcendentals=0),
        name="far_terms",
    )(*operands)


def unpack_kernel(parts, steps, *refs):
    ins, owns = refs[: len(steps)], refs[len(steps) : 2 * len(steps)]
    out, buf, sems = refs[-3:]
    me = lax.axis_index("col")
    fx, _ = flips()
    copies = []
    for i, (s, ref) in enumerate(zip(steps, ins)):
        square = me ^ s
        fy = lax.rem(square, 2)
        own = owns[i] if s == 0 else owns[i].at[s // 2 if s % 2 else 0]
        for a in range(2):
            copies.append(
                pltpu.make_async_copy(own.at[2 * a : 2 * a + 2], out.at[square, a, 4], sems.at[len(copies)])
            )
            copies[-1].start()
        one = functools.partial(bit_row, ref)
        split_y = jnp.abs(one(0) - one(1))

        def send(piece, owner, code):
            copies.append(pltpu.make_async_copy(buf.at[i, piece], out.at[owner, :, code], sems.at[len(copies)]))
            copies[-1].start()

        split_x = 1.0 - split_y
        edges = (
            ((2, 3), (0, 1), (10, 11), split_y, 7 - 6 * fx),
            ((0, 1), (2, 3), (12, 13), split_y, 1 + 6 * fx),
            ((1, 3), None, (10, 11), split_x, 3 + turn3(2, fy)),
            ((0, 2), (4, 5), (12, 13), split_x, 3 + turn3(0, fy)),
        )
        for e, (ps, base, more, used, code) in enumerate(edges):
            values = [slot(ref, t) for t in base] if base else [own[4 + t].astype(F32) for t in range(2)]
            second = [slot(ref, t) for t in more]
            spread_edge(buf, (i, e), one, ps, (4 + 2 * e, 5 + 2 * e), values, second, used)
            send(e, square, code)
        high = square ^ 1
        low = square + 2 * fy - 1
        low = jnp.where((low < 0) | (low >= parts), square, low)
        corners = (
            (high, 6 - 6 * fx, 2, 9, 5),
            (low, 6 - 6 * fx, 0, 11, 4),
            (high, 6 * fx, 2, 8, 7),
            (low, 6 * fx, 0, 10, 6),
        )
        for e, (owner, group, side, a_bit, b_bit) in enumerate(corners):
            spread_corner(buf, (i, 4 + e), slot(ref, 6 + e), one(a_bit), one(b_bit))
            send(4 + e, owner, group + turn3(side, lax.rem(owner, 2)))
    for copy in copies:
        copy.wait()


def unpack(messages, owns, steps, coarse):
    parts = lax.axis_size("col")
    rows = BS // parts
    fresh = coarse is None
    return pl.pallas_call(
        functools.partial(unpack_kernel, parts, steps),
        out_shape=jax.ShapeDtypeStruct((parts, 2, 9, 2, rows, BS), BF16),
        in_specs=[VMEM] * (2 * len(steps)) + [ANY] * (not fresh),
        out_specs=ANY,
        scratch_shapes=[
            pltpu.VMEM((len(steps), 8, 2, 2, rows, BS), BF16),
            pltpu.SemaphoreType.DMA((10 * len(steps),)),
        ],
        input_output_aliases={} if fresh else {2 * len(steps): 0},
        compiler_params=pltpu.CompilerParams(vmem_limit_bytes=16 << 20),
        cost_estimate=pl.CostEstimate(flops=1, bytes_accessed=1, transcendentals=0),
        name="unpack",
    )(*messages, *owns, *(() if fresh else (coarse,)))


def turn3(index, flip):
    return index + flip * (2 - 2 * index)


def bit_row(ref, k):
    at = ref.shape[0] - BITS + k
    return ref[at : at + 1, :].astype(F32)


def slot(ref, t):
    rows = (ref.shape[0] - BITS) // SLOTS
    return ref[t * rows : (t + 1) * rows, :].astype(F32)


def spread(buf, at, center):
    i, piece = at
    for a in range(2):
        for b in range(2):
            buf[i, piece, a, b] = center[2 * a + b].astype(BF16)


def spread_edge(buf, at, one, ps, qs, values, more, used):
    a_bits = [one(p) for p in ps]
    b_bits = [one(q) for q in qs]
    center = [None] * 4
    for b in range(2):
        picks = [bit if b else 1.0 - bit for bit in b_bits]
        first = picks[0] * values[0] + picks[1] * values[1]
        second = (used * picks[0]) * more[0] + (used * picks[1]) * more[1]
        for a in range(2):
            ia = [bit if a else 1.0 - bit for bit in a_bits]
            center[2 * a + b] = ia[0] * first + ia[1] * second
    spread(buf, at, center)


def spread_corner(buf, at, value, a_bit, b_bit):
    center = []
    for a in range(2):
        for b in range(2):
            center.append(((a_bit if a else 1.0 - a_bit) * (b_bit if b else 1.0 - b_bit)) * value)
    spread(buf, at, center)


def gate_kernel(*refs):
    pass


def gate(values, after):
    count = len(values)
    return pl.pallas_call(
        gate_kernel,
        out_shape=tuple(jax.ShapeDtypeStruct(v.shape, v.dtype) for v in values),
        in_specs=[ANY] * (count + len(after)),
        out_specs=(ANY,) * count,
        input_output_aliases={i: i for i in range(count)},
        compiler_params=pltpu.CompilerParams(vmem_limit_bytes=1 << 20),
        cost_estimate=pl.CostEstimate(flops=1 << 33, bytes_accessed=1, transcendentals=0),
        name="gate",
    )(*values, *after)


def other_side(index):
    return index + 1 if index % 2 else index - 1


def row_low(r, c, rows, cols):
    far = other_side(r)
    return (far, c) if 0 <= far < rows else (r, c ^ 1)


def col_low(r, c, rows, cols):
    far = other_side(c)
    if 0 <= far < cols:
        return r, far
    if r % 2:
        return (r - 2 if r >= 2 else r - 1), c
    return (r + 2 if r + 2 < rows else r + 1), c


def row_high(r, c, rows, cols):
    return r ^ 1, c


def col_high(r, c, rows, cols):
    return r, c ^ 1


def swap(value, partner):
    rows, cols = lax.axis_size("row"), lax.axis_size("col")
    pairs = []
    for r in range(rows):
        for c in range(cols):
            to_r, to_c = partner(r, c, rows, cols)
            pairs.append((r * cols + c, to_r * cols + to_c))
    return lax.ppermute(value, ("row", "col"), pairs)


def xor_swap(value, s):
    return lax.ppermute(value, "col", [(i, i ^ s) for i in range(lax.axis_size("col"))])


def local(coupling, neighbours, prolong, aggregate):
    parts = lax.axis_size("col")
    counts = (lax.axis_size("row"), parts)
    coupling = pltpu.with_memory_space_constraint(coupling.reshape(-1, BS, BS), pltpu.HBM)
    neighbours = pltpu.with_memory_space_constraint(neighbours, pltpu.HBM)
    aggregate = pltpu.with_memory_space_constraint(aggregate, pltpu.HBM)
    prolong_rows = pltpu.with_memory_space_constraint(prolong.reshape(SIDE, SIDE * BS, BS), pltpu.HBM)
    to_row_a, to_row_b, to_col_a, to_col_b, bits = rims(aggregate, prolong_rows)
    row_a = swap(to_row_a, row_high)
    row_b = swap(to_row_b, row_low)
    col_a = swap(to_col_a, col_high)
    col_b = swap(to_col_b, col_low)
    r, to_a, to_b, own_blocks = step_one(neighbours, coupling, prolong_rows, bits)
    from_b = swap(to_b, col_low)
    from_a = swap(to_a, col_high)
    mine, pair, *cross, extra_a = near_terms(parts, bits, r, own_blocks, col_a)
    from_a, *cross = lax.optimization_barrier((from_a, *cross))
    direct = [xor_swap(value, 2 * h + 2) for h, value in enumerate(cross)]
    columns, column_head = mid_terms(parts, bits, r, col_a, col_b)
    row_a, row_b, columns, from_b = gate((row_a, row_b, columns, from_b), (mine,))
    outs = list(far_terms(counts, bits, r, row_a, row_b, from_a, from_b, columns, column_head, extra_a))
    outs[0], *direct = lax.optimization_barrier((outs[0], *direct))
    outs = [outs[0]] + [xor_swap(outs[s], s) for s in range(1, parts)]
    relayed = xor_swap(jnp.stack([pair] + [value[1] for value in direct]), 1)
    owns = [mine, relayed]
    for value in direct:
        owns += [value, relayed]
    coarse = unpack(outs[:2], owns[:2], range(2), None)
    coarse = unpack(outs[2:], owns[2:], range(2, parts), coarse)
    return coarse[None]


def solution(mesh):
    return jax.shard_map(
        local,
        mesh=mesh,
        in_specs=(
            P("row", "col", None, None, None),
            P("row", "col", None),
            P("row", "col", None, None),
            P("row", "col"),
        ),
        out_specs=P("row", None, None, None, None, "col", None),
        check_vma=False,
    )
```

```python
import functools

import jax
import jax.numpy as jnp
from jax import lax
from jax.experimental import pallas as pl
from jax.experimental.pallas import tpu as pltpu
from jax.sharding import PartitionSpec as P

BS = 128
KA = 12
SIDE = 4
QUAD = 4 * BS
HEAD = 8
ROWS = 2 * QUAD + HEAD
BITS = 16
OWN_SLOTS = 8
SLOTS = 12
ANY = pl.BlockSpec(memory_space=pl.ANY)
VMEM = pl.BlockSpec(memory_space=pltpu.VMEM)
HBM = pl.BlockSpec(memory_space=pltpu.HBM)
BF16 = jnp.bfloat16
F32 = jnp.float32


def flips():
    return lax.rem(lax.axis_index("row"), 2), lax.rem(lax.axis_index("col"), 2)


def turned(index, flip):
    return index + flip - 2 * index * flip


def rims_kernel(agg_hbm, prolong, row_a, row_b, col_a, col_b, bits, agg, sems):
    fx, fy = flips()
    load = pltpu.make_async_copy(agg_hbm, agg, sems.at[16])
    load.start()
    copies = []
    plans = (
        (row_a, ((1, 0), (1, 1))),
        (row_b, ((0, 0), (0, 1))),
        (col_a, ((0, 1), (1, 1))),
        (col_b, ((0, 0), (1, 0))),
    )
    for out, quads in plans:
        for h, (u, v) in enumerate(quads):
            ur, vr = turned(u, fx), turned(v, fy)
            for m in range(2):
                copies.append(
                    pltpu.make_async_copy(
                        prolong.at[2 * ur + m, pl.ds(pl.multiple_of(vr * 256, 256), 256), :],
                        out.at[QUAD * h + 256 * m : QUAD * h + 256 * (m + 1), :],
                        sems.at[len(copies)],
                    )
                )
                copies[-1].start()
    load.wait()
    own = {}
    for k, (u, v) in enumerate(((0, 0), (0, 1), (1, 0), (1, 1))):
        own[u, v] = lax.rem(agg[2 * turned(u, fx), 2 * turned(v, fy)], 2).astype(F32)
        bits[k : k + 1, :] = jnp.full((1, BS), own[u, v], F32)
    bits[4:, :] = jnp.zeros((4, BS), F32)
    for out, quads in plans:
        at = lax.broadcasted_iota(jnp.int32, (HEAD, BS), 0)
        out[2 * QUAD :, :] = jnp.where(at == 0, own[quads[0]], own[quads[1]]).astype(BF16)
    for copy in copies:
        copy.wait()


def rims(agg, prolong_rows):
    shape = jax.ShapeDtypeStruct((ROWS, BS), BF16)
    return pl.pallas_call(
        rims_kernel,
        out_shape=(shape,) * 4 + (jax.ShapeDtypeStruct((8, BS), F32),),
        in_specs=[HBM, HBM],
        out_specs=(VMEM,) * 5,
        scratch_shapes=[pltpu.SMEM((SIDE, SIDE), jnp.int32), pltpu.SemaphoreType.DMA((17,))],
        compiler_params=pltpu.CompilerParams(vmem_limit_bytes=4 << 20),
        name="rims",
    )(agg, prolong_rows)


def sums(r, p, quads):
    fx, fy = flips()
    raw = 2 * turned(p[0] - 1, fx) + turned(p[1] - 1, fy)
    blocks = [r[raw, (u - p[0] + 1) * 3 + v - p[1] + 1] for u, v in quads]
    return blocks[0] if len(blocks) == 1 else jnp.concatenate(blocks, axis=1)


OWN = ((1, 1), (1, 2), (2, 1), (2, 2))
NONE = 16 * KA


def step_one_kernel(
    codes_hbm, coupling, prolong_hbm, after, out, to_a, to_b, prolong, blocks, codes, slot_of, sems
):
    fx, fy = flips()
    load_codes = pltpu.make_async_copy(codes_hbm, codes, sems.at[8])
    load_codes.start()
    load_prolong = pltpu.make_async_copy(prolong_hbm, prolong, sems.at[9])
    load_prolong.start()

    def load(quad, m):
        first = (2 * (quad // 2) + m) * SIDE + 2 * (quad % 2)
        at = pl.ds(first * KA, 2 * KA)
        return pltpu.make_async_copy(coupling.at[at], blocks.at[at], sems.at[2 * quad + m])

    def start(quad):
        for m in range(2):
            load(quad, m).start()

    start(0)
    blocks[NONE] = jnp.zeros((BS, BS), BF16)

    @pl.loop(0, 16)
    def _(n):
        for t in range(25):
            slot_of[n * 25 + t] = NONE

    start(1)
    load_codes.wait()

    @pl.loop(0, 16)
    def _(n):
        for k in range(KA):
            slot_of[n * 25 + codes[n // SIDE, n % SIDE, k]] = n * KA + k

    start(2)
    load_prolong.wait()
    zero = jnp.zeros((BS, BS), BF16)

    @pl.loop(0, 4)
    def _(quad):
        qx, qy = quad // 2, quad % 2
        for m in range(2):
            load(quad, m).wait()

        @pl.when(quad == 0)
        def _():
            start(3)

        left = []
        for ix in range(2):
            rows = prolong[2 * qx + ix, pl.ds(pl.multiple_of(qy * 256, 256), 256), :]
            left.append(rows.T)

        def block(ix, iy, jx, jy):
            if not (0 <= jy - iy <= 4):
                return zero
            n = (2 * qx + ix) * SIDE + 2 * qy + iy
            return blocks[slot_of[n * 25 + (jx - ix) * 5 + jy - iy]]

        for jx in range(6):
            for t in range(3):
                total = None
                for ix in range(2):
                    if not (0 <= jx - ix <= 4):
                        continue
                    right = jnp.concatenate(
                        [
                            jnp.concatenate([block(ix, iy, jx, 2 * t + e) for e in range(2)], axis=1)
                            for iy in range(2)
                        ],
                        axis=0,
                    )
                    part = jnp.dot(left[ix], right, preferred_element_type=F32)
                    total = part if total is None else total + part
                du, dv = jx // 2, t
                at = (du + fx * (2 - 2 * du)) * 3 + dv + fy * (2 - 2 * dv)
                out[quad, at, :, (jx % 2) * 256 : (jx % 2 + 1) * 256] = total.astype(BF16)

    for ref, e, p, q in (
        (to_b, 0, (2, 1), (3, 0)),
        (to_b, 1, (1, 1), (0, 0)),
        (to_a, 0, (2, 2), (3, 3)),
        (to_a, 1, (1, 2), (0, 3)),
    ):
        ref[e] = sums(out, p, (q,))


def step_one(codes, coupling, prolong_rows, after):
    corner = jax.ShapeDtypeStruct((2, BS, QUAD), BF16)
    return pl.pallas_call(
        step_one_kernel,
        out_shape=(
            jax.ShapeDtypeStruct((4, 9, BS, QUAD), BF16),
            corner,
            corner,
            jax.ShapeDtypeStruct(prolong_rows.shape, BF16),
        ),
        in_specs=[HBM] * 3 + [ANY],
        out_specs=(VMEM,) * 4,
        scratch_shapes=[
            pltpu.VMEM((NONE + 1, BS, BS), BF16),
            pltpu.SMEM((SIDE, SIDE, KA), jnp.int32),
            pltpu.SMEM((400,), jnp.int32),
            pltpu.SemaphoreType.DMA((10,)),
        ],
        compiler_params=pltpu.CompilerParams(vmem_limit_bytes=16 << 20),
        cost_estimate=pl.CostEstimate(flops=1 << 33, bytes_accessed=1 << 20, transcendentals=0),
        name="step_one",
    )(codes, coupling, prolong_rows, after)


def half_of(ref, h):
    return ref[2 * QUAD + h : 2 * QUAD + h + 1, :].astype(F32)


def quad_of(ref, h):
    return ref[QUAD * h : QUAD * (h + 1), :]


def edge_slots(near, far, same_a):
    same_b = 1.0 - jnp.abs(half_of(far, 0) - half_of(far, 1))
    second = quad_of(far, 1)
    shared = second * same_b.astype(BF16)
    right = jnp.concatenate(
        [
            jnp.concatenate([quad_of(far, 0), jnp.zeros_like(second)], axis=1),
            jnp.concatenate([shared, second - shared], axis=1),
        ],
        axis=0,
    )
    by_p = [jnp.dot(rows, right, preferred_element_type=F32) for rows in near]
    base, extra = [], []
    for v in range(2):
        one, two = (value[:, v * BS : (v + 1) * BS] for value in by_p)
        shared = same_a * two
        base.append(one + shared)
        extra.append(two - shared)
    return base, extra


def inside(axis, count):
    at = lax.axis_index(axis)
    return jnp.where(at == 0, 0.0, jnp.where(at == count - 1, 0.0, 1.0)).astype(F32)


def store_pieces(outs, at, values):
    rows = BS // len(outs)
    me = lax.axis_index("col")
    for s, out in enumerate(outs):
        start = pl.multiple_of((me ^ s) * rows, rows)
        for t in range(values.shape[0]):
            first = (at + t) * rows
            out[first : first + rows, :] = values[t, pl.ds(start, rows), :].astype(BF16)


def near_kernel(parts, bits, r, prolong, col_a, col_b, *rest):
    outs, (columns, column_head, slots, right) = rest[:-4], rest[-4:]
    fx, fy = flips()

    def by_halves(quads, own, first):
        for j, (_, parts_of, bit) in enumerate(quads):
            for m, rows in enumerate(parts_of):
                step = rows.shape[0]
                at = QUAD * j + step * m
                high = rows * bit.astype(BF16)
                right[at : at + step, 0:BS] = rows - high
                right[at : at + step, BS:] = high
        names = [q for q, _, _ in quads]
        for i, k in enumerate(own):
            value = jnp.dot(sums(r, OWN[k], names), right[0 : QUAD * len(quads), :], preferred_element_type=F32)
            for b in range(2):
                one = value[:, b * BS : (b + 1) * BS]
                high = bits[k : k + 1, :] * one
                low = one - high
                if i == 0:
                    slots[first + b] = low
                    slots[first + 2 + b] = high
                else:
                    slots[first + b] += low
                    slots[first + 2 + b] += high

    quads = []
    for j, (u, v) in enumerate(OWN):
        ur, vr = turned(u - 1, fx), turned(v - 1, fy)
        at = pl.ds(pl.multiple_of(vr * 256, 256), 256)
        quads.append(((u, v), [prolong[2 * ur + m, at, :] for m in range(2)], bits[j : j + 1, :]))
    by_halves(quads, range(4), 0)
    split_y = jnp.abs(bits[0:1, :] - bits[1:2, :])
    for e, (far, own, side, scale) in enumerate(((col_a, 2, 3, None), (col_b, 1, 0, inside("col", parts)))):
        near = [sums(r, (u, own), ((1, side), (2, side))) for u in (1, 2)]
        base, extra = edge_slots(near, far, split_y)
        for t in range(2):
            slots[4 + 2 * e + t] = base[t] if scale is None else base[t] * scale
            columns[2 * e + t] = extra[t] if scale is None else extra[t] * scale
            column_head[2 * e + t : 2 * e + t + 1, :] = half_of(far, t)
    column_head[4:8, :] = bits[0:4, :]
    rows = BS // parts
    me = lax.axis_index("col")
    for s in range(parts):
        start = pl.multiple_of((me ^ s) * rows, rows)
        out = outs[s] if s < 2 else outs[s // 2 + 1]
        for t in range(OWN_SLOTS):
            value = slots[t, pl.ds(start, rows), :].astype(BF16)
            if s < 2:
                out[t] = value
            else:
                out[s % 2, t] = value


def near_terms(parts, *operands):
    rows = BS // parts
    one = jax.ShapeDtypeStruct((OWN_SLOTS, rows, BS), BF16)
    two = jax.ShapeDtypeStruct((2, OWN_SLOTS, rows, BS), BF16)
    shapes = (one, one) + (two,) * (parts // 2 - 1)
    shapes += (jax.ShapeDtypeStruct((4, BS, BS), F32), jax.ShapeDtypeStruct((8, BS), F32))
    return pl.pallas_call(
        functools.partial(near_kernel, parts),
        out_shape=shapes,
        in_specs=[VMEM] * len(operands),
        out_specs=(VMEM,) * len(shapes),
        scratch_shapes=[pltpu.VMEM((OWN_SLOTS, BS, BS), F32), pltpu.VMEM((4 * QUAD, 2 * BS), BF16)],
        compiler_params=pltpu.CompilerParams(vmem_limit_bytes=16 << 20),
        cost_estimate=pl.CostEstimate(flops=1, bytes_accessed=1, transcendentals=0),
        name="near_terms",
    )(*operands)


def fill_edges(r, edges, slots, head):
    for e, (far, own, quads, same_a, scale) in enumerate(edges):
        base, extra = edge_slots([sums(r, p, quads) for p in own], far, same_a)
        for t in range(2):
            slots[2 * e + t] = base[t] if scale is None else base[t] * scale
            slots[4 + 2 * e + t] = extra[t] if scale is None else extra[t] * scale
            head[2 * e + t : 2 * e + t + 1, :] = half_of(far, t)


def far_kernel(counts, bits, r, row_a, row_b, from_a, from_b, columns, column_head, *rest):
    outs, (slots, head) = rest[:-2], rest[-2:]
    split_x = 1.0 - jnp.abs(bits[0:1, :] - bits[1:2, :])
    row_in, col_in = inside("row", counts[0]), inside("col", counts[1])
    head[...] = jnp.zeros_like(head)
    head[0:4, :] = bits[0:4, :]
    head[8:12, :] = column_head[0:4, :]
    edges = (
        (row_a, ((2, 1), (2, 2)), ((3, 1), (3, 2)), split_x, None),
        (row_b, ((1, 1), (1, 2)), ((0, 1), (0, 2)), split_x, row_in),
    )
    fill_edges(r, edges, slots, head.at[4:8])
    for t in range(4):
        slots[4 + t] += columns[t]
    corners = (
        (from_a.at[0], quad_of(row_a, 1), None),
        (from_b.at[0], quad_of(row_a, 0), col_in),
        (from_a.at[1], quad_of(row_b, 1), row_in),
        (from_b.at[1], quad_of(row_b, 0), row_in * col_in),
    )
    for e, (near, far, scale) in enumerate(corners):
        value = jnp.dot(near[...], far, preferred_element_type=F32)
        slots[8 + e] = value if scale is None else value * scale
    store_pieces(outs, 0, slots.at[0:4])
    store_pieces(outs, 4, slots.at[8:12])
    store_pieces(outs, 8, slots.at[4:8])
    for out in outs:
        out[out.shape[0] - BITS :, :] = head[...].astype(BF16)


def far_terms(counts, *operands):
    parts = counts[1]
    message = jax.ShapeDtypeStruct((SLOTS * (BS // parts) + BITS, BS), BF16)
    return pl.pallas_call(
        functools.partial(far_kernel, counts),
        out_shape=(message,) * parts,
        in_specs=[VMEM] * len(operands),
        out_specs=(VMEM,) * parts,
        scratch_shapes=[pltpu.VMEM((12, BS, BS), F32), pltpu.VMEM((BITS, BS), F32)],
        compiler_params=pltpu.CompilerParams(vmem_limit_bytes=16 << 20),
        cost_estimate=pl.CostEstimate(flops=1, bytes_accessed=1, transcendentals=0),
        name="far_terms",
    )(*operands)


def unpack_kernel(parts, steps, *refs):
    ins, owns = refs[: len(steps)], refs[len(steps) : 2 * len(steps)]
    out, buf, sems = refs[-3:]
    me = lax.axis_index("col")
    fx, _ = flips()
    copies = []
    for i, (s, ref) in enumerate(zip(steps, ins)):
        square = me ^ s
        fy = lax.rem(square, 2)
        own = owns[i] if s < 2 else owns[i].at[s // 2 - 1 if s % 2 else 0]
        for a in range(2):
            copies.append(
                pltpu.make_async_copy(own.at[2 * a : 2 * a + 2], out.at[square, a, 4], sems.at[len(copies)])
            )
            copies[-1].start()
        one = functools.partial(bit_row, ref)
        split_y = jnp.abs(one(0) - one(1))

        def send(piece, owner, code):
            copies.append(pltpu.make_async_copy(buf.at[i, piece], out.at[owner, :, code], sems.at[len(copies)]))
            copies[-1].start()

        split_x = 1.0 - split_y
        edges = (
            ((2, 3), (8, 9), split_y, 7 - 6 * fx),
            ((0, 1), (10, 11), split_y, 1 + 6 * fx),
            ((1, 3), (8, 9), split_x, 3 + turn3(2, fy)),
            ((0, 2), (10, 11), split_x, 3 + turn3(0, fy)),
        )
        for e, (ps, more, used, code) in enumerate(edges):
            if e < 2:
                values = [slot(ref, 2 * e + t) for t in range(2)]
            else:
                values = [own[2 * e + t].astype(F32) for t in range(2)]
            second = [slot(ref, t) for t in more]
            spread_edge(buf, (i, e), one, ps, (4 + 2 * e, 5 + 2 * e), values, second, used)
            send(e, square, code)
        high = square ^ 1
        low = square + 2 * fy - 1
        low = jnp.where((low < 0) | (low >= parts), square, low)
        corners = (
            (high, 6 - 6 * fx, 2, 9, 5),
            (low, 6 - 6 * fx, 0, 11, 4),
            (high, 6 * fx, 2, 8, 7),
            (low, 6 * fx, 0, 10, 6),
        )
        for e, (owner, group, side, a_bit, b_bit) in enumerate(corners):
            spread_corner(buf, (i, 4 + e), slot(ref, 4 + e), one(a_bit), one(b_bit))
            send(4 + e, owner, group + turn3(side, lax.rem(owner, 2)))
    for copy in copies:
        copy.wait()


def unpack(messages, owns, steps, coarse):
    parts = lax.axis_size("col")
    rows = BS // parts
    fresh = coarse is None
    return pl.pallas_call(
        functools.partial(unpack_kernel, parts, steps),
        out_shape=jax.ShapeDtypeStruct((parts, 2, 9, 2, rows, BS), BF16),
        in_specs=[VMEM] * (2 * len(steps)) + [ANY] * (not fresh),
        out_specs=ANY,
        scratch_shapes=[
            pltpu.VMEM((len(steps), 8, 2, 2, rows, BS), BF16),
            pltpu.SemaphoreType.DMA((10 * len(steps),)),
        ],
        input_output_aliases={} if fresh else {2 * len(steps): 0},
        compiler_params=pltpu.CompilerParams(vmem_limit_bytes=16 << 20),
        cost_estimate=pl.CostEstimate(flops=1, bytes_accessed=1, transcendentals=0),
        name="unpack",
    )(*messages, *owns, *(() if fresh else (coarse,)))


def turn3(index, flip):
    return index + flip * (2 - 2 * index)


def bit_row(ref, k):
    at = ref.shape[0] - BITS + k
    return ref[at : at + 1, :].astype(F32)


def slot(ref, t):
    rows = (ref.shape[0] - BITS) // SLOTS
    return ref[t * rows : (t + 1) * rows, :].astype(F32)


def spread(buf, at, center):
    i, piece = at
    for a in range(2):
        for b in range(2):
            buf[i, piece, a, b] = center[2 * a + b].astype(BF16)


def spread_edge(buf, at, one, ps, qs, values, more, used):
    a_bits = [one(p) for p in ps]
    b_bits = [one(q) for q in qs]
    center = [None] * 4
    for b in range(2):
        picks = [bit if b else 1.0 - bit for bit in b_bits]
        first = picks[0] * values[0] + picks[1] * values[1]
        second = (used * picks[0]) * more[0] + (used * picks[1]) * more[1]
        for a in range(2):
            ia = [bit if a else 1.0 - bit for bit in a_bits]
            center[2 * a + b] = ia[0] * first + ia[1] * second
    spread(buf, at, center)


def spread_corner(buf, at, value, a_bit, b_bit):
    center = []
    for a in range(2):
        for b in range(2):
            center.append(((a_bit if a else 1.0 - a_bit) * (b_bit if b else 1.0 - b_bit)) * value)
    spread(buf, at, center)


def gate_kernel(*refs):
    pass


def gate(values, after):
    count = len(values)
    return pl.pallas_call(
        gate_kernel,
        out_shape=tuple(jax.ShapeDtypeStruct(v.shape, v.dtype) for v in values),
        in_specs=[ANY] * (count + len(after)),
        out_specs=(ANY,) * count,
        input_output_aliases={i: i for i in range(count)},
        compiler_params=pltpu.CompilerParams(vmem_limit_bytes=1 << 20),
        cost_estimate=pl.CostEstimate(flops=1 << 33, bytes_accessed=1, transcendentals=0),
        name="gate",
    )(*values, *after)


def other_side(index):
    return index + 1 if index % 2 else index - 1


def row_low(r, c, rows, cols):
    far = other_side(r)
    return (far, c) if 0 <= far < rows else (r, c ^ 1)


def col_low(r, c, rows, cols):
    far = other_side(c)
    if 0 <= far < cols:
        return r, far
    if r % 2:
        return (r - 2 if r >= 2 else r - 1), c
    return (r + 2 if r + 2 < rows else r + 1), c


def row_high(r, c, rows, cols):
    return r ^ 1, c


def col_high(r, c, rows, cols):
    return r, c ^ 1


def swap(value, partner):
    rows, cols = lax.axis_size("row"), lax.axis_size("col")
    pairs = []
    for r in range(rows):
        for c in range(cols):
            to_r, to_c = partner(r, c, rows, cols)
            pairs.append((r * cols + c, to_r * cols + to_c))
    return lax.ppermute(value, ("row", "col"), pairs)


def xor_swap(value, s):
    return lax.ppermute(value, "col", [(i, i ^ s) for i in range(lax.axis_size("col"))])


def local(coupling, neighbours, prolong, aggregate):
    parts = lax.axis_size("col")
    counts = (lax.axis_size("row"), parts)
    coupling = pltpu.with_memory_space_constraint(coupling.reshape(-1, BS, BS), pltpu.HBM)
    neighbours = pltpu.with_memory_space_constraint(neighbours, pltpu.HBM)
    aggregate = pltpu.with_memory_space_constraint(aggregate, pltpu.HBM)
    prolong_rows = pltpu.with_memory_space_constraint(prolong.reshape(SIDE, SIDE * BS, BS), pltpu.HBM)
    to_row_a, to_row_b, to_col_a, to_col_b, bits = rims(aggregate, prolong_rows)
    row_a = swap(to_row_a, row_high)
    row_b = swap(to_row_b, row_low)
    col_a = swap(to_col_a, col_high)
    col_b = swap(to_col_b, col_low)
    r, to_a, to_b, own_blocks = step_one(neighbours, coupling, prolong_rows, bits)
    from_b = swap(to_b, col_low)
    from_a = swap(to_a, col_high)
    mine, pair, *cross, columns, column_head = near_terms(parts, bits, r, own_blocks, col_a, col_b)
    direct = [xor_swap(value, 2 * h + 2) for h, value in enumerate(cross)]
    row_a, row_b, columns, from_b = gate((row_a, row_b, columns, from_b), (mine,))
    outs = list(far_terms(counts, bits, r, row_a, row_b, from_a, from_b, columns, column_head))
    outs[0], pair, *direct = lax.optimization_barrier((outs[0], pair, *direct))
    outs = [outs[0]] + [xor_swap(outs[s], s) for s in range(1, parts)]
    pair = xor_swap(pair, 1)
    relayed = xor_swap(jnp.concatenate([value[1:2] for value in direct]), 1)
    owns = [mine, pair]
    for value in direct:
        owns += [value, relayed]
    coarse = unpack(outs[:2], owns[:2], range(2), None)
    coarse = unpack(outs[2:], owns[2:], range(2, parts), coarse)
    return coarse[None]


def solution(mesh):
    return jax.shard_map(
        local,
        mesh=mesh,
        in_specs=(
            P("row", "col", None, None, None),
            P("row", "col", None),
            P("row", "col", None, None),
            P("row", "col"),
        ),
        out_specs=P("row", None, None, None, None, "col", None),
        check_vma=False,
    )
```

```python
import functools

import jax
import jax.numpy as jnp
from jax import lax
from jax.experimental import pallas as pl
from jax.experimental.pallas import tpu as pltpu
from jax.sharding import PartitionSpec as P

BS = 128
KA = 12
SIDE = 4
QUAD = 4 * BS
HEAD = 8
ROWS = 2 * QUAD + HEAD
BITS = 16
OWN_SLOTS = 8
SLOTS = 12
ANY = pl.BlockSpec(memory_space=pl.ANY)
VMEM = pl.BlockSpec(memory_space=pltpu.VMEM)
HBM = pl.BlockSpec(memory_space=pltpu.HBM)
BF16 = jnp.bfloat16
F32 = jnp.float32


def flips():
    return lax.rem(lax.axis_index("row"), 2), lax.rem(lax.axis_index("col"), 2)


def turned(index, flip):
    return index + flip - 2 * index * flip


def rims_kernel(agg_hbm, prolong, row_a, row_b, col_a, col_b, bits, agg, sems):
    fx, fy = flips()
    load = pltpu.make_async_copy(agg_hbm, agg, sems.at[16])
    load.start()
    copies = []
    plans = (
        (row_a, ((1, 0), (1, 1))),
        (row_b, ((0, 0), (0, 1))),
        (col_a, ((0, 1), (1, 1))),
        (col_b, ((0, 0), (1, 0))),
    )
    for out, quads in plans:
        for h, (u, v) in enumerate(quads):
            ur, vr = turned(u, fx), turned(v, fy)
            for m in range(2):
                copies.append(
                    pltpu.make_async_copy(
                        prolong.at[2 * ur + m, pl.ds(pl.multiple_of(vr * 256, 256), 256), :],
                        out.at[QUAD * h + 256 * m : QUAD * h + 256 * (m + 1), :],
                        sems.at[len(copies)],
                    )
                )
                copies[-1].start()
    load.wait()
    own = {}
    for k, (u, v) in enumerate(((0, 0), (0, 1), (1, 0), (1, 1))):
        own[u, v] = lax.rem(agg[2 * turned(u, fx), 2 * turned(v, fy)], 2).astype(F32)
        bits[k : k + 1, :] = jnp.full((1, BS), own[u, v], F32)
    bits[4:, :] = jnp.zeros((4, BS), F32)
    for out, quads in plans:
        at = lax.broadcasted_iota(jnp.int32, (HEAD, BS), 0)
        out[2 * QUAD :, :] = jnp.where(at == 0, own[quads[0]], own[quads[1]]).astype(BF16)
    for copy in copies:
        copy.wait()


def rims(agg, prolong_rows):
    shape = jax.ShapeDtypeStruct((ROWS, BS), BF16)
    return pl.pallas_call(
        rims_kernel,
        out_shape=(shape,) * 4 + (jax.ShapeDtypeStruct((8, BS), F32),),
        in_specs=[HBM, HBM],
        out_specs=(VMEM,) * 5,
        scratch_shapes=[pltpu.SMEM((SIDE, SIDE), jnp.int32), pltpu.SemaphoreType.DMA((17,))],
        compiler_params=pltpu.CompilerParams(vmem_limit_bytes=4 << 20),
        name="rims",
    )(agg, prolong_rows)


def sums(r, p, quads):
    fx, fy = flips()
    raw = 2 * turned(p[0] - 1, fx) + turned(p[1] - 1, fy)
    blocks = [r[raw, (u - p[0] + 1) * 3 + v - p[1] + 1] for u, v in quads]
    return blocks[0] if len(blocks) == 1 else jnp.concatenate(blocks, axis=1)


OWN = ((1, 1), (1, 2), (2, 1), (2, 2))
NONE = 16 * KA


def step_one_kernel(
    codes_hbm, coupling, prolong_hbm, after, out, to_a, to_b, prolong, blocks, codes, slot_of, sems
):
    fx, fy = flips()
    load_codes = pltpu.make_async_copy(codes_hbm, codes, sems.at[8])
    load_codes.start()
    load_prolong = pltpu.make_async_copy(prolong_hbm, prolong, sems.at[9])
    load_prolong.start()

    def load(quad, m):
        first = (2 * (quad // 2) + m) * SIDE + 2 * (quad % 2)
        at = pl.ds(first * KA, 2 * KA)
        return pltpu.make_async_copy(coupling.at[at], blocks.at[at], sems.at[2 * quad + m])

    def start(quad):
        for m in range(2):
            load(quad, m).start()

    start(0)
    blocks[NONE] = jnp.zeros((BS, BS), BF16)

    @pl.loop(0, 16)
    def _(n):
        for t in range(25):
            slot_of[n * 25 + t] = NONE

    start(1)
    load_codes.wait()

    @pl.loop(0, 16)
    def _(n):
        for k in range(KA):
            slot_of[n * 25 + codes[n // SIDE, n % SIDE, k]] = n * KA + k

    start(2)
    load_prolong.wait()
    zero = jnp.zeros((BS, BS), BF16)

    @pl.loop(0, 4)
    def _(quad):
        qx, qy = quad // 2, quad % 2
        for m in range(2):
            load(quad, m).wait()

        @pl.when(quad == 0)
        def _():
            start(3)

        left = []
        for ix in range(2):
            rows = prolong[2 * qx + ix, pl.ds(pl.multiple_of(qy * 256, 256), 256), :]
            left.append(rows.T)

        def block(ix, iy, jx, jy):
            if not (0 <= jy - iy <= 4):
                return zero
            n = (2 * qx + ix) * SIDE + 2 * qy + iy
            return blocks[slot_of[n * 25 + (jx - ix) * 5 + jy - iy]]

        for jx in range(6):
            for t in range(3):
                total = None
                for ix in range(2):
                    if not (0 <= jx - ix <= 4):
                        continue
                    right = jnp.concatenate(
                        [
                            jnp.concatenate([block(ix, iy, jx, 2 * t + e) for e in range(2)], axis=1)
                            for iy in range(2)
                        ],
                        axis=0,
                    )
                    part = jnp.dot(left[ix], right, preferred_element_type=F32)
                    total = part if total is None else total + part
                du, dv = jx // 2, t
                at = (du + fx * (2 - 2 * du)) * 3 + dv + fy * (2 - 2 * dv)
                out[quad, at, :, (jx % 2) * 256 : (jx % 2 + 1) * 256] = total.astype(BF16)

    for ref, e, p, q in (
        (to_b, 0, (2, 1), (3, 0)),
        (to_b, 1, (1, 1), (0, 0)),
        (to_a, 0, (2, 2), (3, 3)),
        (to_a, 1, (1, 2), (0, 3)),
    ):
        ref[e] = sums(out, p, (q,))


def step_one(codes, coupling, prolong_rows, after):
    corner = jax.ShapeDtypeStruct((2, BS, QUAD), BF16)
    return pl.pallas_call(
        step_one_kernel,
        out_shape=(
            jax.ShapeDtypeStruct((4, 9, BS, QUAD), BF16),
            corner,
            corner,
            jax.ShapeDtypeStruct(prolong_rows.shape, BF16),
        ),
        in_specs=[HBM] * 3 + [ANY],
        out_specs=(VMEM,) * 4,
        scratch_shapes=[
            pltpu.VMEM((NONE + 1, BS, BS), BF16),
            pltpu.SMEM((SIDE, SIDE, KA), jnp.int32),
            pltpu.SMEM((400,), jnp.int32),
            pltpu.SemaphoreType.DMA((10,)),
        ],
        compiler_params=pltpu.CompilerParams(vmem_limit_bytes=16 << 20),
        cost_estimate=pl.CostEstimate(flops=1 << 33, bytes_accessed=1 << 20, transcendentals=0),
        name="step_one",
    )(codes, coupling, prolong_rows, after)


def half_of(ref, h):
    return ref[2 * QUAD + h : 2 * QUAD + h + 1, :].astype(F32)


def quad_of(ref, h):
    return ref[QUAD * h : QUAD * (h + 1), :]


def edge_slots(near, far, same_a):
    same_b = 1.0 - jnp.abs(half_of(far, 0) - half_of(far, 1))
    second = quad_of(far, 1)
    shared = second * same_b.astype(BF16)
    right = jnp.concatenate(
        [
            jnp.concatenate([quad_of(far, 0), jnp.zeros_like(second)], axis=1),
            jnp.concatenate([shared, second - shared], axis=1),
        ],
        axis=0,
    )
    by_p = [jnp.dot(rows, right, preferred_element_type=F32) for rows in near]
    base, extra = [], []
    for v in range(2):
        one, two = (value[:, v * BS : (v + 1) * BS] for value in by_p)
        shared = same_a * two
        base.append(one + shared)
        extra.append(two - shared)
    return base, extra


def inside(axis, count):
    at = lax.axis_index(axis)
    return jnp.where(at == 0, 0.0, jnp.where(at == count - 1, 0.0, 1.0)).astype(F32)


def store_pieces(outs, at, values):
    rows = BS // len(outs)
    me = lax.axis_index("col")
    for s, out in enumerate(outs):
        start = pl.multiple_of((me ^ s) * rows, rows)
        for t in range(values.shape[0]):
            first = (at + t) * rows
            out[first : first + rows, :] = values[t, pl.ds(start, rows), :].astype(BF16)


def near_kernel(parts, bits, r, prolong, col_a, col_b, *rest):
    outs, (columns, column_head, slots, right) = rest[:-4], rest[-4:]
    fx, fy = flips()

    def by_halves(quads, own, first):
        for j, (_, parts_of, bit) in enumerate(quads):
            for m, rows in enumerate(parts_of):
                step = rows.shape[0]
                at = QUAD * j + step * m
                high = rows * bit.astype(BF16)
                right[at : at + step, 0:BS] = rows - high
                right[at : at + step, BS:] = high
        names = [q for q, _, _ in quads]
        for i, k in enumerate(own):
            value = jnp.dot(sums(r, OWN[k], names), right[0 : QUAD * len(quads), :], preferred_element_type=F32)
            for b in range(2):
                one = value[:, b * BS : (b + 1) * BS]
                high = bits[k : k + 1, :] * one
                low = one - high
                if i == 0:
                    slots[first + b] = low
                    slots[first + 2 + b] = high
                else:
                    slots[first + b] += low
                    slots[first + 2 + b] += high

    quads = []
    for j, (u, v) in enumerate(OWN):
        ur, vr = turned(u - 1, fx), turned(v - 1, fy)
        at = pl.ds(pl.multiple_of(vr * 256, 256), 256)
        quads.append(((u, v), [prolong[2 * ur + m, at, :] for m in range(2)], bits[j : j + 1, :]))
    by_halves(quads, range(4), 0)
    split_y = jnp.abs(bits[0:1, :] - bits[1:2, :])
    for e, (far, own, side, scale) in enumerate(((col_a, 2, 3, None), (col_b, 1, 0, inside("col", parts)))):
        near = [sums(r, (u, own), ((1, side), (2, side))) for u in (1, 2)]
        base, extra = edge_slots(near, far, split_y)
        for t in range(2):
            slots[4 + 2 * e + t] = base[t] if scale is None else base[t] * scale
            columns[2 * e + t] = extra[t] if scale is None else extra[t] * scale
            column_head[2 * e + t : 2 * e + t + 1, :] = half_of(far, t)
    column_head[4:8, :] = bits[0:4, :]
    rows = BS // parts
    me = lax.axis_index("col")
    for s in range(parts):
        start = pl.multiple_of((me ^ s) * rows, rows)
        out = outs[s] if s < 2 else outs[s // 2 + 1]
        for t in range(OWN_SLOTS):
            value = slots[t, pl.ds(start, rows), :].astype(BF16)
            if s < 2:
                out[t] = value
            else:
                out[s % 2, t] = value


def near_terms(parts, *operands):
    rows = BS // parts
    one = jax.ShapeDtypeStruct((OWN_SLOTS, rows, BS), BF16)
    two = jax.ShapeDtypeStruct((2, OWN_SLOTS, rows, BS), BF16)
    shapes = (one, one) + (two,) * (parts // 2 - 1)
    shapes += (jax.ShapeDtypeStruct((4, BS, BS), F32), jax.ShapeDtypeStruct((8, BS), F32))
    return pl.pallas_call(
        functools.partial(near_kernel, parts),
        out_shape=shapes,
        in_specs=[VMEM] * len(operands),
        out_specs=(VMEM,) * len(shapes),
        scratch_shapes=[pltpu.VMEM((OWN_SLOTS, BS, BS), F32), pltpu.VMEM((4 * QUAD, 2 * BS), BF16)],
        compiler_params=pltpu.CompilerParams(vmem_limit_bytes=16 << 20),
        cost_estimate=pl.CostEstimate(flops=1, bytes_accessed=1, transcendentals=0),
        name="near_terms",
    )(*operands)


def fill_edges(r, edges, slots, head):
    for e, (far, own, quads, same_a, scale) in enumerate(edges):
        base, extra = edge_slots([sums(r, p, quads) for p in own], far, same_a)
        for t in range(2):
            slots[2 * e + t] = base[t] if scale is None else base[t] * scale
            slots[4 + 2 * e + t] = extra[t] if scale is None else extra[t] * scale
            head[2 * e + t : 2 * e + t + 1, :] = half_of(far, t)


def far_kernel(counts, bits, r, row_a, row_b, from_a, from_b, columns, column_head, *rest):
    outs, (slots, head) = rest[:-2], rest[-2:]
    split_x = 1.0 - jnp.abs(bits[0:1, :] - bits[1:2, :])
    row_in, col_in = inside("row", counts[0]), inside("col", counts[1])
    head[...] = jnp.zeros_like(head)
    head[0:4, :] = bits[0:4, :]
    head[8:12, :] = column_head[0:4, :]
    edges = (
        (row_a, ((2, 1), (2, 2)), ((3, 1), (3, 2)), split_x, None),
        (row_b, ((1, 1), (1, 2)), ((0, 1), (0, 2)), split_x, row_in),
    )
    fill_edges(r, edges, slots, head.at[4:8])
    for t in range(4):
        slots[4 + t] += columns[t]
    corners = (
        (from_a.at[0], quad_of(row_a, 1), None),
        (from_b.at[0], quad_of(row_a, 0), col_in),
        (from_a.at[1], quad_of(row_b, 1), row_in),
        (from_b.at[1], quad_of(row_b, 0), row_in * col_in),
    )
    for e, (near, far, scale) in enumerate(corners):
        value = jnp.dot(near[...], far, preferred_element_type=F32)
        slots[8 + e] = value if scale is None else value * scale
    store_pieces(outs, 0, slots.at[0:4])
    store_pieces(outs, 4, slots.at[8:12])
    store_pieces(outs, 8, slots.at[4:8])
    for out in outs:
        out[out.shape[0] - BITS :, :] = head[...].astype(BF16)


def far_terms(counts, *operands):
    parts = counts[1]
    message = jax.ShapeDtypeStruct((SLOTS * (BS // parts) + BITS, BS), BF16)
    return pl.pallas_call(
        functools.partial(far_kernel, counts),
        out_shape=(message,) * parts,
        in_specs=[VMEM] * len(operands),
        out_specs=(VMEM,) * parts,
        scratch_shapes=[pltpu.VMEM((12, BS, BS), F32), pltpu.VMEM((BITS, BS), F32)],
        compiler_params=pltpu.CompilerParams(vmem_limit_bytes=16 << 20),
        cost_estimate=pl.CostEstimate(flops=1, bytes_accessed=1, transcendentals=0),
        name="far_terms",
    )(*operands)


def unpack_kernel(parts, steps, *refs):
    ins, owns = refs[: len(steps)], refs[len(steps) : 2 * len(steps)]
    out, buf, sems = refs[-3:]
    me = lax.axis_index("col")
    fx, _ = flips()
    copies = []
    for i, (s, ref) in enumerate(zip(steps, ins)):
        square = me ^ s
        fy = lax.rem(square, 2)
        own = owns[i] if s < 2 else owns[i].at[s // 2 - 1 if s % 2 else 0]
        for a in range(2):
            copies.append(
                pltpu.make_async_copy(own.at[2 * a : 2 * a + 2], out.at[square, a, 4], sems.at[len(copies)])
            )
            copies[-1].start()
        one = functools.partial(bit_row, ref)
        split_y = jnp.abs(one(0) - one(1))

        def send(piece, owner, code):
            copies.append(pltpu.make_async_copy(buf.at[i, piece], out.at[owner, :, code], sems.at[len(copies)]))
            copies[-1].start()

        split_x = 1.0 - split_y
        edges = (
            ((2, 3), (8, 9), split_y, 7 - 6 * fx),
            ((0, 1), (10, 11), split_y, 1 + 6 * fx),
            ((1, 3), (8, 9), split_x, 3 + turn3(2, fy)),
            ((0, 2), (10, 11), split_x, 3 + turn3(0, fy)),
        )
        for e, (ps, more, used, code) in enumerate(edges):
            if e < 2:
                values = [slot(ref, 2 * e + t) for t in range(2)]
            else:
                values = [own[2 * e + t].astype(F32) for t in range(2)]
            second = [slot(ref, t) for t in more]
            spread_edge(buf, (i, e), one, ps, (4 + 2 * e, 5 + 2 * e), values, second, used)
            send(e, square, code)
        high = square ^ 1
        low = square + 2 * fy - 1
        low = jnp.where((low < 0) | (low >= parts), square, low)
        corners = (
            (high, 6 - 6 * fx, 2, 9, 5),
            (low, 6 - 6 * fx, 0, 11, 4),
            (high, 6 * fx, 2, 8, 7),
            (low, 6 * fx, 0, 10, 6),
        )
        for e, (owner, group, side, a_bit, b_bit) in enumerate(corners):
            spread_corner(buf, (i, 4 + e), slot(ref, 4 + e), one(a_bit), one(b_bit))
            send(4 + e, owner, group + turn3(side, lax.rem(owner, 2)))
    for copy in copies:
        copy.wait()


def unpack(messages, owns, steps, coarse):
    parts = lax.axis_size("col")
    rows = BS // parts
    fresh = coarse is None
    return pl.pallas_call(
        functools.partial(unpack_kernel, parts, steps),
        out_shape=jax.ShapeDtypeStruct((parts, 2, 9, 2, rows, BS), BF16),
        in_specs=[VMEM] * (2 * len(steps)) + [ANY] * (not fresh),
        out_specs=ANY,
        scratch_shapes=[
            pltpu.VMEM((len(steps), 8, 2, 2, rows, BS), BF16),
            pltpu.SemaphoreType.DMA((10 * len(steps),)),
        ],
        input_output_aliases={} if fresh else {2 * len(steps): 0},
        compiler_params=pltpu.CompilerParams(vmem_limit_bytes=16 << 20),
        cost_estimate=pl.CostEstimate(flops=1, bytes_accessed=1, transcendentals=0),
        name="unpack",
    )(*messages, *owns, *(() if fresh else (coarse,)))


def turn3(index, flip):
    return index + flip * (2 - 2 * index)


def bit_row(ref, k):
    at = ref.shape[0] - BITS + k
    return ref[at : at + 1, :].astype(F32)


def slot(ref, t):
    rows = (ref.shape[0] - BITS) // SLOTS
    return ref[t * rows : (t + 1) * rows, :].astype(F32)


def spread(buf, at, center):
    i, piece = at
    for a in range(2):
        for b in range(2):
            buf[i, piece, a, b] = center[2 * a + b].astype(BF16)


def spread_edge(buf, at, one, ps, qs, values, more, used):
    a_bits = [one(p) for p in ps]
    b_bits = [one(q) for q in qs]
    center = [None] * 4
    for b in range(2):
        picks = [bit if b else 1.0 - bit for bit in b_bits]
        first = picks[0] * values[0] + picks[1] * values[1]
        second = (used * picks[0]) * more[0] + (used * picks[1]) * more[1]
        for a in range(2):
            ia = [bit if a else 1.0 - bit for bit in a_bits]
            center[2 * a + b] = ia[0] * first + ia[1] * second
    spread(buf, at, center)


def spread_corner(buf, at, value, a_bit, b_bit):
    center = []
    for a in range(2):
        for b in range(2):
            center.append(((a_bit if a else 1.0 - a_bit) * (b_bit if b else 1.0 - b_bit)) * value)
    spread(buf, at, center)


def gate_kernel(*refs):
    pass


def gate(values, after):
    count = len(values)
    return pl.pallas_call(
        gate_kernel,
        out_shape=tuple(jax.ShapeDtypeStruct(v.shape, v.dtype) for v in values),
        in_specs=[ANY] * (count + len(after)),
        out_specs=(ANY,) * count,
        input_output_aliases={i: i for i in range(count)},
        compiler_params=pltpu.CompilerParams(vmem_limit_bytes=1 << 20),
        cost_estimate=pl.CostEstimate(flops=1 << 33, bytes_accessed=1, transcendentals=0),
        name="gate",
    )(*values, *after)


def other_side(index):
    return index + 1 if index % 2 else index - 1


def row_low(r, c, rows, cols):
    far = other_side(r)
    return (far, c) if 0 <= far < rows else (r, c ^ 1)


def col_low(r, c, rows, cols):
    far = other_side(c)
    if 0 <= far < cols:
        return r, far
    if r % 2:
        return (r - 2 if r >= 2 else r - 1), c
    return (r + 2 if r + 2 < rows else r + 1), c


def row_high(r, c, rows, cols):
    return r ^ 1, c


def col_high(r, c, rows, cols):
    return r, c ^ 1


def swap(value, partner):
    rows, cols = lax.axis_size("row"), lax.axis_size("col")
    pairs = []
    for r in range(rows):
        for c in range(cols):
            to_r, to_c = partner(r, c, rows, cols)
            pairs.append((r * cols + c, to_r * cols + to_c))
    return lax.ppermute(value, ("row", "col"), pairs)


def xor_swap(value, s):
    return lax.ppermute(value, "col", [(i, i ^ s) for i in range(lax.axis_size("col"))])


def local(coupling, neighbours, prolong, aggregate):
    parts = lax.axis_size("col")
    counts = (lax.axis_size("row"), parts)
    coupling = pltpu.with_memory_space_constraint(coupling.reshape(-1, BS, BS), pltpu.HBM)
    neighbours = pltpu.with_memory_space_constraint(neighbours, pltpu.HBM)
    aggregate = pltpu.with_memory_space_constraint(aggregate, pltpu.HBM)
    prolong_rows = pltpu.with_memory_space_constraint(prolong.reshape(SIDE, SIDE * BS, BS), pltpu.HBM)
    to_row_a, to_row_b, to_col_a, to_col_b, bits = rims(aggregate, prolong_rows)
    row_a = swap(to_row_a, row_high)
    row_b = swap(to_row_b, row_low)
    col_a = swap(to_col_a, col_high)
    col_b = swap(to_col_b, col_low)
    r, to_a, to_b, own_blocks = step_one(neighbours, coupling, prolong_rows, bits)
    from_b = swap(to_b, col_low)
    from_a = swap(to_a, col_high)
    mine, pair, *cross, columns, column_head = near_terms(parts, bits, r, own_blocks, col_a, col_b)
    direct = [xor_swap(value, 2 * h + 2) for h, value in enumerate(cross)]
    row_a, row_b, columns, from_b = gate((row_a, row_b, columns, from_b), (mine,))
    outs = list(far_terms(counts, bits, r, row_a, row_b, from_a, from_b, columns, column_head))
    outs[0], pair, *direct = lax.optimization_barrier((outs[0], pair, *direct))
    outs = [outs[0]] + [xor_swap(outs[s], s) for s in range(1, parts)]
    pair = xor_swap(pair, 1)
    relayed = xor_swap(jnp.concatenate([value[1:2] for value in direct]), 1)
    owns = [mine, pair]
    for value in direct:
        owns += [value, relayed]
    coarse = None
    for first, last in ((0, 2), (2, parts - 1), (parts - 1, parts)):
        coarse = unpack(outs[first:last], owns[first:last], range(first, last), coarse)
    return coarse[None]


def solution(mesh):
    return jax.shard_map(
        local,
        mesh=mesh,
        in_specs=(
            P("row", "col", None, None, None),
            P("row", "col", None),
            P("row", "col", None, None),
            P("row", "col"),
        ),
        out_specs=P("row", None, None, None, None, "col", None),
        check_vma=False,
    )
```

```python
import functools

import jax
import jax.numpy as jnp
from jax import lax
from jax.experimental import pallas as pl
from jax.experimental.pallas import tpu as pltpu
from jax.sharding import PartitionSpec as P

BS = 128
KA = 12
SIDE = 4
QUAD = 4 * BS
HEAD = 8
ROWS = 2 * QUAD + HEAD
BITS = 16
OWN_SLOTS = 8
SLOTS = 12
ANY = pl.BlockSpec(memory_space=pl.ANY)
VMEM = pl.BlockSpec(memory_space=pltpu.VMEM)
HBM = pl.BlockSpec(memory_space=pltpu.HBM)
BF16 = jnp.bfloat16
F32 = jnp.float32


def flips():
    return lax.rem(lax.axis_index("row"), 2), lax.rem(lax.axis_index("col"), 2)


def turned(index, flip):
    return index + flip - 2 * index * flip


def rims_kernel(agg_hbm, prolong, row_a, row_b, bits, agg, sems):
    fx, fy = flips()
    load = pltpu.make_async_copy(agg_hbm, agg, sems.at[8])
    load.start()
    copies = []
    plans = (
        (row_a, ((1, 0), (1, 1))),
        (row_b, ((0, 0), (0, 1))),
    )
    for out, quads in plans:
        for h, (u, v) in enumerate(quads):
            ur, vr = turned(u, fx), turned(v, fy)
            for m in range(2):
                copies.append(
                    pltpu.make_async_copy(
                        prolong.at[2 * ur + m, pl.ds(pl.multiple_of(vr * 256, 256), 256), :],
                        out.at[QUAD * h + 256 * m : QUAD * h + 256 * (m + 1), :],
                        sems.at[len(copies)],
                    )
                )
                copies[-1].start()
    load.wait()
    own = {}
    for k, (u, v) in enumerate(((0, 0), (0, 1), (1, 0), (1, 1))):
        own[u, v] = lax.rem(agg[2 * turned(u, fx), 2 * turned(v, fy)], 2).astype(F32)
        bits[k : k + 1, :] = jnp.full((1, BS), own[u, v], F32)
    bits[4:, :] = jnp.zeros((4, BS), F32)
    for out, quads in plans:
        at = lax.broadcasted_iota(jnp.int32, (HEAD, BS), 0)
        out[2 * QUAD :, :] = jnp.where(at == 0, own[quads[0]], own[quads[1]]).astype(BF16)
    for copy in copies:
        copy.wait()


def rims(agg, prolong_rows):
    shape = jax.ShapeDtypeStruct((ROWS, BS), BF16)
    return pl.pallas_call(
        rims_kernel,
        out_shape=(shape,) * 2 + (jax.ShapeDtypeStruct((8, BS), F32),),
        in_specs=[HBM, HBM],
        out_specs=(VMEM,) * 3,
        scratch_shapes=[pltpu.SMEM((SIDE, SIDE), jnp.int32), pltpu.SemaphoreType.DMA((9,))],
        compiler_params=pltpu.CompilerParams(vmem_limit_bytes=4 << 20),
        name="rims",
    )(agg, prolong_rows)


def column_rims_kernel(row_a, row_b, bits, col_a, col_b):
    at = lax.broadcasted_iota(jnp.int32, (HEAD, BS), 0)
    for v, out in ((1, col_a), (0, col_b)):
        for h, rows in enumerate((row_b, row_a)):
            out[QUAD * h : QUAD * (h + 1), :] = rows[QUAD * v : QUAD * (v + 1), :]
        out[2 * QUAD :, :] = jnp.where(at == 0, bits[v : v + 1, :], bits[2 + v : 3 + v, :]).astype(BF16)


def column_rims(row_a, row_b, bits):
    shape = jax.ShapeDtypeStruct((ROWS, BS), BF16)
    return pl.pallas_call(
        column_rims_kernel,
        out_shape=(shape,) * 2,
        in_specs=[VMEM] * 3,
        out_specs=(VMEM,) * 2,
        compiler_params=pltpu.CompilerParams(vmem_limit_bytes=4 << 20),
        cost_estimate=pl.CostEstimate(flops=1, bytes_accessed=1, transcendentals=0),
        name="column_rims",
    )(row_a, row_b, bits)


def sums(r, p, quads):
    fx, fy = flips()
    raw = 2 * turned(p[0] - 1, fx) + turned(p[1] - 1, fy)
    blocks = [r[raw, (u - p[0] + 1) * 3 + v - p[1] + 1] for u, v in quads]
    return blocks[0] if len(blocks) == 1 else jnp.concatenate(blocks, axis=1)


OWN = ((1, 1), (1, 2), (2, 1), (2, 2))
NONE = 16 * KA


def step_one_kernel(
    codes_hbm, coupling, prolong_hbm, after, out, to_a, to_b, prolong, blocks, codes, slot_of, sems
):
    fx, fy = flips()
    load_codes = pltpu.make_async_copy(codes_hbm, codes, sems.at[8])
    load_codes.start()
    load_prolong = pltpu.make_async_copy(prolong_hbm, prolong, sems.at[9])
    load_prolong.start()

    def load(quad, m):
        first = (2 * (quad // 2) + m) * SIDE + 2 * (quad % 2)
        at = pl.ds(first * KA, 2 * KA)
        return pltpu.make_async_copy(coupling.at[at], blocks.at[at], sems.at[2 * quad + m])

    def start(quad):
        for m in range(2):
            load(quad, m).start()

    start(0)
    blocks[NONE] = jnp.zeros((BS, BS), BF16)

    @pl.loop(0, 16)
    def _(n):
        for t in range(25):
            slot_of[n * 25 + t] = NONE

    start(1)
    load_codes.wait()

    @pl.loop(0, 16)
    def _(n):
        for k in range(KA):
            slot_of[n * 25 + codes[n // SIDE, n % SIDE, k]] = n * KA + k

    start(2)
    load_prolong.wait()
    zero = jnp.zeros((BS, BS), BF16)

    @pl.loop(0, 4)
    def _(quad):
        qx, qy = quad // 2, quad % 2
        for m in range(2):
            load(quad, m).wait()

        @pl.when(quad == 0)
        def _():
            start(3)

        left = []
        for ix in range(2):
            rows = prolong[2 * qx + ix, pl.ds(pl.multiple_of(qy * 256, 256), 256), :]
            left.append(rows.T)

        def block(ix, iy, jx, jy):
            if not (0 <= jy - iy <= 4):
                return zero
            n = (2 * qx + ix) * SIDE + 2 * qy + iy
            return blocks[slot_of[n * 25 + (jx - ix) * 5 + jy - iy]]

        for jx in range(6):
            for t in range(3):
                total = None
                for ix in range(2):
                    if not (0 <= jx - ix <= 4):
                        continue
                    right = jnp.concatenate(
                        [
                            jnp.concatenate([block(ix, iy, jx, 2 * t + e) for e in range(2)], axis=1)
                            for iy in range(2)
                        ],
                        axis=0,
                    )
                    part = jnp.dot(left[ix], right, preferred_element_type=F32)
                    total = part if total is None else total + part
                du, dv = jx // 2, t
                at = (du + fx * (2 - 2 * du)) * 3 + dv + fy * (2 - 2 * dv)
                out[quad, at, :, (jx % 2) * 256 : (jx % 2 + 1) * 256] = total.astype(BF16)

    for ref, e, p, q in (
        (to_b, 0, (2, 1), (3, 0)),
        (to_b, 1, (1, 1), (0, 0)),
        (to_a, 0, (2, 2), (3, 3)),
        (to_a, 1, (1, 2), (0, 3)),
    ):
        ref[e] = sums(out, p, (q,))


def step_one(codes, coupling, prolong_rows, after):
    corner = jax.ShapeDtypeStruct((2, BS, QUAD), BF16)
    return pl.pallas_call(
        step_one_kernel,
        out_shape=(
            jax.ShapeDtypeStruct((4, 9, BS, QUAD), BF16),
            corner,
            corner,
            jax.ShapeDtypeStruct(prolong_rows.shape, BF16),
        ),
        in_specs=[HBM] * 3 + [ANY],
        out_specs=(VMEM,) * 4,
        scratch_shapes=[
            pltpu.VMEM((NONE + 1, BS, BS), BF16),
            pltpu.SMEM((SIDE, SIDE, KA), jnp.int32),
            pltpu.SMEM((400,), jnp.int32),
            pltpu.SemaphoreType.DMA((10,)),
        ],
        compiler_params=pltpu.CompilerParams(vmem_limit_bytes=16 << 20),
        cost_estimate=pl.CostEstimate(flops=1 << 33, bytes_accessed=1 << 20, transcendentals=0),
        name="step_one",
    )(codes, coupling, prolong_rows, after)


def half_of(ref, h):
    return ref[2 * QUAD + h : 2 * QUAD + h + 1, :].astype(F32)


def quad_of(ref, h):
    return ref[QUAD * h : QUAD * (h + 1), :]


def edge_slots(near, far, same_a):
    same_b = 1.0 - jnp.abs(half_of(far, 0) - half_of(far, 1))
    second = quad_of(far, 1)
    shared = second * same_b.astype(BF16)
    right = jnp.concatenate(
        [
            jnp.concatenate([quad_of(far, 0), jnp.zeros_like(second)], axis=1),
            jnp.concatenate([shared, second - shared], axis=1),
        ],
        axis=0,
    )
    by_p = [jnp.dot(rows, right, preferred_element_type=F32) for rows in near]
    base, extra = [], []
    for v in range(2):
        one, two = (value[:, v * BS : (v + 1) * BS] for value in by_p)
        shared = same_a * two
        base.append(one + shared)
        extra.append(two - shared)
    return base, extra


def inside(axis, count):
    at = lax.axis_index(axis)
    return jnp.where(at == 0, 0.0, jnp.where(at == count - 1, 0.0, 1.0)).astype(F32)


def store_pieces(outs, at, values):
    rows = BS // len(outs)
    me = lax.axis_index("col")
    for s, out in enumerate(outs):
        start = pl.multiple_of((me ^ s) * rows, rows)
        for t in range(values.shape[0]):
            first = (at + t) * rows
            out[first : first + rows, :] = values[t, pl.ds(start, rows), :].astype(BF16)


def near_kernel(parts, bits, r, prolong, col_a, col_b, *rest):
    outs, (columns, column_head, slots, right) = rest[:-4], rest[-4:]
    fx, fy = flips()

    def by_halves(quads, own, first):
        for j, (_, parts_of, bit) in enumerate(quads):
            for m, rows in enumerate(parts_of):
                step = rows.shape[0]
                at = QUAD * j + step * m
                high = rows * bit.astype(BF16)
                right[at : at + step, 0:BS] = rows - high
                right[at : at + step, BS:] = high
        names = [q for q, _, _ in quads]
        for i, k in enumerate(own):
            value = jnp.dot(sums(r, OWN[k], names), right[0 : QUAD * len(quads), :], preferred_element_type=F32)
            for b in range(2):
                one = value[:, b * BS : (b + 1) * BS]
                high = bits[k : k + 1, :] * one
                low = one - high
                if i == 0:
                    slots[first + b] = low
                    slots[first + 2 + b] = high
                else:
                    slots[first + b] += low
                    slots[first + 2 + b] += high

    quads = []
    for j, (u, v) in enumerate(OWN):
        ur, vr = turned(u - 1, fx), turned(v - 1, fy)
        at = pl.ds(pl.multiple_of(vr * 256, 256), 256)
        quads.append(((u, v), [prolong[2 * ur + m, at, :] for m in range(2)], bits[j : j + 1, :]))
    by_halves(quads, range(4), 0)
    split_y = jnp.abs(bits[0:1, :] - bits[1:2, :])
    for e, (far, own, side, scale) in enumerate(((col_a, 2, 3, None), (col_b, 1, 0, inside("col", parts)))):
        near = [sums(r, (u, own), ((1, side), (2, side))) for u in (1, 2)]
        base, extra = edge_slots(near, far, split_y)
        for t in range(2):
            slots[4 + 2 * e + t] = base[t] if scale is None else base[t] * scale
            columns[2 * e + t] = extra[t] if scale is None else extra[t] * scale
            column_head[2 * e + t : 2 * e + t + 1, :] = half_of(far, t)
    column_head[4:8, :] = bits[0:4, :]
    rows = BS // parts
    me = lax.axis_index("col")
    for s in range(parts):
        start = pl.multiple_of((me ^ s) * rows, rows)
        out = outs[s] if s < 2 else outs[s // 2 + 1]
        for t in range(OWN_SLOTS):
            value = slots[t, pl.ds(start, rows), :].astype(BF16)
            if s < 2:
                out[t] = value
            else:
                out[s % 2, t] = value


def near_terms(parts, *operands):
    rows = BS // parts
    one = jax.ShapeDtypeStruct((OWN_SLOTS, rows, BS), BF16)
    two = jax.ShapeDtypeStruct((2, OWN_SLOTS, rows, BS), BF16)
    shapes = (one, one) + (two,) * (parts // 2 - 1)
    shapes += (jax.ShapeDtypeStruct((4, BS, BS), F32), jax.ShapeDtypeStruct((8, BS), F32))
    return pl.pallas_call(
        functools.partial(near_kernel, parts),
        out_shape=shapes,
        in_specs=[VMEM] * len(operands),
        out_specs=(VMEM,) * len(shapes),
        scratch_shapes=[pltpu.VMEM((OWN_SLOTS, BS, BS), F32), pltpu.VMEM((4 * QUAD, 2 * BS), BF16)],
        compiler_params=pltpu.CompilerParams(vmem_limit_bytes=16 << 20),
        cost_estimate=pl.CostEstimate(flops=1, bytes_accessed=1, transcendentals=0),
        name="near_terms",
    )(*operands)


def fill_edges(r, edges, slots, head):
    for e, (far, own, quads, same_a, scale) in enumerate(edges):
        base, extra = edge_slots([sums(r, p, quads) for p in own], far, same_a)
        for t in range(2):
            slots[2 * e + t] = base[t] if scale is None else base[t] * scale
            slots[4 + 2 * e + t] = extra[t] if scale is None else extra[t] * scale
            head[2 * e + t : 2 * e + t + 1, :] = half_of(far, t)


def far_kernel(counts, bits, r, row_a, row_b, from_a, from_b, columns, column_head, *rest):
    outs, (slots, head) = rest[:-2], rest[-2:]
    split_x = 1.0 - jnp.abs(bits[0:1, :] - bits[1:2, :])
    row_in, col_in = inside("row", counts[0]), inside("col", counts[1])
    head[...] = jnp.zeros_like(head)
    head[0:4, :] = bits[0:4, :]
    head[8:12, :] = column_head[0:4, :]
    edges = (
        (row_a, ((2, 1), (2, 2)), ((3, 1), (3, 2)), split_x, None),
        (row_b, ((1, 1), (1, 2)), ((0, 1), (0, 2)), split_x, row_in),
    )
    fill_edges(r, edges, slots, head.at[4:8])
    for t in range(4):
        slots[4 + t] += columns[t]
    corners = (
        (from_a.at[0], quad_of(row_a, 1), None),
        (from_b.at[0], quad_of(row_a, 0), col_in),
        (from_a.at[1], quad_of(row_b, 1), row_in),
        (from_b.at[1], quad_of(row_b, 0), row_in * col_in),
    )
    for e, (near, far, scale) in enumerate(corners):
        value = jnp.dot(near[...], far, preferred_element_type=F32)
        slots[8 + e] = value if scale is None else value * scale
    store_pieces(outs, 0, slots.at[0:4])
    store_pieces(outs, 4, slots.at[8:12])
    store_pieces(outs, 8, slots.at[4:8])
    for out in outs:
        out[out.shape[0] - BITS :, :] = head[...].astype(BF16)


def far_terms(counts, *operands):
    parts = counts[1]
    message = jax.ShapeDtypeStruct((SLOTS * (BS // parts) + BITS, BS), BF16)
    return pl.pallas_call(
        functools.partial(far_kernel, counts),
        out_shape=(message,) * parts,
        in_specs=[VMEM] * len(operands),
        out_specs=(VMEM,) * parts,
        scratch_shapes=[pltpu.VMEM((12, BS, BS), F32), pltpu.VMEM((BITS, BS), F32)],
        compiler_params=pltpu.CompilerParams(vmem_limit_bytes=16 << 20),
        cost_estimate=pl.CostEstimate(flops=1, bytes_accessed=1, transcendentals=0),
        name="far_terms",
    )(*operands)


def unpack_kernel(parts, steps, *refs):
    ins, owns = refs[: len(steps)], refs[len(steps) : 2 * len(steps)]
    out, buf, sems = refs[-3:]
    me = lax.axis_index("col")
    fx, _ = flips()
    copies = []
    for i, (s, ref) in enumerate(zip(steps, ins)):
        square = me ^ s
        fy = lax.rem(square, 2)
        own = owns[i] if s < 2 else owns[i].at[s // 2 - 1 if s % 2 else 0]
        for a in range(2):
            copies.append(
                pltpu.make_async_copy(own.at[2 * a : 2 * a + 2], out.at[square, a, 4], sems.at[len(copies)])
            )
            copies[-1].start()
        one = functools.partial(bit_row, ref)
        split_y = jnp.abs(one(0) - one(1))

        def send(piece, owner, code):
            copies.append(pltpu.make_async_copy(buf.at[i, piece], out.at[owner, :, code], sems.at[len(copies)]))
            copies[-1].start()

        split_x = 1.0 - split_y
        edges = (
            ((2, 3), (8, 9), split_y, 7 - 6 * fx),
            ((0, 1), (10, 11), split_y, 1 + 6 * fx),
            ((1, 3), (8, 9), split_x, 3 + turn3(2, fy)),
            ((0, 2), (10, 11), split_x, 3 + turn3(0, fy)),
        )
        for e, (ps, more, used, code) in enumerate(edges):
            if e < 2:
                values = [slot(ref, 2 * e + t) for t in range(2)]
            else:
                values = [own[2 * e + t].astype(F32) for t in range(2)]
            second = [slot(ref, t) for t in more]
            spread_edge(buf, (i, e), one, ps, (4 + 2 * e, 5 + 2 * e), values, second, used)
            send(e, square, code)
        high = square ^ 1
        low = square + 2 * fy - 1
        low = jnp.where((low < 0) | (low >= parts), square, low)
        corners = (
            (high, 6 - 6 * fx, 2, 9, 5),
            (low, 6 - 6 * fx, 0, 11, 4),
            (high, 6 * fx, 2, 8, 7),
            (low, 6 * fx, 0, 10, 6),
        )
        for e, (owner, group, side, a_bit, b_bit) in enumerate(corners):
            spread_corner(buf, (i, 4 + e), slot(ref, 4 + e), one(a_bit), one(b_bit))
            send(4 + e, owner, group + turn3(side, lax.rem(owner, 2)))
    for copy in copies:
        copy.wait()


def unpack(messages, owns, steps, coarse):
    parts = lax.axis_size("col")
    rows = BS // parts
    fresh = coarse is None
    return pl.pallas_call(
        functools.partial(unpack_kernel, parts, steps),
        out_shape=jax.ShapeDtypeStruct((parts, 2, 9, 2, rows, BS), BF16),
        in_specs=[VMEM] * (2 * len(steps)) + [ANY] * (not fresh),
        out_specs=ANY,
        scratch_shapes=[
            pltpu.VMEM((len(steps), 8, 2, 2, rows, BS), BF16),
            pltpu.SemaphoreType.DMA((10 * len(steps),)),
        ],
        input_output_aliases={} if fresh else {2 * len(steps): 0},
        compiler_params=pltpu.CompilerParams(vmem_limit_bytes=16 << 20),
        cost_estimate=pl.CostEstimate(flops=1, bytes_accessed=1, transcendentals=0),
        name="unpack",
    )(*messages, *owns, *(() if fresh else (coarse,)))


def turn3(index, flip):
    return index + flip * (2 - 2 * index)


def bit_row(ref, k):
    at = ref.shape[0] - BITS + k
    return ref[at : at + 1, :].astype(F32)


def slot(ref, t):
    rows = (ref.shape[0] - BITS) // SLOTS
    return ref[t * rows : (t + 1) * rows, :].astype(F32)


def spread(buf, at, center):
    i, piece = at
    for a in range(2):
        for b in range(2):
            buf[i, piece, a, b] = center[2 * a + b].astype(BF16)


def spread_edge(buf, at, one, ps, qs, values, more, used):
    a_bits = [one(p) for p in ps]
    b_bits = [one(q) for q in qs]
    center = [None] * 4
    for b in range(2):
        picks = [bit if b else 1.0 - bit for bit in b_bits]
        first = picks[0] * values[0] + picks[1] * values[1]
        second = (used * picks[0]) * more[0] + (used * picks[1]) * more[1]
        for a in range(2):
            ia = [bit if a else 1.0 - bit for bit in a_bits]
            center[2 * a + b] = ia[0] * first + ia[1] * second
    spread(buf, at, center)


def spread_corner(buf, at, value, a_bit, b_bit):
    center = []
    for a in range(2):
        for b in range(2):
            center.append(((a_bit if a else 1.0 - a_bit) * (b_bit if b else 1.0 - b_bit)) * value)
    spread(buf, at, center)


def gate_kernel(*refs):
    pass


def gate(values, after):
    count = len(values)
    return pl.pallas_call(
        gate_kernel,
        out_shape=tuple(jax.ShapeDtypeStruct(v.shape, v.dtype) for v in values),
        in_specs=[ANY] * (count + len(after)),
        out_specs=(ANY,) * count,
        input_output_aliases={i: i for i in range(count)},
        compiler_params=pltpu.CompilerParams(vmem_limit_bytes=1 << 20),
        cost_estimate=pl.CostEstimate(flops=1 << 33, bytes_accessed=1, transcendentals=0),
        name="gate",
    )(*values, *after)


def other_side(index):
    return index + 1 if index % 2 else index - 1


def row_low(r, c, rows, cols):
    far = other_side(r)
    return (far, c) if 0 <= far < rows else (r, c ^ 1)


def col_low(r, c, rows, cols):
    far = other_side(c)
    if 0 <= far < cols:
        return r, far
    if r % 2:
        return (r - 2 if r >= 2 else r - 1), c
    return (r + 2 if r + 2 < rows else r + 1), c


def row_high(r, c, rows, cols):
    return r ^ 1, c


def col_high(r, c, rows, cols):
    return r, c ^ 1


def swap(value, partner):
    rows, cols = lax.axis_size("row"), lax.axis_size("col")
    pairs = []
    for r in range(rows):
        for c in range(cols):
            to_r, to_c = partner(r, c, rows, cols)
            pairs.append((r * cols + c, to_r * cols + to_c))
    return lax.ppermute(value, ("row", "col"), pairs)


def xor_swap(value, s):
    return lax.ppermute(value, "col", [(i, i ^ s) for i in range(lax.axis_size("col"))])


def local(coupling, neighbours, prolong, aggregate):
    parts = lax.axis_size("col")
    counts = (lax.axis_size("row"), parts)
    coupling = pltpu.with_memory_space_constraint(coupling.reshape(-1, BS, BS), pltpu.HBM)
    neighbours = pltpu.with_memory_space_constraint(neighbours, pltpu.HBM)
    aggregate = pltpu.with_memory_space_constraint(aggregate, pltpu.HBM)
    prolong_rows = pltpu.with_memory_space_constraint(prolong.reshape(SIDE, SIDE * BS, BS), pltpu.HBM)
    to_row_a, to_row_b, bits = rims(aggregate, prolong_rows)
    to_col_a, to_col_b = column_rims(to_row_a, to_row_b, bits)
    row_a = swap(to_row_a, row_high)
    row_b = swap(to_row_b, row_low)
    col_a = swap(to_col_a, col_high)
    col_b = swap(to_col_b, col_low)
    r, to_a, to_b, own_blocks = step_one(neighbours, coupling, prolong_rows, to_col_b)
    from_b = swap(to_b, col_low)
    from_a = swap(to_a, col_high)
    mine, pair, *cross, columns, column_head = near_terms(parts, bits, r, own_blocks, col_a, col_b)
    direct = [xor_swap(value, 2 * h + 2) for h, value in enumerate(cross)]
    row_a, row_b, columns, from_b = gate((row_a, row_b, columns, from_b), (mine,))
    outs = list(far_terms(counts, bits, r, row_a, row_b, from_a, from_b, columns, column_head))
    outs[0], pair, *direct = lax.optimization_barrier((outs[0], pair, *direct))
    outs = [outs[0]] + [xor_swap(outs[s], s) for s in range(1, parts)]
    pair = xor_swap(pair, 1)
    relayed = xor_swap(jnp.concatenate([value[1:2] for value in direct]), 1)
    owns = [mine, pair]
    for value in direct:
        owns += [value, relayed]
    coarse = None
    for first, last in ((0, 2), (2, parts - 1), (parts - 1, parts)):
        coarse = unpack(outs[first:last], owns[first:last], range(first, last), coarse)
    return coarse[None]


def solution(mesh):
    return jax.shard_map(
        local,
        mesh=mesh,
        in_specs=(
            P("row", "col", None, None, None),
            P("row", "col", None),
            P("row", "col", None, None),
            P("row", "col"),
        ),
        out_specs=P("row", None, None, None, None, "col", None),
        check_vma=False,
    )
```

```python
import functools

import jax
import jax.numpy as jnp
from jax import lax
from jax.experimental import pallas as pl
from jax.experimental.pallas import tpu as pltpu
from jax.sharding import PartitionSpec as P

BS = 128
KA = 12
SIDE = 4
QUAD = 4 * BS
HEAD = 8
ROWS = 2 * QUAD + HEAD
BITS = 16
OWN_SLOTS = 8
SLOTS = 12
ANY = pl.BlockSpec(memory_space=pl.ANY)
VMEM = pl.BlockSpec(memory_space=pltpu.VMEM)
HBM = pl.BlockSpec(memory_space=pltpu.HBM)
BF16 = jnp.bfloat16
F32 = jnp.float32


def flips():
    return lax.rem(lax.axis_index("row"), 2), lax.rem(lax.axis_index("col"), 2)


def turned(index, flip):
    return index + flip - 2 * index * flip


def rims_kernel(agg_hbm, prolong, row_a, row_b, bits, agg, sems):
    fx, fy = flips()
    load = pltpu.make_async_copy(agg_hbm, agg, sems.at[8])
    load.start()
    copies = []
    plans = (
        (row_a, ((1, 0), (1, 1))),
        (row_b, ((0, 0), (0, 1))),
    )
    for out, quads in plans:
        for h, (u, v) in enumerate(quads):
            ur, vr = turned(u, fx), turned(v, fy)
            for m in range(2):
                copies.append(
                    pltpu.make_async_copy(
                        prolong.at[2 * ur + m, pl.ds(pl.multiple_of(vr * 256, 256), 256), :],
                        out.at[QUAD * h + 256 * m : QUAD * h + 256 * (m + 1), :],
                        sems.at[len(copies)],
                    )
                )
                copies[-1].start()
    load.wait()
    own = {}
    for k, (u, v) in enumerate(((0, 0), (0, 1), (1, 0), (1, 1))):
        own[u, v] = lax.rem(agg[2 * turned(u, fx), 2 * turned(v, fy)], 2).astype(F32)
        bits[k : k + 1, :] = jnp.full((1, BS), own[u, v], F32)
    bits[4:, :] = jnp.zeros((4, BS), F32)
    for out, quads in plans:
        at = lax.broadcasted_iota(jnp.int32, (HEAD, BS), 0)
        out[2 * QUAD :, :] = jnp.where(at == 0, own[quads[0]], own[quads[1]]).astype(BF16)
    for copy in copies:
        copy.wait()


def rims(agg, prolong_rows):
    shape = jax.ShapeDtypeStruct((ROWS, BS), BF16)
    return pl.pallas_call(
        rims_kernel,
        out_shape=(shape,) * 2 + (jax.ShapeDtypeStruct((8, BS), F32),),
        in_specs=[HBM, HBM],
        out_specs=(VMEM,) * 3,
        scratch_shapes=[pltpu.SMEM((SIDE, SIDE), jnp.int32), pltpu.SemaphoreType.DMA((9,))],
        compiler_params=pltpu.CompilerParams(vmem_limit_bytes=4 << 20),
        name="rims",
    )(agg, prolong_rows)


def column_rims_kernel(row_a, row_b, bits, col_a, col_b):
    at = lax.broadcasted_iota(jnp.int32, (HEAD, BS), 0)
    for v, out in ((1, col_a), (0, col_b)):
        for h, rows in enumerate((row_b, row_a)):
            out[QUAD * h : QUAD * (h + 1), :] = rows[QUAD * v : QUAD * (v + 1), :]
        out[2 * QUAD :, :] = jnp.where(at == 0, bits[v : v + 1, :], bits[2 + v : 3 + v, :]).astype(BF16)


def column_rims(row_a, row_b, bits):
    shape = jax.ShapeDtypeStruct((ROWS, BS), BF16)
    return pl.pallas_call(
        column_rims_kernel,
        out_shape=(shape,) * 2,
        in_specs=[VMEM] * 3,
        out_specs=(VMEM,) * 2,
        compiler_params=pltpu.CompilerParams(vmem_limit_bytes=4 << 20),
        cost_estimate=pl.CostEstimate(flops=1, bytes_accessed=1, transcendentals=0),
        name="column_rims",
    )(row_a, row_b, bits)


def sums(r, p, quads):
    fx, fy = flips()
    raw = 2 * turned(p[0] - 1, fx) + turned(p[1] - 1, fy)
    blocks = [r[raw, (u - p[0] + 1) * 3 + v - p[1] + 1] for u, v in quads]
    return blocks[0] if len(blocks) == 1 else jnp.concatenate(blocks, axis=1)


OWN = ((1, 1), (1, 2), (2, 1), (2, 2))
NONE = 16 * KA


def step_one_kernel(
    codes_hbm, coupling, prolong_hbm, after, out, to_a, to_b, prolong, blocks, codes, slot_of, sems
):
    fx, fy = flips()
    load_codes = pltpu.make_async_copy(codes_hbm, codes, sems.at[8])
    load_codes.start()
    load_prolong = pltpu.make_async_copy(prolong_hbm, prolong, sems.at[9])
    load_prolong.start()

    def load(quad, m):
        first = (2 * (quad // 2) + m) * SIDE + 2 * (quad % 2)
        at = pl.ds(first * KA, 2 * KA)
        return pltpu.make_async_copy(coupling.at[at], blocks.at[at], sems.at[2 * quad + m])

    def start(quad):
        for m in range(2):
            load(quad, m).start()

    start(0)
    blocks[NONE] = jnp.zeros((BS, BS), BF16)

    @pl.loop(0, 16)
    def _(n):
        for t in range(25):
            slot_of[n * 25 + t] = NONE

    start(1)
    load_codes.wait()

    @pl.loop(0, 16)
    def _(n):
        for k in range(KA):
            slot_of[n * 25 + codes[n // SIDE, n % SIDE, k]] = n * KA + k

    start(2)
    load_prolong.wait()
    zero = jnp.zeros((BS, BS), BF16)

    @pl.loop(0, 4)
    def _(quad):
        qx, qy = quad // 2, quad % 2
        for m in range(2):
            load(quad, m).wait()

        @pl.when(quad == 0)
        def _():
            start(3)

        left = []
        for ix in range(2):
            rows = prolong[2 * qx + ix, pl.ds(pl.multiple_of(qy * 256, 256), 256), :]
            left.append(rows.T)

        def block(ix, iy, jx, jy):
            if not (0 <= jy - iy <= 4):
                return zero
            n = (2 * qx + ix) * SIDE + 2 * qy + iy
            return blocks[slot_of[n * 25 + (jx - ix) * 5 + jy - iy]]

        for jx in range(6):
            for t in range(3):
                total = None
                for ix in range(2):
                    if not (0 <= jx - ix <= 4):
                        continue
                    right = jnp.concatenate(
                        [
                            jnp.concatenate([block(ix, iy, jx, 2 * t + e) for e in range(2)], axis=1)
                            for iy in range(2)
                        ],
                        axis=0,
                    )
                    part = jnp.dot(left[ix], right, preferred_element_type=F32)
                    total = part if total is None else total + part
                du, dv = jx // 2, t
                at = (du + fx * (2 - 2 * du)) * 3 + dv + fy * (2 - 2 * dv)
                out[quad, at, :, (jx % 2) * 256 : (jx % 2 + 1) * 256] = total.astype(BF16)

    for ref, e, p, q in (
        (to_b, 0, (2, 1), (3, 0)),
        (to_b, 1, (1, 1), (0, 0)),
        (to_a, 0, (2, 2), (3, 3)),
        (to_a, 1, (1, 2), (0, 3)),
    ):
        ref[e] = sums(out, p, (q,))


def step_one(codes, coupling, prolong_rows, after):
    corner = jax.ShapeDtypeStruct((2, BS, QUAD), BF16)
    return pl.pallas_call(
        step_one_kernel,
        out_shape=(
            jax.ShapeDtypeStruct((4, 9, BS, QUAD), BF16),
            corner,
            corner,
            jax.ShapeDtypeStruct(prolong_rows.shape, BF16),
        ),
        in_specs=[HBM] * 3 + [ANY],
        out_specs=(VMEM,) * 4,
        scratch_shapes=[
            pltpu.VMEM((NONE + 1, BS, BS), BF16),
            pltpu.SMEM((SIDE, SIDE, KA), jnp.int32),
            pltpu.SMEM((400,), jnp.int32),
            pltpu.SemaphoreType.DMA((10,)),
        ],
        compiler_params=pltpu.CompilerParams(vmem_limit_bytes=16 << 20),
        cost_estimate=pl.CostEstimate(flops=1 << 33, bytes_accessed=1 << 20, transcendentals=0),
        name="step_one",
    )(codes, coupling, prolong_rows, after)


def half_of(ref, h):
    return ref[2 * QUAD + h : 2 * QUAD + h + 1, :].astype(F32)


def quad_of(ref, h):
    return ref[QUAD * h : QUAD * (h + 1), :]


def edge_slots(near, far, same_a):
    same_b = 1.0 - jnp.abs(half_of(far, 0) - half_of(far, 1))
    second = quad_of(far, 1)
    shared = second * same_b.astype(BF16)
    right = jnp.concatenate(
        [
            jnp.concatenate([quad_of(far, 0), jnp.zeros_like(second)], axis=1),
            jnp.concatenate([shared, second - shared], axis=1),
        ],
        axis=0,
    )
    by_p = [jnp.dot(rows, right, preferred_element_type=F32) for rows in near]
    base, extra = [], []
    for v in range(2):
        one, two = (value[:, v * BS : (v + 1) * BS] for value in by_p)
        shared = same_a * two
        base.append(one + shared)
        extra.append(two - shared)
    return base, extra


def inside(axis, count):
    at = lax.axis_index(axis)
    return jnp.where(at == 0, 0.0, jnp.where(at == count - 1, 0.0, 1.0)).astype(F32)


def store_pieces(outs, at, values):
    rows = BS // len(outs)
    me = lax.axis_index("col")
    for s, out in enumerate(outs):
        start = pl.multiple_of((me ^ s) * rows, rows)
        for t in range(values.shape[0]):
            first = (at + t) * rows
            out[first : first + rows, :] = values[t, pl.ds(start, rows), :].astype(BF16)


def near_kernel(parts, bits, r, prolong, col_a, col_b, *rest):
    outs, (columns, column_head, slots, right) = rest[:-4], rest[-4:]
    fx, fy = flips()

    def by_halves(quads, own, first):
        for j, (_, parts_of, bit) in enumerate(quads):
            for m, rows in enumerate(parts_of):
                step = rows.shape[0]
                at = QUAD * j + step * m
                high = rows * bit.astype(BF16)
                right[at : at + step, 0:BS] = rows - high
                right[at : at + step, BS:] = high
        names = [q for q, _, _ in quads]
        for i, k in enumerate(own):
            value = jnp.dot(sums(r, OWN[k], names), right[0 : QUAD * len(quads), :], preferred_element_type=F32)
            for b in range(2):
                one = value[:, b * BS : (b + 1) * BS]
                high = bits[k : k + 1, :] * one
                low = one - high
                if i == 0:
                    slots[first + b] = low
                    slots[first + 2 + b] = high
                else:
                    slots[first + b] += low
                    slots[first + 2 + b] += high

    quads = []
    for j, (u, v) in enumerate(OWN):
        ur, vr = turned(u - 1, fx), turned(v - 1, fy)
        at = pl.ds(pl.multiple_of(vr * 256, 256), 256)
        quads.append(((u, v), [prolong[2 * ur + m, at, :] for m in range(2)], bits[j : j + 1, :]))
    by_halves(quads, range(4), 0)
    split_y = jnp.abs(bits[0:1, :] - bits[1:2, :])
    for e, (far, own, side, scale) in enumerate(((col_a, 2, 3, None), (col_b, 1, 0, inside("col", parts)))):
        near = [sums(r, (u, own), ((1, side), (2, side))) for u in (1, 2)]
        base, extra = edge_slots(near, far, split_y)
        for t in range(2):
            slots[4 + 2 * e + t] = base[t] if scale is None else base[t] * scale
            columns[2 * e + t] = extra[t] if scale is None else extra[t] * scale
            column_head[2 * e + t : 2 * e + t + 1, :] = half_of(far, t)
    column_head[4:8, :] = bits[0:4, :]
    rows = BS // parts
    me = lax.axis_index("col")
    for s in range(parts):
        start = pl.multiple_of((me ^ s) * rows, rows)
        out = outs[s] if s < 2 else outs[s // 2 + 1]
        for t in range(OWN_SLOTS):
            value = slots[t, pl.ds(start, rows), :].astype(BF16)
            if s < 2:
                out[t] = value
            else:
                out[s % 2, t] = value


def near_terms(parts, *operands):
    rows = BS // parts
    one = jax.ShapeDtypeStruct((OWN_SLOTS, rows, BS), BF16)
    two = jax.ShapeDtypeStruct((2, OWN_SLOTS, rows, BS), BF16)
    shapes = (one, one) + (two,) * (parts // 2 - 1)
    shapes += (jax.ShapeDtypeStruct((4, BS, BS), F32), jax.ShapeDtypeStruct((8, BS), F32))
    return pl.pallas_call(
        functools.partial(near_kernel, parts),
        out_shape=shapes,
        in_specs=[VMEM] * len(operands),
        out_specs=(VMEM,) * len(shapes),
        scratch_shapes=[pltpu.VMEM((OWN_SLOTS, BS, BS), F32), pltpu.VMEM((4 * QUAD, 2 * BS), BF16)],
        compiler_params=pltpu.CompilerParams(vmem_limit_bytes=16 << 20),
        cost_estimate=pl.CostEstimate(flops=1, bytes_accessed=1, transcendentals=0),
        name="near_terms",
    )(*operands)


def fill_edges(r, edges, slots, head):
    for e, (far, own, quads, same_a, scale) in enumerate(edges):
        base, extra = edge_slots([sums(r, p, quads) for p in own], far, same_a)
        for t in range(2):
            slots[2 * e + t] = base[t] if scale is None else base[t] * scale
            slots[4 + 2 * e + t] = extra[t] if scale is None else extra[t] * scale
            head[2 * e + t : 2 * e + t + 1, :] = half_of(far, t)


def far_kernel(counts, bits, r, row_a, row_b, from_a, from_b, columns, column_head, *rest):
    outs, (slots, head) = rest[:-2], rest[-2:]
    split_x = 1.0 - jnp.abs(bits[0:1, :] - bits[1:2, :])
    row_in, col_in = inside("row", counts[0]), inside("col", counts[1])
    head[...] = jnp.zeros_like(head)
    head[0:4, :] = bits[0:4, :]
    head[8:12, :] = column_head[0:4, :]
    edges = (
        (row_a, ((2, 1), (2, 2)), ((3, 1), (3, 2)), split_x, None),
        (row_b, ((1, 1), (1, 2)), ((0, 1), (0, 2)), split_x, row_in),
    )
    fill_edges(r, edges, slots, head.at[4:8])
    for t in range(4):
        slots[4 + t] += columns[t]
    corners = (
        (from_a.at[0], quad_of(row_a, 1), None),
        (from_b.at[0], quad_of(row_a, 0), col_in),
        (from_a.at[1], quad_of(row_b, 1), row_in),
        (from_b.at[1], quad_of(row_b, 0), row_in * col_in),
    )
    for e, (near, far, scale) in enumerate(corners):
        value = jnp.dot(near[...], far, preferred_element_type=F32)
        slots[8 + e] = value if scale is None else value * scale
    store_pieces(outs, 0, slots.at[0:4])
    store_pieces(outs, 4, slots.at[8:12])
    store_pieces(outs, 8, slots.at[4:8])
    for out in outs:
        out[out.shape[0] - BITS :, :] = head[...].astype(BF16)


def far_terms(counts, *operands):
    parts = counts[1]
    message = jax.ShapeDtypeStruct((SLOTS * (BS // parts) + BITS, BS), BF16)
    return pl.pallas_call(
        functools.partial(far_kernel, counts),
        out_shape=(message,) * parts,
        in_specs=[VMEM] * len(operands),
        out_specs=(VMEM,) * parts,
        scratch_shapes=[pltpu.VMEM((12, BS, BS), F32), pltpu.VMEM((BITS, BS), F32)],
        compiler_params=pltpu.CompilerParams(vmem_limit_bytes=16 << 20),
        cost_estimate=pl.CostEstimate(flops=1, bytes_accessed=1, transcendentals=0),
        name="far_terms",
    )(*operands)


def unpack_kernel(parts, steps, *refs):
    ins, owns = refs[: len(steps)], refs[len(steps) : 2 * len(steps)]
    out, buf, sems = refs[-3:]
    me = lax.axis_index("col")
    fx, _ = flips()
    copies = []
    for i, (s, ref) in enumerate(zip(steps, ins)):
        square = me ^ s
        fy = lax.rem(square, 2)
        own = owns[i] if s < 2 else owns[i].at[s // 2 - 1 if s % 2 else 0]
        for a in range(2):
            copies.append(
                pltpu.make_async_copy(own.at[2 * a : 2 * a + 2], out.at[square, a, 4], sems.at[len(copies)])
            )
            copies[-1].start()
        one = functools.partial(bit_row, ref)
        split_y = jnp.abs(one(0) - one(1))

        def send(piece, owner, code):
            copies.append(pltpu.make_async_copy(buf.at[i, piece], out.at[owner, :, code], sems.at[len(copies)]))
            copies[-1].start()

        split_x = 1.0 - split_y
        edges = (
            ((2, 3), (8, 9), split_y, 7 - 6 * fx),
            ((0, 1), (10, 11), split_y, 1 + 6 * fx),
            ((1, 3), (8, 9), split_x, 3 + turn3(2, fy)),
            ((0, 2), (10, 11), split_x, 3 + turn3(0, fy)),
        )
        for e, (ps, more, used, code) in enumerate(edges):
            if e < 2:
                values = [slot(ref, 2 * e + t) for t in range(2)]
            else:
                values = [own[2 * e + t].astype(F32) for t in range(2)]
            second = [slot(ref, t) for t in more]
            spread_edge(buf, (i, e), one, ps, (4 + 2 * e, 5 + 2 * e), values, second, used)
            send(e, square, code)
        high = square ^ 1
        low = square + 2 * fy - 1
        low = jnp.where((low < 0) | (low >= parts), square, low)
        corners = (
            (high, 6 - 6 * fx, 2, 9, 5),
            (low, 6 - 6 * fx, 0, 11, 4),
            (high, 6 * fx, 2, 8, 7),
            (low, 6 * fx, 0, 10, 6),
        )
        for e, (owner, group, side, a_bit, b_bit) in enumerate(corners):
            spread_corner(buf, (i, 4 + e), slot(ref, 4 + e), one(a_bit), one(b_bit))
            send(4 + e, owner, group + turn3(side, lax.rem(owner, 2)))
    for copy in copies:
        copy.wait()


def unpack(messages, owns, steps, coarse):
    parts = lax.axis_size("col")
    rows = BS // parts
    fresh = coarse is None
    return pl.pallas_call(
        functools.partial(unpack_kernel, parts, steps),
        out_shape=jax.ShapeDtypeStruct((parts, 2, 9, 2, rows, BS), BF16),
        in_specs=[VMEM] * (2 * len(steps)) + [ANY] * (not fresh),
        out_specs=ANY,
        scratch_shapes=[
            pltpu.VMEM((len(steps), 8, 2, 2, rows, BS), BF16),
            pltpu.SemaphoreType.DMA((10 * len(steps),)),
        ],
        input_output_aliases={} if fresh else {2 * len(steps): 0},
        compiler_params=pltpu.CompilerParams(vmem_limit_bytes=16 << 20),
        cost_estimate=pl.CostEstimate(flops=1, bytes_accessed=1, transcendentals=0),
        name="unpack",
    )(*messages, *owns, *(() if fresh else (coarse,)))


def turn3(index, flip):
    return index + flip * (2 - 2 * index)


def bit_row(ref, k):
    at = ref.shape[0] - BITS + k
    return ref[at : at + 1, :].astype(F32)


def slot(ref, t):
    rows = (ref.shape[0] - BITS) // SLOTS
    return ref[t * rows : (t + 1) * rows, :].astype(F32)


def spread(buf, at, center):
    i, piece = at
    for a in range(2):
        for b in range(2):
            buf[i, piece, a, b] = center[2 * a + b].astype(BF16)


def spread_edge(buf, at, one, ps, qs, values, more, used):
    a_bits = [one(p) for p in ps]
    b_bits = [one(q) for q in qs]
    center = [None] * 4
    for b in range(2):
        picks = [bit if b else 1.0 - bit for bit in b_bits]
        first = picks[0] * values[0] + picks[1] * values[1]
        second = (used * picks[0]) * more[0] + (used * picks[1]) * more[1]
        for a in range(2):
            ia = [bit if a else 1.0 - bit for bit in a_bits]
            center[2 * a + b] = ia[0] * first + ia[1] * second
    spread(buf, at, center)


def spread_corner(buf, at, value, a_bit, b_bit):
    center = []
    for a in range(2):
        for b in range(2):
            center.append(((a_bit if a else 1.0 - a_bit) * (b_bit if b else 1.0 - b_bit)) * value)
    spread(buf, at, center)


def gate_kernel(*refs):
    pass


def gate(values, after):
    count = len(values)
    return pl.pallas_call(
        gate_kernel,
        out_shape=tuple(jax.ShapeDtypeStruct(v.shape, v.dtype) for v in values),
        in_specs=[ANY] * (count + len(after)),
        out_specs=(ANY,) * count,
        input_output_aliases={i: i for i in range(count)},
        compiler_params=pltpu.CompilerParams(vmem_limit_bytes=1 << 20),
        cost_estimate=pl.CostEstimate(flops=1 << 33, bytes_accessed=1, transcendentals=0),
        name="gate",
    )(*values, *after)


def other_side(index):
    return index + 1 if index % 2 else index - 1


def row_low(r, c, rows, cols):
    far = other_side(r)
    return (far, c) if 0 <= far < rows else (r, c ^ 1)


def col_low(r, c, rows, cols):
    far = other_side(c)
    if 0 <= far < cols:
        return r, far
    if r % 2:
        return (r - 2 if r >= 2 else r - 1), c
    return (r + 2 if r + 2 < rows else r + 1), c


def row_high(r, c, rows, cols):
    return r ^ 1, c


def col_high(r, c, rows, cols):
    return r, c ^ 1


def swap(value, partner):
    rows, cols = lax.axis_size("row"), lax.axis_size("col")
    pairs = []
    for r in range(rows):
        for c in range(cols):
            to_r, to_c = partner(r, c, rows, cols)
            pairs.append((r * cols + c, to_r * cols + to_c))
    return lax.ppermute(value, ("row", "col"), pairs)


def xor_swap(value, s):
    return lax.ppermute(value, "col", [(i, i ^ s) for i in range(lax.axis_size("col"))])


def local(coupling, neighbours, prolong, aggregate):
    parts = lax.axis_size("col")
    counts = (lax.axis_size("row"), parts)
    coupling = pltpu.with_memory_space_constraint(coupling.reshape(-1, BS, BS), pltpu.HBM)
    neighbours = pltpu.with_memory_space_constraint(neighbours, pltpu.HBM)
    aggregate = pltpu.with_memory_space_constraint(aggregate, pltpu.HBM)
    prolong_rows = pltpu.with_memory_space_constraint(prolong.reshape(SIDE, SIDE * BS, BS), pltpu.HBM)
    to_row_a, to_row_b, bits = rims(aggregate, prolong_rows)
    to_col_a, to_col_b = column_rims(to_row_a, to_row_b, bits)
    row_a = swap(to_row_a, row_high)
    row_b = swap(to_row_b, row_low)
    col_a = swap(to_col_a, col_high)
    col_b = swap(to_col_b, col_low)
    r, to_a, to_b, own_blocks = step_one(neighbours, coupling, prolong_rows, to_col_b)
    from_b = swap(to_b, col_low)
    from_a = swap(to_a, col_high)
    mine, pair, *cross, columns, column_head = near_terms(parts, bits, r, own_blocks, col_a, col_b)
    direct = [xor_swap(value, 2 * h + 2) for h, value in enumerate(cross)]
    row_a, row_b, columns, from_b = gate((row_a, row_b, columns, from_b), (mine,))
    outs = list(far_terms(counts, bits, r, row_a, row_b, from_a, from_b, columns, column_head))
    outs[0], pair, *direct = lax.optimization_barrier((outs[0], pair, *direct))
    outs = [outs[0]] + [xor_swap(outs[s], s) for s in range(1, parts)]
    pair = xor_swap(pair, 1)
    relayed = xor_swap(jnp.concatenate([value[1:2] for value in direct]), 1)
    owns = [mine, pair]
    for value in direct:
        owns += [value, relayed]
    coarse = None
    for steps in (range(0, parts, 2), range(1, parts, 2)):
        coarse = unpack([outs[t] for t in steps], [owns[t] for t in steps], steps, coarse)
    return coarse[None]


def solution(mesh):
    return jax.shard_map(
        local,
        mesh=mesh,
        in_specs=(
            P("row", "col", None, None, None),
            P("row", "col", None),
            P("row", "col", None, None),
            P("row", "col"),
        ),
        out_specs=P("row", None, None, None, None, "col", None),
        check_vma=False,
    )
```

```python
import functools

import jax
import jax.numpy as jnp
from jax import lax
from jax.experimental import pallas as pl
from jax.experimental.pallas import tpu as pltpu
from jax.sharding import PartitionSpec as P

BS = 128
KA = 12
SIDE = 4
QUAD = 4 * BS
HEAD = 8
ROWS = 2 * QUAD + HEAD
BITS = 16
OWN_SLOTS = 8
SLOTS = 12
ANY = pl.BlockSpec(memory_space=pl.ANY)
VMEM = pl.BlockSpec(memory_space=pltpu.VMEM)
HBM = pl.BlockSpec(memory_space=pltpu.HBM)
BF16 = jnp.bfloat16
F32 = jnp.float32


def flips():
    return lax.rem(lax.axis_index("row"), 2), lax.rem(lax.axis_index("col"), 2)


def turned(index, flip):
    return index + flip - 2 * index * flip


def rims_kernel(agg_hbm, prolong, row_a, row_b, bits, agg, sems):
    fx, fy = flips()
    load = pltpu.make_async_copy(agg_hbm, agg, sems.at[8])
    load.start()
    copies = []
    plans = (
        (row_a, ((1, 0), (1, 1))),
        (row_b, ((0, 0), (0, 1))),
    )
    for out, quads in plans:
        for h, (u, v) in enumerate(quads):
            ur, vr = turned(u, fx), turned(v, fy)
            for m in range(2):
                copies.append(
                    pltpu.make_async_copy(
                        prolong.at[2 * ur + m, pl.ds(pl.multiple_of(vr * 256, 256), 256), :],
                        out.at[QUAD * h + 256 * m : QUAD * h + 256 * (m + 1), :],
                        sems.at[len(copies)],
                    )
                )
                copies[-1].start()
    load.wait()
    own = {}
    for k, (u, v) in enumerate(((0, 0), (0, 1), (1, 0), (1, 1))):
        own[u, v] = lax.rem(agg[2 * turned(u, fx), 2 * turned(v, fy)], 2).astype(F32)
        bits[k : k + 1, :] = jnp.full((1, BS), own[u, v], F32)
    bits[4:, :] = jnp.zeros((4, BS), F32)
    for out, quads in plans:
        at = lax.broadcasted_iota(jnp.int32, (HEAD, BS), 0)
        out[2 * QUAD :, :] = jnp.where(at == 0, own[quads[0]], own[quads[1]]).astype(BF16)
    for copy in copies:
        copy.wait()


def rims(agg, prolong_rows):
    shape = jax.ShapeDtypeStruct((ROWS, BS), BF16)
    return pl.pallas_call(
        rims_kernel,
        out_shape=(shape,) * 2 + (jax.ShapeDtypeStruct((8, BS), F32),),
        in_specs=[HBM, HBM],
        out_specs=(VMEM,) * 3,
        scratch_shapes=[pltpu.SMEM((SIDE, SIDE), jnp.int32), pltpu.SemaphoreType.DMA((9,))],
        compiler_params=pltpu.CompilerParams(vmem_limit_bytes=4 << 20),
        name="rims",
    )(agg, prolong_rows)


def column_rims_kernel(row_a, row_b, bits, col_a, col_b):
    at = lax.broadcasted_iota(jnp.int32, (HEAD, BS), 0)
    for v, out in ((1, col_a), (0, col_b)):
        for h, rows in enumerate((row_b, row_a)):
            out[QUAD * h : QUAD * (h + 1), :] = rows[QUAD * v : QUAD * (v + 1), :]
        out[2 * QUAD :, :] = jnp.where(at == 0, bits[v : v + 1, :], bits[2 + v : 3 + v, :]).astype(BF16)


def column_rims(row_a, row_b, bits):
    shape = jax.ShapeDtypeStruct((ROWS, BS), BF16)
    return pl.pallas_call(
        column_rims_kernel,
        out_shape=(shape,) * 2,
        in_specs=[VMEM] * 3,
        out_specs=(VMEM,) * 2,
        compiler_params=pltpu.CompilerParams(vmem_limit_bytes=4 << 20),
        cost_estimate=pl.CostEstimate(flops=1, bytes_accessed=1, transcendentals=0),
        name="column_rims",
    )(row_a, row_b, bits)


def sums(r, p, quads):
    fx, fy = flips()
    raw = 2 * turned(p[0] - 1, fx) + turned(p[1] - 1, fy)
    blocks = [r[raw, (u - p[0] + 1) * 3 + v - p[1] + 1] for u, v in quads]
    return blocks[0] if len(blocks) == 1 else jnp.concatenate(blocks, axis=1)


OWN = ((1, 1), (1, 2), (2, 1), (2, 2))
NONE = 16 * KA


def step_one_kernel(
    codes_hbm, coupling, prolong_hbm, after, out, to_a, to_b, prolong, blocks, codes, slot_of, sems
):
    fx, fy = flips()
    load_codes = pltpu.make_async_copy(codes_hbm, codes, sems.at[8])
    load_codes.start()
    load_prolong = pltpu.make_async_copy(prolong_hbm, prolong, sems.at[9])
    load_prolong.start()

    def load(quad, m):
        first = (2 * (quad // 2) + m) * SIDE + 2 * (quad % 2)
        at = pl.ds(first * KA, 2 * KA)
        return pltpu.make_async_copy(coupling.at[at], blocks.at[at], sems.at[2 * quad + m])

    def start(quad):
        for m in range(2):
            load(quad, m).start()

    start(0)
    blocks[NONE] = jnp.zeros((BS, BS), BF16)

    @pl.loop(0, 16)
    def _(n):
        for t in range(25):
            slot_of[n * 25 + t] = NONE

    start(1)
    load_codes.wait()

    @pl.loop(0, 16)
    def _(n):
        for k in range(KA):
            slot_of[n * 25 + codes[n // SIDE, n % SIDE, k]] = n * KA + k

    start(2)
    load_prolong.wait()
    zero = jnp.zeros((BS, BS), BF16)

    @pl.loop(0, 4)
    def _(quad):
        qx, qy = quad // 2, quad % 2
        for m in range(2):
            load(quad, m).wait()

        @pl.when(quad == 0)
        def _():
            start(3)

        left = []
        for ix in range(2):
            rows = prolong[2 * qx + ix, pl.ds(pl.multiple_of(qy * 256, 256), 256), :]
            left.append(rows.T)

        def block(ix, iy, jx, jy):
            if not (0 <= jy - iy <= 4):
                return zero
            n = (2 * qx + ix) * SIDE + 2 * qy + iy
            return blocks[slot_of[n * 25 + (jx - ix) * 5 + jy - iy]]

        for jx in range(6):
            for t in range(3):
                total = None
                for ix in range(2):
                    if not (0 <= jx - ix <= 4):
                        continue
                    right = jnp.concatenate(
                        [
                            jnp.concatenate([block(ix, iy, jx, 2 * t + e) for e in range(2)], axis=1)
                            for iy in range(2)
                        ],
                        axis=0,
                    )
                    part = jnp.dot(left[ix], right, preferred_element_type=F32)
                    total = part if total is None else total + part
                du, dv = jx // 2, t
                at = (du + fx * (2 - 2 * du)) * 3 + dv + fy * (2 - 2 * dv)
                out[quad, at, :, (jx % 2) * 256 : (jx % 2 + 1) * 256] = total.astype(BF16)

    for ref, e, p, q in (
        (to_b, 0, (2, 1), (3, 0)),
        (to_b, 1, (1, 1), (0, 0)),
        (to_a, 0, (2, 2), (3, 3)),
        (to_a, 1, (1, 2), (0, 3)),
    ):
        ref[e] = sums(out, p, (q,))


def step_one(codes, coupling, prolong_rows, after):
    corner = jax.ShapeDtypeStruct((2, BS, QUAD), BF16)
    return pl.pallas_call(
        step_one_kernel,
        out_shape=(
            jax.ShapeDtypeStruct((4, 9, BS, QUAD), BF16),
            corner,
            corner,
            jax.ShapeDtypeStruct(prolong_rows.shape, BF16),
        ),
        in_specs=[HBM] * 3 + [ANY],
        out_specs=(VMEM,) * 4,
        scratch_shapes=[
            pltpu.VMEM((NONE + 1, BS, BS), BF16),
            pltpu.SMEM((SIDE, SIDE, KA), jnp.int32),
            pltpu.SMEM((400,), jnp.int32),
            pltpu.SemaphoreType.DMA((10,)),
        ],
        compiler_params=pltpu.CompilerParams(vmem_limit_bytes=16 << 20),
        cost_estimate=pl.CostEstimate(flops=1 << 33, bytes_accessed=1 << 20, transcendentals=0),
        name="step_one",
    )(codes, coupling, prolong_rows, after)


def half_of(ref, h):
    return ref[2 * QUAD + h : 2 * QUAD + h + 1, :].astype(F32)


def quad_of(ref, h):
    return ref[QUAD * h : QUAD * (h + 1), :]


def edge_slots(near, far, same_a):
    same_b = 1.0 - jnp.abs(half_of(far, 0) - half_of(far, 1))
    second = quad_of(far, 1)
    shared = second * same_b.astype(BF16)
    right = jnp.concatenate(
        [
            jnp.concatenate([quad_of(far, 0), jnp.zeros_like(second)], axis=1),
            jnp.concatenate([shared, second - shared], axis=1),
        ],
        axis=0,
    )
    by_p = [jnp.dot(rows, right, preferred_element_type=F32) for rows in near]
    base, extra = [], []
    for v in range(2):
        one, two = (value[:, v * BS : (v + 1) * BS] for value in by_p)
        shared = same_a * two
        base.append(one + shared)
        extra.append(two - shared)
    return base, extra


def inside(axis, count):
    at = lax.axis_index(axis)
    return jnp.where(at == 0, 0.0, jnp.where(at == count - 1, 0.0, 1.0)).astype(F32)


def store_pieces(outs, at, values):
    rows = BS // len(outs)
    me = lax.axis_index("col")
    for s, out in enumerate(outs):
        start = pl.multiple_of((me ^ s) * rows, rows)
        for t in range(values.shape[0]):
            first = (at + t) * rows
            out[first : first + rows, :] = values[t, pl.ds(start, rows), :].astype(BF16)


def near_kernel(parts, bits, r, prolong, col_a, col_b, *rest):
    outs, (columns, column_head, slots, right) = rest[:-4], rest[-4:]
    fx, fy = flips()

    def by_halves(quads, own, first):
        for j, (_, parts_of, bit) in enumerate(quads):
            for m, rows in enumerate(parts_of):
                step = rows.shape[0]
                at = QUAD * j + step * m
                high = rows * bit.astype(BF16)
                right[at : at + step, 0:BS] = rows - high
                right[at : at + step, BS:] = high
        names = [q for q, _, _ in quads]
        for i, k in enumerate(own):
            value = jnp.dot(sums(r, OWN[k], names), right[0 : QUAD * len(quads), :], preferred_element_type=F32)
            for b in range(2):
                one = value[:, b * BS : (b + 1) * BS]
                high = bits[k : k + 1, :] * one
                low = one - high
                if i == 0:
                    slots[first + b] = low
                    slots[first + 2 + b] = high
                else:
                    slots[first + b] += low
                    slots[first + 2 + b] += high

    quads = []
    for j, (u, v) in enumerate(OWN):
        ur, vr = turned(u - 1, fx), turned(v - 1, fy)
        at = pl.ds(pl.multiple_of(vr * 256, 256), 256)
        quads.append(((u, v), [prolong[2 * ur + m, at, :] for m in range(2)], bits[j : j + 1, :]))
    by_halves(quads, range(4), 0)
    split_y = jnp.abs(bits[0:1, :] - bits[1:2, :])
    for e, (far, own, side, scale) in enumerate(((col_a, 2, 3, None), (col_b, 1, 0, inside("col", parts)))):
        near = [sums(r, (u, own), ((1, side), (2, side))) for u in (1, 2)]
        base, extra = edge_slots(near, far, split_y)
        for t in range(2):
            slots[4 + 2 * e + t] = base[t] if scale is None else base[t] * scale
            columns[2 * e + t] = extra[t] if scale is None else extra[t] * scale
            column_head[2 * e + t : 2 * e + t + 1, :] = half_of(far, t)
    column_head[4:8, :] = bits[0:4, :]
    rows = BS // parts
    me = lax.axis_index("col")
    for s in range(parts):
        start = pl.multiple_of((me ^ s) * rows, rows)
        out = outs[s] if s < 2 else outs[s // 2 + 1]
        for t in range(OWN_SLOTS):
            value = slots[t, pl.ds(start, rows), :].astype(BF16)
            if s < 2:
                out[t] = value
            else:
                out[s % 2, t] = value


def near_terms(parts, *operands):
    rows = BS // parts
    one = jax.ShapeDtypeStruct((OWN_SLOTS, rows, BS), BF16)
    two = jax.ShapeDtypeStruct((2, OWN_SLOTS, rows, BS), BF16)
    shapes = (one, one) + (two,) * (parts // 2 - 1)
    shapes += (jax.ShapeDtypeStruct((4, BS, BS), F32), jax.ShapeDtypeStruct((8, BS), F32))
    return pl.pallas_call(
        functools.partial(near_kernel, parts),
        out_shape=shapes,
        in_specs=[VMEM] * len(operands),
        out_specs=(VMEM,) * len(shapes),
        scratch_shapes=[pltpu.VMEM((OWN_SLOTS, BS, BS), F32), pltpu.VMEM((4 * QUAD, 2 * BS), BF16)],
        compiler_params=pltpu.CompilerParams(vmem_limit_bytes=16 << 20),
        cost_estimate=pl.CostEstimate(flops=1, bytes_accessed=1, transcendentals=0),
        name="near_terms",
    )(*operands)


def fill_edges(r, edges, slots, head):
    for e, (far, own, quads, same_a, scale) in enumerate(edges):
        base, extra = edge_slots([sums(r, p, quads) for p in own], far, same_a)
        for t in range(2):
            slots[2 * e + t] = base[t] if scale is None else base[t] * scale
            slots[4 + 2 * e + t] = extra[t] if scale is None else extra[t] * scale
            head[2 * e + t : 2 * e + t + 1, :] = half_of(far, t)


def far_kernel(counts, bits, r, row_a, row_b, from_a, from_b, columns, column_head, *rest):
    outs, (slots, head) = rest[:-2], rest[-2:]
    split_x = 1.0 - jnp.abs(bits[0:1, :] - bits[1:2, :])
    row_in, col_in = inside("row", counts[0]), inside("col", counts[1])
    head[...] = jnp.zeros_like(head)
    head[0:4, :] = bits[0:4, :]
    head[8:12, :] = column_head[0:4, :]
    edges = (
        (row_a, ((2, 1), (2, 2)), ((3, 1), (3, 2)), split_x, None),
        (row_b, ((1, 1), (1, 2)), ((0, 1), (0, 2)), split_x, row_in),
    )
    fill_edges(r, edges, slots, head.at[4:8])
    for t in range(4):
        slots[4 + t] += columns[t]
    corners = (
        (from_a.at[0], quad_of(row_a, 1), None),
        (from_b.at[0], quad_of(row_a, 0), col_in),
        (from_a.at[1], quad_of(row_b, 1), row_in),
        (from_b.at[1], quad_of(row_b, 0), row_in * col_in),
    )
    for e, (near, far, scale) in enumerate(corners):
        value = jnp.dot(near[...], far, preferred_element_type=F32)
        slots[8 + e] = value if scale is None else value * scale
    store_pieces(outs, 0, slots.at[0:4])
    store_pieces(outs, 4, slots.at[8:12])
    store_pieces(outs, 8, slots.at[4:8])
    for out in outs:
        out[out.shape[0] - BITS :, :] = head[...].astype(BF16)


def far_terms(counts, *operands):
    parts = counts[1]
    message = jax.ShapeDtypeStruct((SLOTS * (BS // parts) + BITS, BS), BF16)
    return pl.pallas_call(
        functools.partial(far_kernel, counts),
        out_shape=(message,) * parts,
        in_specs=[VMEM] * len(operands),
        out_specs=(VMEM,) * parts,
        scratch_shapes=[pltpu.VMEM((12, BS, BS), F32), pltpu.VMEM((BITS, BS), F32)],
        compiler_params=pltpu.CompilerParams(vmem_limit_bytes=16 << 20),
        cost_estimate=pl.CostEstimate(flops=1, bytes_accessed=1, transcendentals=0),
        name="far_terms",
    )(*operands)


def unpack_kernel(parts, steps, *refs):
    ins, owns = refs[: len(steps)], refs[len(steps) : 2 * len(steps)]
    out, buf, sems = refs[-3:]
    me = lax.axis_index("col")
    fx, _ = flips()
    copies = []
    for i, (s, ref) in enumerate(zip(steps, ins)):
        square = me ^ s
        fy = lax.rem(square, 2)
        own = owns[i] if s < 2 else owns[i].at[s // 2 - 1 if s % 2 else 0]
        for a in range(2):
            copies.append(
                pltpu.make_async_copy(own.at[2 * a : 2 * a + 2], out.at[square, a, 4], sems.at[len(copies)])
            )
            copies[-1].start()
        one = functools.partial(bit_row, ref)
        split_y = jnp.abs(one(0) - one(1))

        def send(piece, owner, code):
            copies.append(pltpu.make_async_copy(buf.at[i, piece], out.at[owner, :, code], sems.at[len(copies)]))
            copies[-1].start()

        split_x = 1.0 - split_y
        edges = (
            ((2, 3), (8, 9), split_y, 7 - 6 * fx),
            ((0, 1), (10, 11), split_y, 1 + 6 * fx),
            ((1, 3), (8, 9), split_x, 3 + turn3(2, fy)),
            ((0, 2), (10, 11), split_x, 3 + turn3(0, fy)),
        )
        for e, (ps, more, used, code) in enumerate(edges):
            if e < 2:
                values = [slot(ref, 2 * e + t) for t in range(2)]
            else:
                values = [own[2 * e + t].astype(F32) for t in range(2)]
            second = [slot(ref, t) for t in more]
            spread_edge(buf, (i, e), one, ps, (4 + 2 * e, 5 + 2 * e), values, second, used)
            send(e, square, code)
        high = square ^ 1
        low = square + 2 * fy - 1
        low = jnp.where((low < 0) | (low >= parts), square, low)
        corners = (
            (high, 6 - 6 * fx, 2, 9, 5),
            (low, 6 - 6 * fx, 0, 11, 4),
            (high, 6 * fx, 2, 8, 7),
            (low, 6 * fx, 0, 10, 6),
        )
        for e, (owner, group, side, a_bit, b_bit) in enumerate(corners):
            spread_corner(buf, (i, 4 + e), slot(ref, 4 + e), one(a_bit), one(b_bit))
            send(4 + e, owner, group + turn3(side, lax.rem(owner, 2)))
    for copy in copies:
        copy.wait()


def unpack(messages, owns, steps, coarse):
    parts = lax.axis_size("col")
    rows = BS // parts
    fresh = coarse is None
    return pl.pallas_call(
        functools.partial(unpack_kernel, parts, steps),
        out_shape=jax.ShapeDtypeStruct((parts, 2, 9, 2, rows, BS), BF16),
        in_specs=[VMEM] * (2 * len(steps)) + [ANY] * (not fresh),
        out_specs=ANY,
        scratch_shapes=[
            pltpu.VMEM((len(steps), 8, 2, 2, rows, BS), BF16),
            pltpu.SemaphoreType.DMA((10 * len(steps),)),
        ],
        input_output_aliases={} if fresh else {2 * len(steps): 0},
        compiler_params=pltpu.CompilerParams(vmem_limit_bytes=16 << 20),
        cost_estimate=pl.CostEstimate(flops=1, bytes_accessed=1, transcendentals=0),
        name="unpack",
    )(*messages, *owns, *(() if fresh else (coarse,)))


def turn3(index, flip):
    return index + flip * (2 - 2 * index)


def bit_row(ref, k):
    at = ref.shape[0] - BITS + k
    return ref[at : at + 1, :].astype(F32)


def slot(ref, t):
    rows = (ref.shape[0] - BITS) // SLOTS
    return ref[t * rows : (t + 1) * rows, :].astype(F32)


def spread(buf, at, center):
    i, piece = at
    for a in range(2):
        for b in range(2):
            buf[i, piece, a, b] = center[2 * a + b].astype(BF16)


def spread_edge(buf, at, one, ps, qs, values, more, used):
    a_bits = [one(p) for p in ps]
    b_bits = [one(q) for q in qs]
    center = [None] * 4
    for b in range(2):
        picks = [bit if b else 1.0 - bit for bit in b_bits]
        first = picks[0] * values[0] + picks[1] * values[1]
        second = (used * picks[0]) * more[0] + (used * picks[1]) * more[1]
        for a in range(2):
            ia = [bit if a else 1.0 - bit for bit in a_bits]
            center[2 * a + b] = ia[0] * first + ia[1] * second
    spread(buf, at, center)


def spread_corner(buf, at, value, a_bit, b_bit):
    center = []
    for a in range(2):
        for b in range(2):
            center.append(((a_bit if a else 1.0 - a_bit) * (b_bit if b else 1.0 - b_bit)) * value)
    spread(buf, at, center)


def gate_kernel(*refs):
    pass


def gate(values, after):
    count = len(values)
    return pl.pallas_call(
        gate_kernel,
        out_shape=tuple(jax.ShapeDtypeStruct(v.shape, v.dtype) for v in values),
        in_specs=[ANY] * (count + len(after)),
        out_specs=(ANY,) * count,
        input_output_aliases={i: i for i in range(count)},
        compiler_params=pltpu.CompilerParams(vmem_limit_bytes=1 << 20),
        cost_estimate=pl.CostEstimate(flops=1 << 33, bytes_accessed=1, transcendentals=0),
        name="gate",
    )(*values, *after)


def other_side(index):
    return index + 1 if index % 2 else index - 1


def row_low(r, c, rows, cols):
    far = other_side(r)
    return (far, c) if 0 <= far < rows else (r, c ^ 1)


def col_low(r, c, rows, cols):
    far = other_side(c)
    if 0 <= far < cols:
        return r, far
    if r % 2:
        return (r - 2 if r >= 2 else r - 1), c
    return (r + 2 if r + 2 < rows else r + 1), c


def row_high(r, c, rows, cols):
    return r ^ 1, c


def col_high(r, c, rows, cols):
    return r, c ^ 1


def swap(value, partner):
    rows, cols = lax.axis_size("row"), lax.axis_size("col")
    pairs = []
    for r in range(rows):
        for c in range(cols):
            to_r, to_c = partner(r, c, rows, cols)
            pairs.append((r * cols + c, to_r * cols + to_c))
    return lax.ppermute(value, ("row", "col"), pairs)


def xor_swap(value, s):
    return lax.ppermute(value, "col", [(i, i ^ s) for i in range(lax.axis_size("col"))])


def local(coupling, neighbours, prolong, aggregate):
    parts = lax.axis_size("col")
    counts = (lax.axis_size("row"), parts)
    coupling = pltpu.with_memory_space_constraint(coupling.reshape(-1, BS, BS), pltpu.HBM)
    neighbours = pltpu.with_memory_space_constraint(neighbours, pltpu.HBM)
    aggregate = pltpu.with_memory_space_constraint(aggregate, pltpu.HBM)
    prolong_rows = pltpu.with_memory_space_constraint(prolong.reshape(SIDE, SIDE * BS, BS), pltpu.HBM)
    to_row_a, to_row_b, bits = rims(aggregate, prolong_rows)
    to_col_a, to_col_b = column_rims(to_row_a, to_row_b, bits)
    row_a = swap(to_row_a, row_high)
    row_b = swap(to_row_b, row_low)
    col_a = swap(to_col_a, col_high)
    col_b = swap(to_col_b, col_low)
    r, to_a, to_b, own_blocks = step_one(neighbours, coupling, prolong_rows, to_col_b)
    from_b = swap(to_b, col_low)
    from_a = swap(to_a, col_high)
    mine, pair, *cross, columns, column_head = near_terms(parts, bits, r, own_blocks, col_a, col_b)
    direct = [xor_swap(value, 2 * h + 2) for h, value in enumerate(cross)]
    row_a, row_b, columns, from_b = gate((row_a, row_b, columns, from_b), (mine,))
    outs = list(far_terms(counts, bits, r, row_a, row_b, from_a, from_b, columns, column_head))
    outs[0], pair, *direct = lax.optimization_barrier((outs[0], pair, *direct))
    outs = [outs[0]] + [xor_swap(outs[s], s) for s in range(1, parts)]
    pair = xor_swap(pair, 1)
    relayed = xor_swap(jnp.concatenate([value[1:2] for value in direct]), 1)
    owns = [mine, pair]
    for value in direct:
        owns += [value, relayed]
    coarse = None
    for steps in (range(0, parts, 2), range(parts - 1, 0, -2)):
        coarse = unpack([outs[t] for t in steps], [owns[t] for t in steps], steps, coarse)
    return coarse[None]


def solution(mesh):
    return jax.shard_map(
        local,
        mesh=mesh,
        in_specs=(
            P("row", "col", None, None, None),
            P("row", "col", None),
            P("row", "col", None, None),
            P("row", "col"),
        ),
        out_specs=P("row", None, None, None, None, "col", None),
        check_vma=False,
    )
```
